32 devices in a mesh: groups: 2 (over y), row: 4 (over z), col: 2 (over x), pole: 2 (over core).
Axes of the slice: x: 2, y: 2, z: 4, core: 2. Of those that a mesh axis runs over, the one named last changes fastest.
Arguments:
- inverse: bfloat16 [4, 2, 8192, 8192], P(('groups', 'pole'), None, 'row', 'col'), parts along dimension 0, may hold values from -6 to 6
- lower: bfloat16 [4, 8192, 2, 3, 256], P(('groups', 'pole'), ('col', 'row')), parts along dimension 0, may hold values from -0.0625 to 0.0625
- upper: bfloat16 [4, 8192, 2, 3, 256], P(('groups', 'pole'), ('row', 'col')), parts along dimension 0, may hold values from -0.0625 to 0.0625
- diag_inverse: bfloat16 [4, 3, 2, 256, 256], P(('groups', 'pole')), parts along dimension 0, may hold values from -6 to 6
- weights: float32 [4, 2], P(('groups', 'pole')), parts along dimension 0, may hold values from -4 to 4
- pattern: int32 [6, 16], P('groups'), parts along dimension 0, may hold values from 0 to 31, as said below
Outputs:
- column_density: float32 [16384, 3, 256], P(('groups', 'row', 'col', 'pole')), parts along dimension 0
- row_density: float32 [16384, 3, 256], P(('groups', 'col', 'row', 'pole')), parts along dimension 0
- diagonal_density: float32 [6, 256, 256], P('groups'), parts along dimension 0
The draws below stay inside these ranges and needn't reach their ends.
There are 2 independent parts, one for each index of `groups`. The reference program is written for one: setup_inputs(seed, part) draws one part's arguments, and reference() takes and returns one part's arrays. A program takes and returns all parts, laid end to end along the dimension named above; each array names one. Nothing has to cross between parts.
Inputs may be any that keep to these rules, and one draw needn't show every extreme that they name: `pattern`: each row names 16 different ancestor blocks, and the rows together name every ancestor block.
All inputs are finite; a program needn't handle non-finite values.
Results may differ from the reference program's by a relative error of at most 0.0003.
Values may be sent and summed in bfloat16 or wider, within the bound.
A program may use at most 192 MiB of HBM per device.

```python
import jax
import jax.numpy as jnp
from jax import lax

BW = 256
NB = 32
PAT = 16
SUPER = 3
ANC = 8192
POLES = 2


def draw_pattern(key, part):
    order = jax.random.permutation(jax.random.fold_in(key, 17), NB).astype(jnp.int32)
    supers = jnp.arange(SUPER, dtype=jnp.int32)[:, None]
    slots = jnp.arange(PAT, dtype=jnp.int32)[None, :]
    positions = (supers * PAT + slots) % NB
    return order[positions].astype(jnp.int32)


def levels(key, dims, shards, least, high):
    def one(axis_at, blocks):
        heights = jax.random.uniform(jax.random.fold_in(jax.random.fold_in(key, 6), axis_at), (blocks,), jnp.float32, least / len(shards), high / len(shards))
        return jnp.repeat(jnp.exp(heights), dims[axis_at] // blocks).reshape((-1,) + (1,) * (len(dims) - axis_at - 1))

    factor_of = one(*shards[0])
    for cut in shards[1:]:
        factor_of = factor_of * one(*cut)
    return factor_of


def normal_values(own_key, dims, deviation, most, split=(), kind=jnp.bfloat16):
    array = deviation * jax.random.normal(own_key, dims, jnp.float32)
    if split:
        array = array * levels(own_key, dims, split, -0.22, 0.18)
    return jnp.clip(array, -most, most).astype(kind)


def setup_inputs(seed: int = 0, part: int = 0) -> dict:
    splits = jax.random.split(jax.random.key(seed), 7)
    own_keys = jax.random.split(jax.random.fold_in(splits[6], part), 7)
    inverse = normal_values(own_keys[0], (POLES, 2, ANC, ANC), 1.0, 6.0, ((0, 2), (2, 4), (3, 2)))
    lower = normal_values(own_keys[1], (POLES, ANC, 2, SUPER, BW), (2 * PAT * BW) ** -0.5, 0.0625, ((0, 2), (1, 8)))
    upper = normal_values(own_keys[2], (POLES, ANC, 2, SUPER, BW), (2 * PAT * BW) ** -0.5, 0.0625, ((0, 2), (1, 8)))
    diag_inverse = normal_values(own_keys[3], (POLES, SUPER, 2, BW, BW), 1.0, 6.0, ((0, 2),))
    weights = normal_values(own_keys[4], (POLES, 2), 1.0, 4.0, ((0, 2),), jnp.float32)
    pattern = draw_pattern(jax.random.fold_in(jax.random.fold_in(splits[6], part), 71), part)
    return dict(inverse=inverse, lower=lower, upper=upper, diag_inverse=diag_inverse, weights=weights, pattern=pattern)


def kept_rows(pattern):
    blocks = jnp.arange(ANC, dtype=jnp.int32) // BW
    hits = pattern[:, :, None] == blocks[None, None, :]
    return jnp.any(hits, axis=1)


def transposed_dot(left, right):
    return lax.dot_general(left, right, (((0,), (0,)), ((), ())), preferred_element_type=jnp.float32)


def reference(inverse, lower, upper, diag_inverse, weights, pattern):
    keep = jnp.transpose(kept_rows(pattern))[:, None, :, None]
    column_density = jnp.zeros((ANC, SUPER * BW), jnp.float32)
    row_density = jnp.zeros((ANC, SUPER * BW), jnp.float32)
    diagonal_density = jnp.zeros((SUPER, BW, BW), jnp.float32)
    highest = lax.Precision.HIGHEST
    for pole in range(POLES):
        real_inverse = inverse[pole, 0]
        imag_inverse = inverse[pole, 1]
        lower_kept = jnp.where(keep, lower[pole], jnp.zeros_like(lower[pole]))
        upper_kept = jnp.where(keep, upper[pole], jnp.zeros_like(upper[pole]))
        real_lower = lower_kept[:, 0].reshape(ANC, SUPER * BW)
        imag_lower = lower_kept[:, 1].reshape(ANC, SUPER * BW)
        real_upper = upper_kept[:, 0].reshape(ANC, SUPER * BW)
        imag_upper = upper_kept[:, 1].reshape(ANC, SUPER * BW)
        column_real = -(jnp.dot(real_inverse, real_lower, preferred_element_type=jnp.float32)
                        - jnp.dot(imag_inverse, imag_lower, preferred_element_type=jnp.float32))
        column_imag = -(jnp.dot(real_inverse, imag_lower, preferred_element_type=jnp.float32)
                        + jnp.dot(imag_inverse, real_lower, preferred_element_type=jnp.float32))
        row_real = -(transposed_dot(real_inverse, real_upper) - transposed_dot(imag_inverse, imag_upper))
        row_imag = -(transposed_dot(real_inverse, imag_upper) + transposed_dot(imag_inverse, real_upper))
        weight_real = weights[pole, 0]
        weight_imag = weights[pole, 1]
        column_density = column_density + weight_real * column_imag + weight_imag * column_real
        row_density = row_density + weight_real * row_imag + weight_imag * row_real
        zeta_real = row_real.reshape(ANC, SUPER, BW)
        zeta_imag = row_imag.reshape(ANC, SUPER, BW)
        lower_real = real_lower.astype(jnp.float32).reshape(ANC, SUPER, BW)
        lower_imag = imag_lower.astype(jnp.float32).reshape(ANC, SUPER, BW)
        prod_real = (jnp.einsum("nsa,nsb->sab", zeta_real, lower_real, precision=highest)
                     - jnp.einsum("nsa,nsb->sab", zeta_imag, lower_imag, precision=highest))
        prod_imag = (jnp.einsum("nsa,nsb->sab", zeta_real, lower_imag, precision=highest)
                     + jnp.einsum("nsa,nsb->sab", zeta_imag, lower_real, precision=highest))
        given = diag_inverse[pole].astype(jnp.float32)
        diag_real = given[:, 0] - prod_real
        diag_imag = given[:, 1] - prod_imag
        diagonal_density = diagonal_density + weight_real * diag_imag + weight_imag * diag_real
    return (column_density.reshape(ANC, SUPER, BW), row_density.reshape(ANC, SUPER, BW), diagonal_density)
```

```python
import functools
import math

import jax
import jax.numpy as jnp
from jax import lax
from jax.experimental import pallas as pl
from jax.experimental.pallas import tpu as pltpu
from jax.sharding import PartitionSpec as P

MESH = pl.DeviceIdType.MESH
RING = 6
TOP = 32767.0


def usual_caps(n, per):
    return [0] + [min(per * d, math.ceil(per * d * (0.5 + 1 / (6 * math.sqrt(d))))) for d in range(1, n)]


def full_caps(n, per):
    return [per * d for d in range(n)]


def room(caps):
    n = len(caps)
    return max(caps[z] + caps[n - 1 - z] for z in range(n)) + 1


def stepped(caps, count):
    total = jnp.int32(0)
    for d in range(1, len(caps)):
        total = total + jnp.where(count >= d, caps[d] - caps[d - 1], 0)
    return total


class Streams:
    def __init__(self, caps, first, n, order, lown, lin, stage, send_sem, recv_sem, out_sem, lall):
        self.caps, self.first, self.n = caps, first, n
        self.order, self.lown, self.lin, self.stage = order, lown, lin, stage
        self.send_sem, self.recv_sem, self.out_sem, self.lall = send_sem, recv_sem, out_sem, lall
        self.per = lown.shape[0]
        self.size = lin.shape[0]
        self.z = lax.axis_index("row")
        z = self.z
        self.sent = (jnp.where(z > 0, stepped(caps, n - z), 0), jnp.where(z < n - 1, stepped(caps, z + 1), 0))
        self.taken = (stepped(caps, n - 1 - z), stepped(caps, z))
        self.events = max(caps) - first

    def place(self, way, c):
        return c if way == 0 else self.size - 1 - c

    def remote(self, way, c):
        slot = lax.rem(c, RING)
        place = self.place(way, c)
        return pltpu.make_async_remote_copy(
            src_ref=self.stage.at[way, slot],
            dst_ref=self.lin.at[place],
            send_sem=self.send_sem.at[way, slot],
            recv_sem=self.recv_sem.at[place],
            device_id={"row": self.z - 1 if way == 0 else self.z + 1},
            device_id_type=MESH,
        )

    def kept(self, way, c):
        place = self.place(way, c)
        return pltpu.make_async_copy(self.lin.at[place], self.lall.at[self.per + place], self.out_sem.at[place])

    def begin(self):
        for way in range(2):
            @pl.when(self.sent[way] > 0)
            def _():
                for c in range(self.first):
                    if c >= RING:
                        self.remote(way, c - RING).wait_send()
                    self.stage[way, c % RING] = self.lown[self.order[c]]
                    self.remote(way, c).start()

    def forward(self, d):
        c = d + self.first
        for way in range(2):
            @pl.when(c < self.sent[way])
            def _():
                @pl.when(d < self.taken[way])
                def _():
                    self.remote(way, d).wait_recv()
                    self.kept(way, d).start()

                @pl.when(c >= RING)
                def _():
                    self.remote(way, c - RING).wait_send()

                count = self.order[self.per + way]
                mine = self.lown[self.order[jnp.clip(c - count, 0, self.per - 1)]]
                arrived = self.lin[self.place(way, jnp.clip(d, 0, jnp.maximum(self.taken[way] - 1, 0)))]
                self.stage[way, lax.rem(c, RING)] = jnp.where(d < count, arrived, mine)
                self.remote(way, c).start()

    def drain(self):
        def step(c, carry):
            for way in range(2):
                @pl.when(jnp.logical_and(c < self.taken[way], c + self.first >= self.sent[way]))
                def _():
                    self.remote(way, c).wait_recv()
                    self.kept(way, c).start()

                @pl.when(jnp.logical_and(c < self.sent[way], c + RING >= self.sent[way]))
                def _():
                    self.remote(way, c).wait_send()
            return carry

        lax.fori_loop(0, max(self.caps), step, 0)

        def last(c, carry):
            for way in range(2):
                @pl.when(c < self.taken[way])
                def _():
                    self.kept(way, c).wait()
            return carry

        lax.fori_loop(0, max(self.caps), last, 0)


def greet(targets):
    barrier = pltpu.get_barrier_semaphore()
    total = jnp.int32(0)
    for axis, size, near in targets:
        me = lax.axis_index(axis)
        if near:
            for step in (-1, 1):
                there = jnp.logical_and(me + step >= 0, me + step < size)

                @pl.when(there)
                def _():
                    pl.semaphore_signal(barrier, inc=1, device_id={axis: me + step}, device_id_type=MESH)

                total = total + there.astype(jnp.int32)
        else:
            for d in range(1, size):
                pl.semaphore_signal(barrier, inc=1, device_id={axis: lax.rem(me + d, size)}, device_id_type=MESH)
            total = total + (size - 1)
    pl.semaphore_wait(barrier, total)


def packed(value):
    most = jnp.max(jnp.abs(value), axis=0, keepdims=True)
    factor = jnp.where(most > 0, TOP / jnp.maximum(most, 1e-30), 0.0)
    return jnp.round(value * factor).astype(jnp.int32).astype(jnp.int16), most * (1.0 / TOP)


def unpacked(code, scale):
    return code.astype(jnp.int32).astype(jnp.float32) * scale


def stream_kernel(cfg, order, weights, pattern, inverse, own_l, own_u, lall, uall, row_out, patterns, *scratch):
    (acc, lhs, abuf, ubuf, lown, lin, stage, prec, qstage, qrecv, mstage, mrecv,
     a_sem, u_send, u_recv, l_sem, s_send, s_recv, s_out, p_send, p_recv, q_send, q_recv, m_send, m_recv, g_send, g_recv) = scratch
    n, n_col, n_groups, caps = cfg
    per = lown.shape[0]
    kbs, _, supers, unit, width = ubuf.shape
    blocks = kbs // n_col
    half = acc.shape[2]
    tile = 2 * half
    z = lax.axis_index("row")
    x = lax.axis_index("col")
    p = lax.axis_index("pole")
    g = lax.axis_index("groups")

    lcopy = pltpu.make_async_copy(own_l, lown, l_sem.at[0])
    lcopy.start()
    ucopy = pltpu.make_async_copy(own_u, ubuf.at[pl.ds(0, blocks)], l_sem.at[1])
    ucopy.start()

    def a_copy(t):
        kb = t // n
        origin = lax.rem(x - kb // blocks + n_col, n_col)
        row = (origin * blocks + lax.rem(kb, blocks)) * unit
        return pltpu.make_async_copy(
            inverse.at[:, pl.ds(pl.multiple_of(row, unit), unit), pl.ds(pl.multiple_of(lax.rem(t, n) * tile, tile), tile)],
            abuf.at[lax.rem(t, 3)],
            a_sem.at[lax.rem(t, 3)],
        )

    a_copy(0).start()
    a_copy(1).start()
    greet((("row", n, True), ("col", n_col, False), ("pole", 2, False), ("groups", n_groups, False)))

    def u_remote(d, b):
        return pltpu.make_async_remote_copy(
            src_ref=own_u.at[b],
            dst_ref=ubuf.at[d * blocks + b],
            send_sem=u_send.at[d * blocks + b],
            recv_sem=u_recv.at[d * blocks + b],
            device_id={"col": lax.rem(x + d, n_col)},
            device_id_type=MESH,
        )

    for b in range(blocks):
        for d in range(1, n_col):
            u_remote(d, b).start()

    def g_remote(d):
        return pltpu.make_async_remote_copy(
            src_ref=pattern,
            dst_ref=patterns.at[d],
            send_sem=g_send.at[d],
            recv_sem=g_recv.at[d],
            device_id={"groups": lax.rem(g + d, n_groups)},
            device_id_type=MESH,
        )

    for d in range(1, n_groups):
        g_remote(d).start()
    patterns[0] = pattern[...]

    lcopy.wait()
    streams = Streams(caps, blocks, n, order, lown, lin, stage, s_send, s_recv, s_out, lall)
    streams.begin()
    lout = pltpu.make_async_copy(lown, lall.at[pl.ds(0, per)], l_sem.at[0])
    lout.start()
    ucopy.wait()

    tiles = kbs * n
    early = blocks * n
    events = streams.events
    events_early = events * 5 // 18
    events_late = events - events_early
    late = tiles - early

    def due(t):
        if late == 0:
            return t * events // early
        return jnp.where(t < early, t * events_early // early, events_early + (t - early) * events_late // late)

    def row_tile(t, carry):
        kb = t // n
        j = lax.rem(t, n)

        @pl.when(j == 0)
        def _():
            @pl.when(kb >= blocks)
            def _():
                u_remote(kb // blocks, lax.rem(kb, blocks)).wait_recv()

            for s in range(supers):
                kept = order[per + 2 + kb * supers + s] > 0
                real = jnp.where(kept, ubuf[kb, 0, s].astype(jnp.float32), 0.0)
                imag = jnp.where(kept, ubuf[kb, 1, s].astype(jnp.float32), 0.0)
                span = slice(s * width, (s + 1) * width)
                for i, value in enumerate((weights[1] * real + weights[0] * imag, weights[0] * real - weights[1] * imag)):
                    turned = jnp.transpose(value)
                    high = turned.astype(jnp.bfloat16)
                    lhs[0, span, i * unit:(i + 1) * unit] = high
                    lhs[1, span, i * unit:(i + 1) * unit] = (turned - high.astype(jnp.float32)).astype(jnp.bfloat16)

        @pl.when(t + 2 < tiles)
        def _():
            a_copy(t + 2).start()

        a_copy(t).wait()
        slot = lax.rem(t, 3)
        for q in range(2):
            right = abuf[slot, :, :, q * half:(q + 1) * half].reshape(2 * unit, half)
            total = jnp.dot(lhs[0], right, preferred_element_type=jnp.float32) + jnp.dot(
                lhs[1], right, preferred_element_type=jnp.float32
            )
            before = acc[2 * j + q]
            acc[2 * j + q] = total + jnp.where(kb == 0, jnp.zeros_like(before), before)

        now = due(t)

        def some(d, carry):
            streams.forward(d)
            return carry

        lax.fori_loop(now, due(t + 1), some, 0)
        return carry

    lax.fori_loop(0, tiles, row_tile, 0)

    uout = pltpu.make_async_copy(ubuf, uall, l_sem.at[1])
    uout.start()

    def p_remote(ch):
        return pltpu.make_async_remote_copy(
            src_ref=acc.at[2 * ch + 1 - p],
            dst_ref=prec.at[ch],
            send_sem=p_send.at[ch],
            recv_sem=p_recv.at[ch],
            device_id={"pole": 1 - p},
            device_id_type=MESH,
        )

    for i in range((n + 1) // 2):
        p_remote(n - 1 - i).start()
        if i != n - 1 - i:
            p_remote(i).start()

    def q_remote(way, i):
        to = {"row": z + 1 if way == 0 else z - 1}
        return (
            pltpu.make_async_remote_copy(
                src_ref=qstage.at[way, i], dst_ref=qrecv.at[way, i], send_sem=q_send.at[way, i], recv_sem=q_recv.at[way, i],
                device_id=to, device_id_type=MESH,
            ),
            pltpu.make_async_remote_copy(
                src_ref=mstage.at[way, i], dst_ref=mrecv.at[way, i], send_sem=m_send.at[way, i], recv_sem=m_recv.at[way, i],
                device_id=to, device_id_type=MESH,
            ),
        )

    def arrived(way, i):
        for copy in q_remote(way, i):
            copy.wait_recv()
        return unpacked(qrecv[way, i], mrecv[way, i, :1])

    def row_step(i, carry):
        for way in range(2):
            ch = n - 1 - i if way == 0 else i

            @pl.when(z < ch if way == 0 else z > ch)
            def _():
                p_remote(ch).wait_recv()
                acc[2 * ch + p] = acc[2 * ch + p] + prec[ch]

                @pl.when(z > 0 if way == 0 else z < n - 1)
                def _():
                    acc[2 * ch + p] = acc[2 * ch + p] + arrived(way, i)

                code, scale = packed(acc[2 * ch + p])
                qstage[way, i] = code
                mstage[way, i] = jnp.broadcast_to(scale, mstage.shape[2:])
                for copy in q_remote(way, i):
                    copy.start()
        return carry

    lax.fori_loop(0, n - 1, row_step, 0)

    p_remote(z).wait_recv()
    row_out[...] = acc[2 * z + p] + prec[z]

    @pl.when(z > 0)
    def _():
        row_out[...] = row_out[...] + arrived(0, n - 1 - z)

    @pl.when(z < n - 1)
    def _():
        row_out[...] = row_out[...] + arrived(1, z)

    row_out[...] = -row_out[...]
    streams.drain()

    def finish(i, carry):
        for way in range(2):
            ch = n - 1 - i if way == 0 else i

            @pl.when(z < ch if way == 0 else z > ch)
            def _():
                for copy in q_remote(way, i):
                    copy.wait_send()
        return carry

    lax.fori_loop(0, n - 1, finish, 0)
    for ch in range(n):
        p_remote(ch).wait_send()
    for d in range(1, n_col):
        for b in range(blocks):
            u_remote(d, b).wait_send()
    for d in range(1, n_groups):
        g_remote(d).wait_send()
        g_remote(d).wait_recv()
    lout.wait()
    uout.wait()


def stream_call(order, weights, pattern, inverse, own_l, own_u, sizes):
    n, n_col, n_groups = sizes
    _, rows, cols = inverse.shape
    per, _, unit, width = own_l.shape
    blocks, _, supers, _, _ = own_u.shape
    wide = supers * width
    caps = usual_caps(n, per)
    kbs = blocks * n_col
    half = cols // n // 2
    space = room(caps)
    dma = pltpu.SemaphoreType.DMA
    scratch = [
        pltpu.VMEM((2 * n, wide, half), jnp.float32),
        pltpu.VMEM((2, wide, 2 * unit), jnp.bfloat16),
        pltpu.VMEM((3, 2, unit, 2 * half), jnp.bfloat16),
        pltpu.VMEM((kbs, 2, supers, unit, width), jnp.bfloat16),
        pltpu.VMEM((per, 2, unit, width), jnp.bfloat16),
        pltpu.VMEM((space, 2, unit, width), jnp.bfloat16),
        pltpu.VMEM((2, RING, 2, unit, width), jnp.bfloat16),
        pltpu.VMEM((n, wide, half), jnp.float32),
        pltpu.VMEM((2, n - 1, wide, half), jnp.int16),
        pltpu.VMEM((2, n - 1, wide, half), jnp.int16),
        pltpu.VMEM((2, n - 1, 8, half), jnp.float32),
        pltpu.VMEM((2, n - 1, 8, half), jnp.float32),
        dma((3,)), dma((kbs,)), dma((kbs,)), dma((2,)),
        dma((2, RING)), dma((space,)), dma((space,)),
        dma((n,)), dma((n,)),
        dma((2, n - 1)), dma((2, n - 1)), dma((2, n - 1)), dma((2, n - 1)),
        dma((n_groups,)), dma((n_groups,)),
    ]
    smem = pl.BlockSpec(memory_space=pltpu.SMEM)
    vmem = pl.BlockSpec(memory_space=pltpu.VMEM)
    hbm = pl.BlockSpec(memory_space=pl.ANY)
    return pl.pallas_call(
        functools.partial(stream_kernel, (n, n_col, n_groups, caps)),
        out_shape=(
            jax.ShapeDtypeStruct((per + space, 2, unit, width), jnp.bfloat16),
            jax.ShapeDtypeStruct((kbs, 2, supers, unit, width), jnp.bfloat16),
            jax.ShapeDtypeStruct((wide, half), jnp.float32),
            jax.ShapeDtypeStruct((n_groups,) + pattern.shape, jnp.int32),
        ),
        in_specs=[smem, smem, vmem, hbm, hbm, hbm],
        out_specs=(hbm, hbm, vmem, vmem),
        scratch_shapes=scratch,
        compiler_params=pltpu.CompilerParams(collective_id=0, has_side_effects=True, vmem_limit_bytes=62 * 2**20),
        name="streams",
    )(order, weights, pattern, inverse, own_l, own_u)


def refill_kernel(cfg, order, own_l, lall, lown, lin, stage, l_sem, s_send, s_recv, s_out):
    n, blocks, caps = cfg
    lcopy = pltpu.make_async_copy(own_l, lown, l_sem.at[0])
    lcopy.start()
    greet((("row", n, True),))
    lcopy.wait()
    streams = Streams(caps, blocks, n, order, lown, lin, stage, s_send, s_recv, s_out, lall)
    streams.begin()
    lout = pltpu.make_async_copy(lown, lall.at[pl.ds(0, lown.shape[0])], l_sem.at[0])
    lout.start()

    def step(d, carry):
        streams.forward(d)
        return carry

    lax.fori_loop(0, streams.events, step, 0)
    streams.drain()
    lout.wait()


def refill_call(order, own_l, n, blocks):
    per, _, unit, width = own_l.shape
    caps = full_caps(n, per)
    space = room(caps)
    dma = pltpu.SemaphoreType.DMA
    return pl.pallas_call(
        functools.partial(refill_kernel, (n, blocks, caps)),
        out_shape=jax.ShapeDtypeStruct((per + space, 2, unit, width), jnp.bfloat16),
        in_specs=[pl.BlockSpec(memory_space=pltpu.SMEM), pl.BlockSpec(memory_space=pl.ANY)],
        out_specs=pl.BlockSpec(memory_space=pl.ANY),
        scratch_shapes=[
            pltpu.VMEM((per, 2, unit, width), jnp.bfloat16),
            pltpu.VMEM((space, 2, unit, width), jnp.bfloat16),
            pltpu.VMEM((2, RING, 2, unit, width), jnp.bfloat16),
            dma((1,)), dma((2, RING)), dma((space,)), dma((space,)),
        ],
        compiler_params=pltpu.CompilerParams(collective_id=1, has_side_effects=True, vmem_limit_bytes=40 * 2**20),
        name="refill",
    )(order, own_l)


def column_kernel(cfg, meta, weights, a_ref, *rest):
    supers, n_col, blocks = cfg
    l_refs = rest[:supers]
    u_ref, given, mine, other, diag, acc = rest[supers:]
    k = pl.program_id(0)
    steps = pl.num_programs(0)
    _, rows, double = acc.shape
    width = double // 2
    unit = a_ref.shape[2]
    base = 2 * supers * steps
    piece = min(rows, 512)

    @pl.when(k == 0)
    def _():
        acc[...] = jnp.zeros_like(acc)

    for s in range(supers):
        @pl.when(meta[k * supers + s] > 0)
        def _():
            real = l_refs[s][0, 0]
            imag = l_refs[s][0, 1]
            right = jnp.concatenate([jnp.concatenate([real, imag], axis=1), jnp.concatenate([-imag, real], axis=1)], axis=0)

            def part(i, carry):
                span = pl.ds(pl.multiple_of(i * piece, piece), piece)
                left = jnp.concatenate([a_ref[0, span], a_ref[1, span]], axis=1)
                acc[s, span] += jnp.dot(left, right, preferred_element_type=jnp.float32)
                return carry

            lax.fori_loop(0, rows // piece, part, 0)

    @pl.when(k == steps - 1)
    def _():
        part = mine.shape[1]
        pole = meta[base]
        for s in range(supers):
            lanes = slice(s * width, (s + 1) * width)
            for c in range(n_col):
                for q in range(2):
                    span = pl.ds((2 * c + q) * part, part)
                    real = acc[s, span, :width]
                    imag = acc[s, span, width:]
                    mixed = weights[0] * imag + weights[1] * real
                    acc[s, span, :width] = mixed
                    acc[s, span, width:] = weights[0] * real - weights[1] * imag

                    @pl.when(pole == q)
                    def _():
                        mine[c, :, lanes] = -mixed

                    @pl.when(pole != q)
                    def _():
                        other[c, :, lanes] = -mixed

            @pl.when(meta[base + 1] > 0)
            def _():
                diag[lanes, :] = weights[0] * given[s, 1].astype(jnp.float32) + weights[1] * given[s, 0].astype(jnp.float32)

            @pl.when(meta[base + 1] == 0)
            def _():
                diag[lanes, :] = jnp.zeros((width, diag.shape[1]), jnp.float32)

        def one(kb, carry):
            for s in range(supers):
                lanes = slice(s * width, (s + 1) * width)

                @pl.when(meta[base + 2 + n_col + kb * supers + s] > 0)
                def _():
                    start = pl.multiple_of(meta[base + 2 + kb // blocks] + lax.rem(kb, blocks) * unit, unit)
                    total = jnp.zeros((width, width), jnp.float32)
                    for c in range(2):
                        value = acc[s, pl.ds(start, unit), c * width:(c + 1) * width]
                        high = value.astype(jnp.bfloat16)
                        low = (value - high.astype(jnp.float32)).astype(jnp.bfloat16)
                        turned = jnp.transpose(u_ref[kb, c, s])
                        total += jnp.dot(turned, high, preferred_element_type=jnp.float32) + jnp.dot(
                            turned, low, preferred_element_type=jnp.float32
                        )
                    diag[lanes, :] += total
            return carry

        lax.fori_loop(0, u_ref.shape[0], one, 0)


def column_call(meta, weights, inverse, lall, uall, given, sizes):
    n_col, supers, blocks = sizes
    _, rows, cols = inverse.shape
    _, _, unit, width = lall.shape
    steps = cols // unit
    part = rows // (2 * n_col)

    def slot(s):
        return lambda k, meta: (meta[supers * steps + k * supers + s], 0, 0, 0)

    whole = pl.BlockSpec(uall.shape, lambda k, meta: (0, 0, 0, 0, 0))
    out = pl.BlockSpec((n_col, part, supers * width), lambda k, meta: (0, 0, 0))
    return pl.pallas_call(
        functools.partial(column_kernel, (supers, n_col, blocks)),
        out_shape=(
            jax.ShapeDtypeStruct((n_col, part, supers * width), jnp.float32),
            jax.ShapeDtypeStruct((n_col, part, supers * width), jnp.float32),
            jax.ShapeDtypeStruct((supers * width, width), jnp.float32),
        ),
        grid_spec=pltpu.PrefetchScalarGridSpec(
            num_scalar_prefetch=1,
            grid=(steps,),
            in_specs=[
                pl.BlockSpec(memory_space=pltpu.SMEM),
                pl.BlockSpec((2, rows, unit), lambda k, meta: (0, 0, k)),
            ]
            + [pl.BlockSpec((1, 2, unit, width), slot(s)) for s in range(supers)]
            + [whole, pl.BlockSpec(given.shape, lambda k, meta: (0, 0, 0, 0))],
            out_specs=(out, out, pl.BlockSpec((supers * width, width), lambda k, meta: (0, 0))),
            scratch_shapes=[pltpu.VMEM((supers, rows, 2 * width), jnp.float32)],
        ),
        compiler_params=pltpu.CompilerParams(vmem_limit_bytes=60 * 2**20),
        name="columns",
    )(meta, weights, inverse, *([lall] * supers), uall, given)


def close_kernel(cfg, mine, other, diag, column, total, *scratch):
    (prec, kept, qstage, qrecv, mstage, mrecv, dpole, dz, dzrecv, dx,
     p_send, p_recv, q_send, q_recv, m_send, m_recv, dp_send, dp_recv, dz_send, dz_recv, dx_send, dx_recv,
     gz_send, gz_recv, gp_send, gp_recv) = scratch
    n, n_col = cfg
    z = lax.axis_index("row")
    x = lax.axis_index("col")
    p = lax.axis_index("pole")
    high = diag.shape[0] // 2
    slab = high // n

    def remote(src, dst, send, recv, to):
        return pltpu.make_async_remote_copy(
            src_ref=src, dst_ref=dst, send_sem=send, recv_sem=recv, device_id=to, device_id_type=MESH
        )

    def p_remote(d):
        c = lax.rem(x + d, n_col)
        return remote(other.at[c], prec.at[d], p_send.at[d], p_recv.at[d], {"pole": 1 - p})

    def dp_remote():
        return remote(diag.at[pl.ds(pl.multiple_of((1 - p) * high, 8), high)], dpole, dp_send.at[0], dp_recv.at[0], {"pole": 1 - p})

    def dz_remote(d):
        to = lax.rem(z + d, n)
        return remote(dz.at[to], dzrecv.at[d], dz_send.at[d], dz_recv.at[d], {"row": to})

    def dx_remote(d):
        return remote(dx.at[0], dx.at[d], dx_send.at[d], dx_recv.at[d], {"col": lax.rem(x + d, n_col)})

    def rows_of(pole, place):
        return pl.ds(pl.multiple_of(pole * high + place * slab, 8), slab)

    def gz_remote(d):
        return remote(total.at[rows_of(p, z)], total.at[rows_of(p, z)], gz_send.at[d], gz_recv.at[d], {"row": lax.rem(z + d, n)})

    def gp_remote():
        span = pl.ds(pl.multiple_of(p * high, 8), high)
        return remote(total.at[span], total.at[span], gp_send.at[0], gp_recv.at[0], {"pole": 1 - p})

    def q_remote(d):
        to = {"col": lax.rem(x + d, n_col)}
        return (
            remote(qstage.at[d], qrecv.at[d], q_send.at[d], q_recv.at[d], to),
            remote(mstage.at[d], mrecv.at[d], m_send.at[d], m_recv.at[d], to),
        )

    greet((("row", n, False), ("col", n_col, False), ("pole", 2, False)))
    dp_remote().start()
    for d in range(1, n_col):
        p_remote(d).start()
    p_remote(0).start()

    dp_remote().wait_recv()
    for i in range(n):
        dz[i] = diag[pl.ds(pl.multiple_of(p * high + i * slab, 8), slab)] + dpole[i * slab:(i + 1) * slab]
    for d in range(1, n):
        dz_remote(d).start()

    for d in range(1, n_col):
        p_remote(d).wait_recv()
        code, scale = packed(mine[lax.rem(x + d, n_col)] + prec[d])
        qstage[d] = code
        mstage[d] = jnp.broadcast_to(scale, mstage.shape[1:])
        for copy in q_remote(d):
            copy.start()

    for d in range(1, n):
        dz_remote(d).wait_recv()
    value = dz[z]
    for d in range(1, n):
        value = value + dzrecv[d]
    dx[0] = value
    for d in range(1, n_col):
        dx_remote(d).start()
    p_remote(0).wait_recv()
    kept[...] = mine[x] + prec[0]
    for d in range(1, n_col):
        dx_remote(d).wait_recv()
    value = dx[lax.rem(x + n_col - 0, n_col)]
    for origin in range(1, n_col):
        value = value + dx[lax.rem(x + n_col - origin, n_col)]
    total[rows_of(p, z)] = value
    for d in range(1, n):
        gz_remote(d).start()
    for d in range(1, n):
        gz_remote(d).wait_send()
        gz_in = lax.rem(z + n - d, n)
        remote(total.at[rows_of(p, gz_in)], total.at[rows_of(p, gz_in)], gz_send.at[d], gz_recv.at[d], {"row": gz_in}).wait_recv()
    gp_remote().start()

    for d in range(1, n_col):
        for copy in q_remote(d):
            copy.wait_recv()
        kept[...] = kept[...] + unpacked(qrecv[d], mrecv[d, :1])
    column[...] = kept[...]
    span = pl.ds(pl.multiple_of((1 - p) * high, 8), high)
    gp_remote().wait_send()
    remote(total.at[span], total.at[span], gp_send.at[0], gp_recv.at[0], {"pole": 1 - p}).wait_recv()

    dp_remote().wait_send()
    for d in range(n_col):
        p_remote(d).wait_send()
    for d in range(1, n):
        dz_remote(d).wait_send()
    for d in range(1, n_col):
        dx_remote(d).wait_send()
        for copy in q_remote(d):
            copy.wait_send()


def close_call(mine, other, diag, n, n_col):
    _, part, wide = mine.shape
    tall, width = diag.shape
    slab = tall // 2 // n
    dma = pltpu.SemaphoreType.DMA
    vmem = pl.BlockSpec(memory_space=pltpu.VMEM)
    return pl.pallas_call(
        functools.partial(close_kernel, (n, n_col)),
        out_shape=(
            jax.ShapeDtypeStruct((part, wide), jnp.float32),
            jax.ShapeDtypeStruct((tall, width), jnp.float32),
        ),
        in_specs=[vmem, pl.BlockSpec(memory_space=pl.ANY), vmem],
        out_specs=(vmem, vmem),
        scratch_shapes=[
            pltpu.VMEM((n_col, part, wide), jnp.float32),
            pltpu.VMEM((part, wide), jnp.float32),
            pltpu.VMEM((n_col, part, wide), jnp.int16),
            pltpu.VMEM((n_col, part, wide), jnp.int16),
            pltpu.VMEM((n_col, 8, wide), jnp.float32),
            pltpu.VMEM((n_col, 8, wide), jnp.float32),
            pltpu.VMEM((tall // 2, width), jnp.float32),
            pltpu.VMEM((n, slab, width), jnp.float32),
            pltpu.VMEM((n, slab, width), jnp.float32),
            pltpu.VMEM((n_col, slab, width), jnp.float32),
            dma((n_col,)), dma((n_col,)), dma((n_col,)), dma((n_col,)), dma((n_col,)), dma((n_col,)),
            dma((1,)), dma((1,)), dma((n,)), dma((n,)), dma((n_col,)), dma((n_col,)),
            dma((n,)), dma((n,)), dma((1,)), dma((1,)),
        ],
        compiler_params=pltpu.CompilerParams(collective_id=2, has_side_effects=True, vmem_limit_bytes=40 * 2**20),
        name="close",
    )(mine, other, diag)


def plan_kernel(cfg, pattern, order, usual, full, flag, keep, count):
    n, n_col, blocks, unit, width = cfg
    supers, entries = pattern.shape
    z = lax.axis_index("row")
    x = lax.axis_index("col")
    p = lax.axis_index("pole")
    per = supers * blocks
    units = n * n_col * blocks
    steps = n * blocks
    split = width // unit

    def clear(i, carry):
        keep[i] = 0
        return carry

    lax.fori_loop(0, supers * units, clear, 0)

    def mark(i, carry):
        s = i // entries
        at = s * units + pattern[s, lax.rem(i, entries)] * split
        for r in range(split):
            keep[at + r] = 1
        return carry

    lax.fori_loop(0, supers * entries, mark, 0)

    def number(i, carry):
        total = jnp.int32(0)
        for s in range(supers):
            for b in range(blocks):
                total = total + keep[s * units + i * blocks + b]
        count[i] = total
        return carry

    lax.fori_loop(0, n * n_col, number, 0)

    caps = usual_caps(n, per)

    def fit(i, over):
        down = jnp.int32(0)
        up = jnp.int32(0)
        for d in range(1, n):
            down = down + count[i * n + n - d]
            up = up + count[i * n + d - 1]
            over = jnp.maximum(over, jnp.maximum(down, up) - caps[d])
        return over

    over = lax.fori_loop(0, n_col, fit, jnp.int32(0))
    flag[...] = jnp.broadcast_to(over, flag.shape)

    def pack(r, rank):
        s = r // blocks
        k = keep[s * units + (x * n + z) * blocks + lax.rem(r, blocks)]
        order[r] = 0

        @pl.when(k > 0)
        def _():
            order[rank] = r

        return rank + k

    lax.fori_loop(0, per, pack, jnp.int32(0))

    def around(i, sums):
        k = count[x * n + i]
        return sums[0] + jnp.where(i > z, k, 0), sums[1] + jnp.where(i < z, k, 0)

    above, below = lax.fori_loop(0, n, around, (jnp.int32(0), jnp.int32(0)))
    order[per] = above
    order[per + 1] = below

    base = 2 * supers * steps
    for table in (usual, full):
        table[base] = p
        table[base + 1] = jnp.logical_and(z == 0, x == 0).astype(jnp.int32)
        for d in range(n_col):
            table[base + 2 + d] = lax.rem(x - d + n_col, n_col) * blocks * unit

    def rows(i, carry):
        kb = i // supers
        origin = lax.rem(x - kb // blocks + n_col, n_col)
        k = keep[lax.rem(i, supers) * units + (z * n_col + origin) * blocks + lax.rem(kb, blocks)]
        order[per + 2 + i] = k
        usual[base + 2 + n_col + i] = k
        full[base + 2 + n_col + i] = k
        return carry

    lax.fori_loop(0, n_col * blocks * supers, rows, 0)

    def device(at, before):
        here = count[x * n + at]
        after = jnp.int32(0)
        for i in range(n):
            after = after + jnp.where(i > at, count[x * n + i], 0)

        def pair(r, rank):
            s = r // blocks
            b = lax.rem(r, blocks)
            k = keep[s * units + (x * n + at) * blocks + b]
            down = blocks * (at - z - 1) + rank + jnp.where(rank < blocks, 0, after)
            up = blocks * (z - 1 - at) + rank + jnp.where(rank < blocks, 0, before)
            to = (at * blocks + b) * supers + s
            for table, sizes in ((usual, caps), (full, full_caps(n, per))):
                place = jnp.where(at == z, r, jnp.where(at > z, per + down, per + room(sizes) - 1 - up))
                table[to] = k
                table[supers * steps + to] = jnp.where(k > 0, place, 0)
            return rank + k

        lax.fori_loop(0, per, pair, jnp.int32(0))
        return before + here

    lax.fori_loop(0, n, device, jnp.int32(0))


def plan_call(pattern, sizes, unit, width, blocks):
    n, n_col = sizes
    supers, _ = pattern.shape
    per = supers * blocks
    table = 2 * supers * n * blocks + 2 + n_col + n_col * blocks * supers
    smem = pl.BlockSpec(memory_space=pltpu.SMEM)
    return pl.pallas_call(
        functools.partial(plan_kernel, (n, n_col, blocks, unit, width)),
        out_shape=(
            jax.ShapeDtypeStruct((per + 2 + n_col * blocks * supers,), jnp.int32),
            jax.ShapeDtypeStruct((table,), jnp.int32),
            jax.ShapeDtypeStruct((table,), jnp.int32),
            jax.ShapeDtypeStruct((8, 128), jnp.int32),
        ),
        in_specs=[smem],
        out_specs=(smem, smem, smem, pl.BlockSpec(memory_space=pltpu.VMEM)),
        scratch_shapes=[pltpu.SMEM((supers * n * n_col * blocks,), jnp.int32), pltpu.SMEM((n * n_col,), jnp.int32)],
        name="plan",
    )(pattern)


def body(inverse, lower, upper, diag_inverse, weights, pattern):
    n = lax.axis_size("row")
    n_col = lax.axis_size("col")
    n_groups = lax.axis_size("groups")
    _, local, _, supers, width = lower.shape
    inverse = inverse[0]
    unit = min(width, local)
    blocks = local // unit
    per = supers * blocks
    weights = weights[0]
    order, usual, full, flag = plan_call(pattern, (n, n_col), unit, width, blocks)
    own_l = jnp.transpose(lower[0].reshape(blocks, unit, 2, supers, width), (3, 0, 2, 1, 4)).reshape(per, 2, unit, width)
    own_u = jnp.transpose(upper[0].reshape(blocks, unit, 2, supers, width), (0, 2, 3, 1, 4))
    lall, uall, row, flags = stream_call(order, weights, flag, inverse, own_l, own_u, (n, n_col, n_groups))

    def columns(meta, lall):
        return column_call(meta, weights, inverse, lall, uall, diag_inverse[0], (n_col, supers, blocks))

    mine, other, diag = lax.cond(
        jnp.max(flags) <= 0,
        lambda: columns(usual, lall),
        lambda: columns(full, refill_call(order, own_l, n, blocks)),
    )
    column, diagonal = close_call(mine, other, diag, n, n_col)
    row_density = jnp.transpose(row).reshape(-1, supers, width)
    return (column.reshape(-1, supers, width), row_density, diagonal.reshape(supers, width, width))


def solution(mesh):
    return jax.shard_map(
        body,
        mesh=mesh,
        in_specs=(
            P(("groups", "pole"), None, "row", "col"),
            P(("groups", "pole"), ("col", "row"), None, None, None),
            P(("groups", "pole"), ("row", "col"), None, None, None),
            P(("groups", "pole"), None, None, None, None),
            P(("groups", "pole"), None),
            P("groups", None),
        ),
        out_specs=(
            P(("groups", "row", "col", "pole"), None, None),
            P(("groups", "col", "row", "pole"), None, None),
            P("groups", None, None),
        ),
        check_vma=False,
    )
```

```python
import functools
import math

import jax
import jax.numpy as jnp
from jax import lax
from jax.experimental import pallas as pl
from jax.experimental.pallas import tpu as pltpu
from jax.sharding import PartitionSpec as P

MESH = pl.DeviceIdType.MESH
RING = 6
SLOTS = 2
TOP = 32767.0


def full_caps(n, per):
    return [per * d for d in range(n)]


def room(caps):
    n = len(caps)
    return max(caps[z] + caps[n - 1 - z] for z in range(n)) + 1


def stepped(caps, count):
    total = jnp.int32(0)
    for d in range(1, len(caps)):
        total = total + jnp.where(count >= d, caps[d] - caps[d - 1], 0)
    return total


class Streams:
    def __init__(self, caps, first, n, order, lown, lin, stage, send_sem, recv_sem, out_sem, lall):
        self.caps, self.first, self.n = caps, first, n
        self.order, self.lown, self.lin, self.stage = order, lown, lin, stage
        self.send_sem, self.recv_sem, self.out_sem, self.lall = send_sem, recv_sem, out_sem, lall
        self.per = lown.shape[0]
        self.size = lin.shape[0]
        self.z = lax.axis_index("row")
        z = self.z
        self.sent = (jnp.where(z > 0, stepped(caps, n - z), 0), jnp.where(z < n - 1, stepped(caps, z + 1), 0))
        self.taken = (stepped(caps, n - 1 - z), stepped(caps, z))
        self.events = max(caps) - first

    def place(self, way, c):
        return c if way == 0 else self.size - 1 - c

    def remote(self, way, c):
        slot = lax.rem(c, RING)
        place = self.place(way, c)
        return pltpu.make_async_remote_copy(
            src_ref=self.stage.at[way, slot],
            dst_ref=self.lin.at[place],
            send_sem=self.send_sem.at[way, slot],
            recv_sem=self.recv_sem.at[place],
            device_id={"row": self.z - 1 if way == 0 else self.z + 1},
            device_id_type=MESH,
        )

    def kept(self, way, c):
        place = self.place(way, c)
        return pltpu.make_async_copy(self.lin.at[place], self.lall.at[self.per + place], self.out_sem.at[place])

    def begin(self):
        for way in range(2):
            @pl.when(self.sent[way] > 0)
            def _():
                for c in range(self.first):
                    if c >= RING:
                        self.remote(way, c - RING).wait_send()
                    self.stage[way, c % RING] = self.lown[self.order[c]]
                    self.remote(way, c).start()

    def forward(self, d):
        c = d + self.first
        for way in range(2):
            @pl.when(c < self.sent[way])
            def _():
                @pl.when(d < self.taken[way])
                def _():
                    self.remote(way, d).wait_recv()
                    self.kept(way, d).start()

                @pl.when(c >= RING)
                def _():
                    self.remote(way, c - RING).wait_send()

                count = self.order[self.per + way]
                mine = self.lown[self.order[jnp.clip(c - count, 0, self.per - 1)]]
                arrived = self.lin[self.place(way, jnp.clip(d, 0, jnp.maximum(self.taken[way] - 1, 0)))]
                self.stage[way, lax.rem(c, RING)] = jnp.where(d < count, arrived, mine)
                self.remote(way, c).start()

    def drain(self):
        def step(c, carry):
            for way in range(2):
                @pl.when(jnp.logical_and(c < self.taken[way], c + self.first >= self.sent[way]))
                def _():
                    self.remote(way, c).wait_recv()
                    self.kept(way, c).start()

                @pl.when(jnp.logical_and(c < self.sent[way], c + RING >= self.sent[way]))
                def _():
                    self.remote(way, c).wait_send()
            return carry

        lax.fori_loop(0, max(self.caps), step, 0)

        def last(c, carry):
            for way in range(2):
                @pl.when(c < self.taken[way])
                def _():
                    self.kept(way, c).wait()
            return carry

        lax.fori_loop(0, max(self.caps), last, 0)


def greet(targets):
    barrier = pltpu.get_barrier_semaphore()
    total = jnp.int32(0)
    for axis, size, near in targets:
        me = lax.axis_index(axis)
        if near:
            for step in (-1, 1):
                there = jnp.logical_and(me + step >= 0, me + step < size)

                @pl.when(there)
                def _():
                    pl.semaphore_signal(barrier, inc=1, device_id={axis: me + step}, device_id_type=MESH)

                total = total + there.astype(jnp.int32)
        else:
            for d in range(1, size):
                pl.semaphore_signal(barrier, inc=1, device_id={axis: lax.rem(me + d, size)}, device_id_type=MESH)
            total = total + (size - 1)
    pl.semaphore_wait(barrier, total)


def packed(value):
    most = jnp.max(jnp.abs(value), axis=0, keepdims=True)
    factor = jnp.where(most > 0, TOP / jnp.maximum(most, 1e-30), 0.0)
    return jnp.round(value * factor).astype(jnp.int32).astype(jnp.int16), most * (1.0 / TOP)


def unpacked(code, scale):
    return code.astype(jnp.int32).astype(jnp.float32) * scale


def stream_kernel(cfg, order, weights, inverse, own_l, own_u, lall, uall, row_out, *scratch):
    (acc, lhs, abuf, ubuf, lown, lin, stage, prec, qstage, qrecv, mstage, mrecv,
     a_sem, u_send, u_recv, l_sem, s_send, s_recv, s_out, p_send, p_recv, q_send, q_recv, m_send, m_recv) = scratch
    n, n_col, caps = cfg
    per = lown.shape[0]
    supers, kbs, _, unit, width = ubuf.shape
    blocks = kbs // n_col
    half = acc.shape[2]
    tile = 2 * half
    z = lax.axis_index("row")
    x = lax.axis_index("col")
    p = lax.axis_index("pole")

    lcopy = pltpu.make_async_copy(own_l, lown, l_sem.at[0])
    lcopy.start()
    ucopy = pltpu.make_async_copy(own_u, ubuf.at[:, pl.ds(0, blocks)], l_sem.at[1])
    ucopy.start()

    def a_copy(t):
        kb = t // n
        origin = lax.rem(x - kb // blocks + n_col, n_col)
        row = (origin * blocks + lax.rem(kb, blocks)) * unit
        return pltpu.make_async_copy(
            inverse.at[:, pl.ds(pl.multiple_of(row, unit), unit), pl.ds(pl.multiple_of(lax.rem(t, n) * tile, tile), tile)],
            abuf.at[lax.rem(t, 3)],
            a_sem.at[lax.rem(t, 3)],
        )

    a_copy(0).start()
    a_copy(1).start()
    greet((("row", n, True), ("col", n_col, False), ("pole", 2, False)))

    def u_remote(d, b):
        return pltpu.make_async_remote_copy(
            src_ref=own_u.at[:, b],
            dst_ref=ubuf.at[:, d * blocks + b],
            send_sem=u_send.at[d * blocks + b],
            recv_sem=u_recv.at[d * blocks + b],
            device_id={"col": lax.rem(x + d, n_col)},
            device_id_type=MESH,
        )

    for b in range(blocks):
        for d in range(1, n_col):
            u_remote(d, b).start()

    lcopy.wait()
    streams = Streams(caps, blocks, n, order, lown, lin, stage, s_send, s_recv, s_out, lall)
    streams.begin()
    lout = pltpu.make_async_copy(lown, lall.at[pl.ds(0, per)], l_sem.at[0])
    lout.start()
    ucopy.wait()

    tiles = kbs * n
    early = blocks * n
    events = streams.events
    events_early = events * 5 // 18
    events_late = events - events_early
    late = tiles - early

    def due(t):
        if late == 0:
            return t * events // early
        return jnp.where(t < early, t * events_early // early, events_early + (t - early) * events_late // late)

    def row_tile(t, carry):
        kb = t // n
        j = lax.rem(t, n)

        @pl.when(j == 0)
        def _():
            @pl.when(kb >= blocks)
            def _():
                u_remote(kb // blocks, lax.rem(kb, blocks)).wait_recv()

            for s in range(supers):
                kept = order[per + 2 + kb * supers + s] > 0
                real = jnp.where(kept, ubuf[s, kb, 0].astype(jnp.float32), 0.0)
                imag = jnp.where(kept, ubuf[s, kb, 1].astype(jnp.float32), 0.0)
                span = slice(s * width, (s + 1) * width)
                for i, value in enumerate((weights[1] * real + weights[0] * imag, weights[0] * real - weights[1] * imag)):
                    turned = jnp.transpose(value)
                    high = turned.astype(jnp.bfloat16)
                    lhs[0, span, i * unit:(i + 1) * unit] = high
                    lhs[1, span, i * unit:(i + 1) * unit] = (turned - high.astype(jnp.float32)).astype(jnp.bfloat16)

        @pl.when(t + 2 < tiles)
        def _():
            a_copy(t + 2).start()

        a_copy(t).wait()
        slot = lax.rem(t, 3)
        for q in range(2):
            right = abuf[slot, :, :, q * half:(q + 1) * half].reshape(2 * unit, half)
            total = jnp.dot(lhs[0], right, preferred_element_type=jnp.float32) + jnp.dot(
                lhs[1], right, preferred_element_type=jnp.float32
            )
            before = acc[2 * j + q]
            acc[2 * j + q] = total + jnp.where(kb == 0, jnp.zeros_like(before), before)

        now = due(t)

        def some(d, carry):
            streams.forward(d)
            return carry

        lax.fori_loop(now, due(t + 1), some, 0)
        return carry

    lax.fori_loop(0, tiles, row_tile, 0)

    uout = pltpu.make_async_copy(ubuf, uall, l_sem.at[1])
    uout.start()

    def p_remote(ch):
        return pltpu.make_async_remote_copy(
            src_ref=acc.at[2 * ch + 1 - p],
            dst_ref=prec.at[ch],
            send_sem=p_send.at[ch],
            recv_sem=p_recv.at[ch],
            device_id={"pole": 1 - p},
            device_id_type=MESH,
        )

    for i in range((n + 1) // 2):
        p_remote(n - 1 - i).start()
        if i != n - 1 - i:
            p_remote(i).start()

    def q_remote(way, i):
        to = {"row": z + 1 if way == 0 else z - 1}
        return (
            pltpu.make_async_remote_copy(
                src_ref=qstage.at[way, i], dst_ref=qrecv.at[way, i], send_sem=q_send.at[way, i], recv_sem=q_recv.at[way, i],
                device_id=to, device_id_type=MESH,
            ),
            pltpu.make_async_remote_copy(
                src_ref=mstage.at[way, i], dst_ref=mrecv.at[way, i], send_sem=m_send.at[way, i], recv_sem=m_recv.at[way, i],
                device_id=to, device_id_type=MESH,
            ),
        )

    def arrived(way, i):
        for copy in q_remote(way, i):
            copy.wait_recv()
        return unpacked(qrecv[way, i], mrecv[way, i, :1])

    def row_step(i, carry):
        for way in range(2):
            ch = n - 1 - i if way == 0 else i

            @pl.when(z < ch if way == 0 else z > ch)
            def _():
                p_remote(ch).wait_recv()
                acc[2 * ch + p] = acc[2 * ch + p] + prec[ch]

                @pl.when(z > 0 if way == 0 else z < n - 1)
                def _():
                    acc[2 * ch + p] = acc[2 * ch + p] + arrived(way, i)

                code, scale = packed(acc[2 * ch + p])
                qstage[way, i] = code
                mstage[way, i] = jnp.broadcast_to(scale, mstage.shape[2:])
                for copy in q_remote(way, i):
                    copy.start()
        return carry

    lax.fori_loop(0, n - 1, row_step, 0)

    p_remote(z).wait_recv()
    row_out[...] = acc[2 * z + p] + prec[z]

    @pl.when(z > 0)
    def _():
        row_out[...] = row_out[...] + arrived(0, n - 1 - z)

    @pl.when(z < n - 1)
    def _():
        row_out[...] = row_out[...] + arrived(1, z)

    row_out[...] = -row_out[...]
    streams.drain()

    def finish(i, carry):
        for way in range(2):
            ch = n - 1 - i if way == 0 else i

            @pl.when(z < ch if way == 0 else z > ch)
            def _():
                for copy in q_remote(way, i):
                    copy.wait_send()
        return carry

    lax.fori_loop(0, n - 1, finish, 0)
    for ch in range(n):
        p_remote(ch).wait_send()
    for d in range(1, n_col):
        for b in range(blocks):
            u_remote(d, b).wait_send()
    lout.wait()
    uout.wait()


def stream_call(order, weights, inverse, own_l, own_u, sizes):
    n, n_col = sizes
    _, rows, cols = inverse.shape
    per, _, unit, width = own_l.shape
    supers, blocks = own_u.shape[:2]
    wide = supers * width
    caps = full_caps(n, per)
    kbs = blocks * n_col
    half = cols // n // 2
    space = room(caps)
    dma = pltpu.SemaphoreType.DMA
    scratch = [
        pltpu.VMEM((2 * n, wide, half), jnp.float32),
        pltpu.VMEM((2, wide, 2 * unit), jnp.bfloat16),
        pltpu.VMEM((3, 2, unit, 2 * half), jnp.bfloat16),
        pltpu.VMEM((supers, kbs, 2, unit, width), jnp.bfloat16),
        pltpu.VMEM((per, 2, unit, width), jnp.bfloat16),
        pltpu.VMEM((space, 2, unit, width), jnp.bfloat16),
        pltpu.VMEM((2, RING, 2, unit, width), jnp.bfloat16),
        pltpu.VMEM((n, wide, half), jnp.float32),
        pltpu.VMEM((2, n - 1, wide, half), jnp.int16),
        pltpu.VMEM((2, n - 1, wide, half), jnp.int16),
        pltpu.VMEM((2, n - 1, 8, half), jnp.float32),
        pltpu.VMEM((2, n - 1, 8, half), jnp.float32),
        dma((3,)), dma((kbs,)), dma((kbs,)), dma((2,)),
        dma((2, RING)), dma((space,)), dma((space,)),
        dma((n,)), dma((n,)),
        dma((2, n - 1)), dma((2, n - 1)), dma((2, n - 1)), dma((2, n - 1)),
    ]
    smem = pl.BlockSpec(memory_space=pltpu.SMEM)
    vmem = pl.BlockSpec(memory_space=pltpu.VMEM)
    hbm = pl.BlockSpec(memory_space=pl.ANY)
    return pl.pallas_call(
        functools.partial(stream_kernel, (n, n_col, caps)),
        out_shape=(
            jax.ShapeDtypeStruct((per + space, 2, unit, width), jnp.bfloat16),
            jax.ShapeDtypeStruct((supers, kbs, 2, unit, width), jnp.bfloat16),
            jax.ShapeDtypeStruct((wide, half), jnp.float32),
        ),
        in_specs=[smem, smem, hbm, hbm, hbm],
        out_specs=(hbm, hbm, vmem),
        scratch_shapes=scratch,
        compiler_params=pltpu.CompilerParams(collective_id=0, has_side_effects=True, vmem_limit_bytes=62 * 2**20),
        name="streams",
    )(order, weights, inverse, own_l, own_u)


def column_kernel(cfg, meta, weights, a_ref, *rest):
    supers, n_col, blocks = cfg
    l_refs = rest[:supers]
    u_ref, given, mine, other, diag, acc = rest[supers:]
    k = pl.program_id(0)
    steps = pl.num_programs(0)
    _, rows, double = acc.shape
    width = double // 2
    unit = a_ref.shape[2]
    base = 2 * supers * steps
    piece = rows

    @pl.when(k == 0)
    def _():
        acc[...] = jnp.zeros_like(acc)

    for s in range(supers):
        @pl.when(meta[k * supers + s] > 0)
        def _():
            real = l_refs[s][0, 0]
            imag = l_refs[s][0, 1]
            right = jnp.concatenate([jnp.concatenate([real, imag], axis=1), jnp.concatenate([-imag, real], axis=1)], axis=0)

            def part(i, carry):
                span = pl.ds(pl.multiple_of(i * piece, piece), piece)
                left = jnp.concatenate([a_ref[0, span], a_ref[1, span]], axis=1)
                acc[s, span] += jnp.dot(left, right, preferred_element_type=jnp.float32)
                return carry

            lax.fori_loop(0, rows // piece, part, 0)

    @pl.when(k == steps - 1)
    def _():
        part = mine.shape[1]
        pole = meta[base]
        for s in range(supers):
            lanes = slice(s * width, (s + 1) * width)
            for c in range(n_col):
                for q in range(2):
                    span = pl.ds((2 * c + q) * part, part)
                    real = acc[s, span, :width]
                    imag = acc[s, span, width:]
                    mixed = weights[0] * imag + weights[1] * real
                    acc[s, span, :width] = mixed
                    acc[s, span, width:] = weights[0] * real - weights[1] * imag

                    @pl.when(pole == q)
                    def _():
                        mine[c, :, lanes] = mixed

                    @pl.when(pole != q)
                    def _():
                        other[c, :, lanes] = mixed

            @pl.when(meta[base + 1] > 0)
            def _():
                diag[lanes, :] = weights[0] * given[s, 1].astype(jnp.float32) + weights[1] * given[s, 0].astype(jnp.float32)

            @pl.when(meta[base + 1] == 0)
            def _():
                diag[lanes, :] = jnp.zeros((width, diag.shape[1]), jnp.float32)

        def one(kb, carry):
            for s in range(supers):
                lanes = slice(s * width, (s + 1) * width)

                @pl.when(meta[base + 2 + n_col + kb * supers + s] > 0)
                def _():
                    start = pl.multiple_of(meta[base + 2 + kb // blocks] + lax.rem(kb, blocks) * unit, unit)
                    total = jnp.zeros((width, width), jnp.float32)
                    for c in range(2):
                        value = acc[s, pl.ds(start, unit), c * width:(c + 1) * width]
                        high = value.astype(jnp.bfloat16)
                        low = (value - high.astype(jnp.float32)).astype(jnp.bfloat16)
                        turned = jnp.transpose(u_ref[s, kb, c])
                        total += jnp.dot(turned, high, preferred_element_type=jnp.float32) + jnp.dot(
                            turned, low, preferred_element_type=jnp.float32
                        )
                    diag[lanes, :] += total
            return carry

        lax.fori_loop(0, u_ref.shape[1], one, 0)


def column_call(meta, weights, inverse, lall, uall, given, sizes):
    n_col, supers, blocks = sizes
    _, rows, cols = inverse.shape
    _, _, unit, width = lall.shape
    steps = cols // unit
    part = rows // (2 * n_col)

    def slot(s):
        return lambda k, meta: (meta[supers * steps + k * supers + s], 0, 0, 0)

    whole = pl.BlockSpec(uall.shape, lambda k, meta: (0, 0, 0, 0, 0))
    out = pl.BlockSpec((n_col, part, supers * width), lambda k, meta: (0, 0, 0))
    return pl.pallas_call(
        functools.partial(column_kernel, (supers, n_col, blocks)),
        out_shape=(
            jax.ShapeDtypeStruct((n_col, part, supers * width), jnp.float32),
            jax.ShapeDtypeStruct((n_col, part, supers * width), jnp.float32),
            jax.ShapeDtypeStruct((supers * width, width), jnp.float32),
        ),
        grid_spec=pltpu.PrefetchScalarGridSpec(
            num_scalar_prefetch=1,
            grid=(steps,),
            in_specs=[
                pl.BlockSpec(memory_space=pltpu.SMEM),
                pl.BlockSpec((2, rows, unit), lambda k, meta: (0, 0, k)),
            ]
            + [pl.BlockSpec((1, 2, unit, width), slot(s)) for s in range(supers)]
            + [whole, pl.BlockSpec(given.shape, lambda k, meta: (0, 0, 0, 0))],
            out_specs=(out, out, pl.BlockSpec((supers * width, width), lambda k, meta: (0, 0))),
            scratch_shapes=[pltpu.VMEM((supers, rows, 2 * width), jnp.float32)],
        ),
        compiler_params=pltpu.CompilerParams(vmem_limit_bytes=60 * 2**20),
        name="columns",
    )(meta, weights, inverse, *([lall] * supers), uall, given)


def close_kernel(cfg, mine, other, diag, column, total, *scratch):
    (prec, kept, qstage, qrecv, mstage, mrecv, dpole, dz, dzrecv, dx,
     p_send, p_recv, q_send, q_recv, m_send, m_recv, dp_send, dp_recv, dz_send, dz_recv, dx_send, dx_recv,
     gz_send, gz_recv, gp_send, gp_recv) = scratch
    n, n_col = cfg
    z = lax.axis_index("row")
    x = lax.axis_index("col")
    p = lax.axis_index("pole")
    high = diag.shape[0] // 2
    slab = high // n

    def remote(src, dst, send, recv, to):
        return pltpu.make_async_remote_copy(
            src_ref=src, dst_ref=dst, send_sem=send, recv_sem=recv, device_id=to, device_id_type=MESH
        )

    def p_remote(d):
        c = lax.rem(x + d, n_col)
        return remote(other.at[c], prec.at[d], p_send.at[d], p_recv.at[d], {"pole": 1 - p})

    def dp_remote():
        return remote(diag.at[pl.ds(pl.multiple_of((1 - p) * high, 8), high)], dpole, dp_send.at[0], dp_recv.at[0], {"pole": 1 - p})

    def dz_remote(d):
        to = lax.rem(z + d, n)
        return remote(dz.at[to], dzrecv.at[d], dz_send.at[d], dz_recv.at[d], {"row": to})

    def dx_remote(d):
        return remote(dx.at[0], dx.at[d], dx_send.at[d], dx_recv.at[d], {"col": lax.rem(x + d, n_col)})

    def rows_of(pole, place):
        return pl.ds(pl.multiple_of(pole * high + place * slab, 8), slab)

    def gz_remote(d):
        return remote(total.at[rows_of(p, z)], total.at[rows_of(p, z)], gz_send.at[d], gz_recv.at[d], {"row": lax.rem(z + d, n)})

    def gp_remote():
        span = pl.ds(pl.multiple_of(p * high, 8), high)
        return remote(total.at[span], total.at[span], gp_send.at[0], gp_recv.at[0], {"pole": 1 - p})

    def q_remote(d):
        to = {"col": lax.rem(x + d, n_col)}
        return (
            remote(qstage.at[d], qrecv.at[d], q_send.at[d], q_recv.at[d], to),
            remote(mstage.at[d], mrecv.at[d], m_send.at[d], m_recv.at[d], to),
        )

    greet((("row", n, False), ("col", n_col, False), ("pole", 2, False)))
    dp_remote().start()
    for d in range(1, n_col):
        p_remote(d).start()
    p_remote(0).start()

    dp_remote().wait_recv()
    for i in range(n):
        dz[i] = diag[pl.ds(pl.multiple_of(p * high + i * slab, 8), slab)] + dpole[i * slab:(i + 1) * slab]
    for d in range(1, n):
        dz_remote(d).start()

    for d in range(1, n_col):
        p_remote(d).wait_recv()
        code, scale = packed(mine[lax.rem(x + d, n_col)] + prec[d])
        qstage[d] = code
        mstage[d] = jnp.broadcast_to(scale, mstage.shape[1:])
        for copy in q_remote(d):
            copy.start()

    for d in range(1, n):
        dz_remote(d).wait_recv()
    value = dz[z]
    for d in range(1, n):
        value = value + dzrecv[d]
    dx[0] = value
    for d in range(1, n_col):
        dx_remote(d).start()
    p_remote(0).wait_recv()
    kept[...] = mine[x] + prec[0]
    for d in range(1, n_col):
        dx_remote(d).wait_recv()
    value = dx[lax.rem(x + n_col - 0, n_col)]
    for origin in range(1, n_col):
        value = value + dx[lax.rem(x + n_col - origin, n_col)]
    total[rows_of(p, z)] = value
    for d in range(1, n):
        gz_remote(d).start()
    for d in range(1, n):
        gz_remote(d).wait_send()
        gz_in = lax.rem(z + n - d, n)
        remote(total.at[rows_of(p, gz_in)], total.at[rows_of(p, gz_in)], gz_send.at[d], gz_recv.at[d], {"row": gz_in}).wait_recv()
    gp_remote().start()

    for d in range(1, n_col):
        for copy in q_remote(d):
            copy.wait_recv()
        kept[...] = kept[...] + unpacked(qrecv[d], mrecv[d, :1])
    column[...] = -kept[...]
    span = pl.ds(pl.multiple_of((1 - p) * high, 8), high)
    gp_remote().wait_send()
    remote(total.at[span], total.at[span], gp_send.at[0], gp_recv.at[0], {"pole": 1 - p}).wait_recv()

    dp_remote().wait_send()
    for d in range(n_col):
        p_remote(d).wait_send()
    for d in range(1, n):
        dz_remote(d).wait_send()
    for d in range(1, n_col):
        dx_remote(d).wait_send()
        for copy in q_remote(d):
            copy.wait_send()


def close_call(mine, other, diag, n, n_col):
    _, part, wide = mine.shape
    tall, width = diag.shape
    slab = tall // 2 // n
    dma = pltpu.SemaphoreType.DMA
    vmem = pl.BlockSpec(memory_space=pltpu.VMEM)
    return pl.pallas_call(
        functools.partial(close_kernel, (n, n_col)),
        out_shape=(
            jax.ShapeDtypeStruct((part, wide), jnp.float32),
            jax.ShapeDtypeStruct((tall, width), jnp.float32),
        ),
        in_specs=[vmem, pl.BlockSpec(memory_space=pl.ANY), vmem],
        out_specs=(vmem, vmem),
        scratch_shapes=[
            pltpu.VMEM((n_col, part, wide), jnp.float32),
            pltpu.VMEM((part, wide), jnp.float32),
            pltpu.VMEM((n_col, part, wide), jnp.int16),
            pltpu.VMEM((n_col, part, wide), jnp.int16),
            pltpu.VMEM((n_col, 8, wide), jnp.float32),
            pltpu.VMEM((n_col, 8, wide), jnp.float32),
            pltpu.VMEM((tall // 2, width), jnp.float32),
            pltpu.VMEM((n, slab, width), jnp.float32),
            pltpu.VMEM((n, slab, width), jnp.float32),
            pltpu.VMEM((n_col, slab, width), jnp.float32),
            dma((n_col,)), dma((n_col,)), dma((n_col,)), dma((n_col,)), dma((n_col,)), dma((n_col,)),
            dma((1,)), dma((1,)), dma((n,)), dma((n,)), dma((n_col,)), dma((n_col,)),
            dma((n,)), dma((n,)), dma((1,)), dma((1,)),
        ],
        compiler_params=pltpu.CompilerParams(collective_id=2, has_side_effects=True, vmem_limit_bytes=40 * 2**20),
        name="close",
    )(mine, other, diag)


def plan_kernel(cfg, pattern, order, full, keep, count):
    n, n_col, blocks, unit, width = cfg
    supers, entries = pattern.shape
    z = lax.axis_index("row")
    x = lax.axis_index("col")
    p = lax.axis_index("pole")
    per = supers * blocks
    units = n * n_col * blocks
    steps = n * blocks
    split = width // unit

    def clear(i, carry):
        keep[i] = 0
        return carry

    lax.fori_loop(0, supers * units, clear, 0)

    def mark(i, carry):
        s = i // entries
        at = s * units + pattern[s, lax.rem(i, entries)] * split
        for r in range(split):
            keep[at + r] = 1
        return carry

    lax.fori_loop(0, supers * entries, mark, 0)

    def number(i, carry):
        total = jnp.int32(0)
        for s in range(supers):
            for b in range(blocks):
                total = total + keep[s * units + i * blocks + b]
        count[i] = total
        return carry

    lax.fori_loop(0, n * n_col, number, 0)

    def pack(r, rank):
        s = r // blocks
        k = keep[s * units + (x * n + z) * blocks + lax.rem(r, blocks)]
        order[r] = 0

        @pl.when(k > 0)
        def _():
            order[rank] = r

        return rank + k

    lax.fori_loop(0, per, pack, jnp.int32(0))

    def around(i, sums):
        k = count[x * n + i]
        return sums[0] + jnp.where(i > z, k, 0), sums[1] + jnp.where(i < z, k, 0)

    above, below = lax.fori_loop(0, n, around, (jnp.int32(0), jnp.int32(0)))
    order[per] = above
    order[per + 1] = below

    base = 2 * supers * steps
    full[base] = p
    full[base + 1] = jnp.logical_and(z == 0, x == 0).astype(jnp.int32)
    for d in range(n_col):
        full[base + 2 + d] = lax.rem(x - d + n_col, n_col) * blocks * unit

    def rows(i, carry):
        kb = i // supers
        origin = lax.rem(x - kb // blocks + n_col, n_col)
        k = keep[lax.rem(i, supers) * units + (z * n_col + origin) * blocks + lax.rem(kb, blocks)]
        order[per + 2 + i] = k
        full[base + 2 + n_col + i] = k
        return carry

    lax.fori_loop(0, n_col * blocks * supers, rows, 0)

    def device(at, before):
        here = count[x * n + at]
        after = jnp.int32(0)
        for i in range(n):
            after = after + jnp.where(i > at, count[x * n + i], 0)

        def pair(r, rank):
            s = r // blocks
            b = lax.rem(r, blocks)
            k = keep[s * units + (x * n + at) * blocks + b]
            down = blocks * (at - z - 1) + rank + jnp.where(rank < blocks, 0, after)
            up = blocks * (z - 1 - at) + rank + jnp.where(rank < blocks, 0, before)
            to = (at * blocks + b) * supers + s
            place = jnp.where(at == z, r, jnp.where(at > z, per + down, per + room(full_caps(n, per)) - 1 - up))
            full[to] = k
            full[supers * steps + to] = jnp.where(k > 0, place, 0)
            return rank + k

        lax.fori_loop(0, per, pair, jnp.int32(0))
        return before + here

    lax.fori_loop(0, n, device, jnp.int32(0))


def plan_call(pattern, sizes, unit, width, blocks):
    n, n_col = sizes
    supers, _ = pattern.shape
    per = supers * blocks
    table = 2 * supers * n * blocks + 2 + n_col + n_col * blocks * supers
    smem = pl.BlockSpec(memory_space=pltpu.SMEM)
    return pl.pallas_call(
        functools.partial(plan_kernel, (n, n_col, blocks, unit, width)),
        out_shape=(
            jax.ShapeDtypeStruct((per + 2 + n_col * blocks * supers,), jnp.int32),
            jax.ShapeDtypeStruct((table,), jnp.int32),
        ),
        in_specs=[smem],
        out_specs=(smem, smem),
        scratch_shapes=[pltpu.SMEM((supers * n * n_col * blocks,), jnp.int32), pltpu.SMEM((n * n_col,), jnp.int32)],
        name="plan",
    )(pattern)


def scan_kernel(cfg, pattern, order, over, flags, send, recv):
    n_groups, = cfg
    supers, entries = pattern.shape
    g = lax.axis_index("groups")
    lane = lax.broadcasted_iota(jnp.int32, order.shape, 1)
    row = lax.broadcasted_iota(jnp.int32, order.shape, 0)
    rank = jnp.zeros(order.shape, jnp.int32)
    table = jnp.full(order.shape, -1, jnp.int32)
    for s in range(supers):
        hit = jnp.zeros(order.shape, jnp.int32)
        for j in range(entries):
            hit = jnp.where(lane == pattern[s, j], 1, hit)
        table = jnp.where(jnp.where(row == rank, hit, 0) > 0, s, table)
        rank = rank + hit
    order[...] = table
    bad = jnp.max(jnp.where(rank > SLOTS, 1.0, 0.0))
    flags[0] = jnp.full(flags.shape[1:], bad, jnp.float32)

    def copy(d):
        return pltpu.make_async_remote_copy(
            src_ref=flags.at[0], dst_ref=flags.at[d], send_sem=send.at[d], recv_sem=recv.at[d],
            device_id={"groups": lax.rem(g + d, n_groups)}, device_id_type=MESH,
        )

    greet((("groups", n_groups, False),))
    for d in range(1, n_groups):
        copy(d).start()
    for d in range(1, n_groups):
        copy(d).wait_send()
        copy(d).wait_recv()
    over[0] = jnp.max(flags[...])


def scan_call(pattern, owners, n_groups):
    smem = pl.BlockSpec(memory_space=pltpu.SMEM)
    dma = pltpu.SemaphoreType.DMA
    return pl.pallas_call(
        functools.partial(scan_kernel, (n_groups,)),
        out_shape=(
            jax.ShapeDtypeStruct((8, -(-owners // 128) * 128), jnp.int32),
            jax.ShapeDtypeStruct((1,), jnp.float32),
        ),
        in_specs=[smem],
        out_specs=(pl.BlockSpec(memory_space=pltpu.VMEM), smem),
        scratch_shapes=[pltpu.VMEM((n_groups, 8, 128), jnp.float32), dma((n_groups,)), dma((n_groups,))],
        compiler_params=pltpu.CompilerParams(collective_id=1, has_side_effects=True),
        name="scan",
    )(pattern)


def fused_kernel(cfg, order, weights, inverse, own_l, own_u, given, row_out, mine, other, diag, *scratch):
    (acc, cacc, lhs, rhs, abuf, cbuf, uslots, lin, qstage, qrecv, mstage, mrecv,
     a_sem, c_sem, u_send, u_recv, o_sem, l_send, l_recv, p_send, p_recv, q_send, q_recv, m_send, m_recv, w_sem) = scratch[:26]
    n, n_col, supers = cfg
    z = lax.axis_index("row")
    x = lax.axis_index("col")
    p = lax.axis_index("pole")
    kbs, _, _, unit, width = uslots.shape
    blocks = kbs // n_col
    remote_blocks = (n - 1) * blocks
    half = acc.shape[2]
    tile = 2 * half
    rows = cacc.shape[1]
    apart = len(scratch) > 26
    prec = scratch[26] if apart else cacc
    given_here = scratch[27] if apart else rhs.at[0]
    wide = supers * width

    def lower_owner(k, j):
        return order[j, (x * n * blocks + k) * unit // width]

    def upper_owner(kb, j):
        origin = lax.rem(x - kb // blocks + n_col, n_col)
        return order[j, ((z * n_col + origin) * blocks + lax.rem(kb, blocks)) * unit // width]

    def place_of(ch):
        if not apart:
            fit = rows // wide
            return cacc.at[ch // fit, pl.ds(pl.multiple_of(lax.rem(ch, fit) * wide, wide), wide)]
        return prec.at[ch]

    def a_copy(t):
        kb = t // n
        origin = lax.rem(x - kb // blocks + n_col, n_col)
        row = (origin * blocks + lax.rem(kb, blocks)) * unit
        return pltpu.make_async_copy(
            inverse.at[:, pl.ds(pl.multiple_of(row, unit), unit), pl.ds(pl.multiple_of(lax.rem(t, n) * tile, tile), tile)],
            abuf.at[lax.rem(t, 2)],
            a_sem.at[lax.rem(t, 2)],
        )

    per = supers * blocks
    lcopy = pltpu.make_async_copy(own_l, lin.at[pl.ds(0, per)], o_sem.at[0])
    ucopy = pltpu.make_async_copy(own_u, lin.at[pl.ds(per, per)], o_sem.at[1])
    lcopy.start()
    ucopy.start()
    a_copy(0).start()
    lcopy.wait()
    ucopy.wait()
    for b in range(blocks):
        for j in range(SLOTS):
            chosen = jnp.maximum(lower_owner(z * blocks + b, j), 0)
            lin[(remote_blocks + b) * SLOTS + j] = lin[chosen * blocks + b]
            chosen = jnp.maximum(upper_owner(b, j), 0)
            uslots[b, j] = lin[per + chosen * blocks + b]
    greet((("row", n, True), ("col", n_col, False), ("pole", 2, False)))

    def u_remote(d, b):
        return pltpu.make_async_remote_copy(
            src_ref=uslots.at[b], dst_ref=uslots.at[d * blocks + b],
            send_sem=u_send.at[d * blocks + b], recv_sem=u_recv.at[d * blocks + b],
            device_id={"col": lax.rem(x + d, n_col)}, device_id_type=MESH,
        )

    sent = (jnp.where(z > 0, (n - z) * blocks, 0), jnp.where(z < n - 1, (z + 1) * blocks, 0))
    taken = ((n - 1 - z) * blocks, z * blocks)

    def l_place(way, c):
        return c if way == 0 else remote_blocks - 1 - c

    def l_remote(way, c, source):
        return pltpu.make_async_remote_copy(
            src_ref=lin.at[pl.ds(source * SLOTS, SLOTS)], dst_ref=lin.at[pl.ds(l_place(way, c) * SLOTS, SLOTS)],
            send_sem=l_send.at[way, c], recv_sem=l_recv.at[l_place(way, c)],
            device_id={"row": z - 1 if way == 0 else z + 1}, device_id_type=MESH,
        )

    for b in range(blocks):
        for d in range(1, n_col):
            u_remote(d, b).start()
        for way in range(2):
            @pl.when(sent[way] > 0)
            def _():
                l_remote(way, b, remote_blocks + b).start()

    def forward(c):
        for way in range(2):
            @pl.when(c + blocks < sent[way])
            def _():
                l_remote(way, c, l_place(way, c)).wait_recv()
                l_remote(way, c + blocks, l_place(way, c)).start()

    tiles = kbs * n
    events = (n - 2) * blocks
    events_early = events * 5 // 8

    def row_tile(t, carry):
        kb = t // n
        j = lax.rem(t, n)

        @pl.when(t + 1 < tiles)
        def _():
            a_copy(t + 1).start()

        @pl.when(j == 0)
        def _():
            @pl.when(kb >= blocks)
            def _():
                u_remote(kb // blocks, lax.rem(kb, blocks)).wait_recv()

            owner = [upper_owner(kb, j) for j in range(SLOTS)]
            for j in range(SLOTS):
                real = uslots[kb, j, 0].astype(jnp.float32)
                imag = uslots[kb, j, 1].astype(jnp.float32)
                for i, value in enumerate((weights[1] * real + weights[0] * imag, weights[0] * real - weights[1] * imag)):
                    turned = jnp.transpose(value)
                    for s in range(supers):
                        span = slice(s * width, (s + 1) * width)
                        lanes = slice(i * unit, (i + 1) * unit)
                        kept = jnp.where(owner[j] == s, turned, 0.0)
                        high = kept.astype(jnp.bfloat16)
                        low = (kept - high.astype(jnp.float32)).astype(jnp.bfloat16)
                        down = slice(wide + s * width, wide + (s + 1) * width)
                        if j == 0:
                            lhs[span, lanes] = high
                            lhs[down, lanes] = low
                        else:
                            lhs[span, lanes] = jnp.where(owner[j] == s, high, lhs[span, lanes])
                            lhs[down, lanes] = jnp.where(owner[j] == s, low, lhs[down, lanes])

        a_copy(t).wait()
        slot = lax.rem(t, 2)
        for q in range(2):
            right = abuf[slot, :, :, q * half:(q + 1) * half].reshape(2 * unit, half)
            total = jnp.dot(lhs[...], right, preferred_element_type=jnp.float32)
            before = acc[2 * j + q]
            acc[2 * j + q] = total[:wide] + total[wide:] + jnp.where(kb == 0, jnp.zeros_like(before), before)

        def some(c, carry):
            forward(c)
            return carry

        lax.fori_loop(t * events_early // tiles, (t + 1) * events_early // tiles, some, 0)
        return carry

    lax.fori_loop(0, tiles, row_tile, 0)

    def p_remote(ch):
        return pltpu.make_async_remote_copy(
            src_ref=acc.at[2 * ch + 1 - p], dst_ref=place_of(ch), send_sem=p_send.at[ch], recv_sem=p_recv.at[ch],
            device_id={"pole": 1 - p}, device_id_type=MESH,
        )

    def p_start(i, carry):
        p_remote(i).start()
        return carry

    lax.fori_loop(0, n, p_start, 0)

    steps = n * blocks

    def block_of(q):
        r = q - blocks
        few = jnp.minimum(taken[0], taken[1])
        up = jnp.where(r < 2 * few, lax.rem(r, 2), jnp.where(taken[0] > taken[1], 0, 1))
        c = jnp.where(r < 2 * few, r // 2, r - few)
        c = jnp.maximum(c, 0)
        place = jnp.where(q < blocks, remote_blocks + q, jnp.where(up == 0, c, remote_blocks - 1 - c))
        device = jnp.where(up == 0, z + 1 + c // blocks, z - 1 - c // blocks)
        column = jnp.where(q < blocks, z * blocks + q, device * blocks + lax.rem(c, blocks))
        return place, column, up, c

    def c_copy(v):
        q = v // 2
        _, column, _, _ = block_of(q)
        return pltpu.make_async_copy(
            inverse.at[:, pl.ds(pl.multiple_of(lax.rem(v, 2) * (rows // 2), rows // 2), rows // 2), pl.ds(pl.multiple_of(column * unit, unit), unit)],
            cbuf.at[lax.rem(v, 2)],
            c_sem.at[lax.rem(v, 2)],
        )

    c_copy(0).start()

    def p_add(ch, carry):
        p_remote(ch).wait_recv()
        acc[2 * ch + p] = acc[2 * ch + p] + place_of(ch)[...]
        return carry

    lax.fori_loop(0, n, p_add, 0)

    def q_remote(way, i):
        to = {"row": z + 1 if way == 0 else z - 1}
        return (
            pltpu.make_async_remote_copy(
                src_ref=qstage.at[way, i], dst_ref=qrecv.at[way, i], send_sem=q_send.at[way, i], recv_sem=q_recv.at[way, i],
                device_id=to, device_id_type=MESH,
            ),
            pltpu.make_async_remote_copy(
                src_ref=mstage.at[way, i], dst_ref=mrecv.at[way, i], send_sem=m_send.at[way, i], recv_sem=m_recv.at[way, i],
                device_id=to, device_id_type=MESH,
            ),
        )

    def arrived(way, i):
        for copy in q_remote(way, i):
            copy.wait_recv()
        return unpacked(qrecv[way, i], mrecv[way, i, :1])

    def wave(w):
        for way in range(2):
            i = w - z if way == 0 else w - (n - 1 - z)
            ch = n - 1 - i if way == 0 else i

            @pl.when(jnp.logical_and(i >= 0, z < ch if way == 0 else z > ch))
            def _():
                @pl.when(z > 0 if way == 0 else z < n - 1)
                def _():
                    acc[2 * ch + p] = acc[2 * ch + p] + arrived(way, i)

                code, scale = packed(acc[2 * ch + p])
                qstage[way, i] = code
                mstage[way, i] = jnp.broadcast_to(scale, mstage.shape[2:])
                for copy in q_remote(way, i):
                    copy.start()

    gap = max(1, steps // (n - 1))

    def column_step(q, carry):
        w = q // gap

        @pl.when(jnp.logical_and(lax.rem(q, gap) == 0, w < n - 1))
        def _():
            wave(w)

        e = events_early + q // 2

        @pl.when(jnp.logical_and(lax.rem(q, 2) == 0, e < events))
        def _():
            forward(e)

        place, column, up, c = block_of(q)
        for way in range(2):
            @pl.when(jnp.logical_and(jnp.logical_and(q >= blocks, up == way), c + blocks >= sent[way]))
            def _():
                l_remote(way, c, remote_blocks).wait_recv()

        owner = [lower_owner(column, j) for j in range(SLOTS)]
        for s in range(supers):
            real = jnp.zeros((unit, width), jnp.bfloat16)
            imag = jnp.zeros((unit, width), jnp.bfloat16)
            for j in range(SLOTS):
                real = jnp.where(owner[j] == s, lin[place * SLOTS + j, 0], real)
                imag = jnp.where(owner[j] == s, lin[place * SLOTS + j, 1], imag)
            put_pair(rhs, s, real, imag)

        for h in range(2):
            v = 2 * q + h

            @pl.when(v + 1 < 2 * steps)
            def _():
                c_copy(v + 1).start()

            c_copy(v).wait()
            left = jnp.concatenate([cbuf[h, 0], cbuf[h, 1]], axis=1)
            span = slice(h * (rows // 2), (h + 1) * (rows // 2))
            for s in range(supers):
                total = jnp.dot(left, get_pair(rhs, s, width), preferred_element_type=jnp.float32)
                before = cacc[s, span]
                cacc[s, span] = total + jnp.where(q == 0, jnp.zeros_like(before), before)
        return carry

    lax.fori_loop(0, steps, column_step, 0)

    gcopy = pltpu.make_async_copy(given, given_here, o_sem.at[0])
    gcopy.start()
    row_out[...] = -acc[2 * z + p]

    @pl.when(z > 0)
    def _():
        row_out[...] = row_out[...] - arrived(0, n - 1 - z)

    @pl.when(z < n - 1)
    def _():
        row_out[...] = row_out[...] - arrived(1, z)

    part = mine.shape[1]

    def writes(s, c):
        lanes = pl.ds(s * width, width)
        return (
            pltpu.make_async_copy(cacc.at[s, pl.ds(pl.multiple_of((2 * c + p) * part, part), part), pl.ds(0, width)], mine.at[c, :, lanes], w_sem.at[0, s, c]),
            pltpu.make_async_copy(cacc.at[s, pl.ds(pl.multiple_of((2 * c + 1 - p) * part, part), part), pl.ds(0, width)], other.at[c, :, lanes], w_sem.at[1, s, c]),
        )

    gcopy.wait()
    origin_flag = jnp.where(jnp.logical_and(z == 0, x == 0), 1.0, 0.0)
    for s in range(supers):
        def mix(i, carry):
            span = pl.ds(pl.multiple_of(i * 2 * part, 2 * part), 2 * part)
            real = cacc[s, span, :width]
            imag = cacc[s, span, width:]
            cacc[s, span, :width] = weights[0] * imag + weights[1] * real
            cacc[s, span, width:] = weights[0] * real - weights[1] * imag
            return carry

        lax.fori_loop(0, n_col, mix, 0)
        for c in range(n_col):
            for copy in writes(s, c):
                copy.start()
        diag[s * width:(s + 1) * width, :] = origin_flag * (
            weights[0] * given_here[s, 1].astype(jnp.float32) + weights[1] * given_here[s, 0].astype(jnp.float32)
        )

    def one(kb, carry):
        start = pl.multiple_of((lax.rem(x - kb // blocks + n_col, n_col) * blocks + lax.rem(kb, blocks)) * unit, unit)
        owner = [upper_owner(kb, j) for j in range(SLOTS)]
        for s in range(supers):
            rights = []
            lefts = []
            for c in range(2):
                value = cacc[s, pl.ds(start, unit), c * width:(c + 1) * width]
                high = value.astype(jnp.bfloat16)
                low = (value - high.astype(jnp.float32)).astype(jnp.bfloat16)
                rights.append(jnp.concatenate([high, low], axis=1))
                chosen = jnp.zeros((unit, width), jnp.bfloat16)
                for j in range(SLOTS):
                    chosen = jnp.where(owner[j] == s, uslots[kb, j, c], chosen)
                lefts.append(jnp.transpose(chosen))
            total = jnp.dot(
                jnp.concatenate(lefts, axis=1), jnp.concatenate(rights, axis=0), preferred_element_type=jnp.float32
            )
            diag[s * width:(s + 1) * width, :] += total[:, :width] + total[:, width:]
        return carry

    lax.fori_loop(0, kbs, one, 0)

    for s in range(supers):
        for c in range(n_col):
            for copy in writes(s, c):
                copy.wait()

    def finish(i, carry):
        for way in range(2):
            ch = n - 1 - i if way == 0 else i

            @pl.when(z < ch if way == 0 else z > ch)
            def _():
                for copy in q_remote(way, i):
                    copy.wait_send()
        return carry

    lax.fori_loop(0, n - 1, finish, 0)

    def l_finish(c, carry):
        for way in range(2):
            @pl.when(c < sent[way])
            def _():
                l_remote(way, c, remote_blocks).wait_send()
        return carry

    lax.fori_loop(0, remote_blocks, l_finish, 0)

    def p_finish(ch, carry):
        p_remote(ch).wait_send()
        return carry

    lax.fori_loop(0, n, p_finish, 0)
    for d in range(1, n_col):
        for b in range(blocks):
            u_remote(d, b).wait_send()


def put_pair(rhs, s, real, imag):
    for i, value in enumerate((real, imag, -imag, real)):
        rhs[i // 2, s, i % 2] = value


def get_pair(rhs, s, width):
    return jnp.concatenate(
        [jnp.concatenate([rhs[i, s, 0], rhs[i, s, 1]], axis=1) for i in range(2)], axis=0
    )


def fused_call(order, weights, inverse, own_l, own_u, given, sizes):
    n, n_col, blocks = sizes
    _, rows, cols = inverse.shape
    per, _, unit, width = own_l.shape
    supers = per // blocks
    wide = supers * width
    kbs = blocks * n_col
    half = cols // n // 2
    part = rows // (2 * n_col)
    dma = pltpu.SemaphoreType.DMA
    shared = unit == width and half == 2 * width and n <= supers * (rows // wide)
    scratch = [
        pltpu.VMEM((2 * n, wide, half), jnp.float32),
        pltpu.VMEM((supers, rows, 2 * width), jnp.float32),
        pltpu.VMEM((2 * wide, 2 * unit), jnp.bfloat16),
        pltpu.VMEM((2, supers, 2, unit, width), jnp.bfloat16),
        pltpu.VMEM((2, 2, unit, 2 * half), jnp.bfloat16),
        pltpu.VMEM((2, 2, rows // 2, unit), jnp.bfloat16),
        pltpu.VMEM((kbs, SLOTS, 2, unit, width), jnp.bfloat16),
        pltpu.VMEM((n * blocks * SLOTS, 2, unit, width), jnp.bfloat16),
        pltpu.VMEM((2, n - 1, wide, half), jnp.int16),
        pltpu.VMEM((2, n - 1, wide, half), jnp.int16),
        pltpu.VMEM((2, n - 1, 8, half), jnp.float32),
        pltpu.VMEM((2, n - 1, 8, half), jnp.float32),
        dma((2,)), dma((2,)), dma((kbs,)), dma((kbs,)), dma((2,)),
        dma((2, n * blocks)), dma((n * blocks,)),
        dma((n,)), dma((n,)),
        dma((2, n - 1)), dma((2, n - 1)), dma((2, n - 1)), dma((2, n - 1)),
        dma((2, supers, n_col)),
    ]
    if not shared:
        scratch.append(pltpu.VMEM((n, wide, half), jnp.float32))
        scratch.append(pltpu.VMEM(given.shape, jnp.bfloat16))
    smem = pl.BlockSpec(memory_space=pltpu.SMEM)
    vmem = pl.BlockSpec(memory_space=pltpu.VMEM)
    hbm = pl.BlockSpec(memory_space=pl.ANY)
    return pl.pallas_call(
        functools.partial(fused_kernel, (n, n_col, supers)),
        out_shape=(
            jax.ShapeDtypeStruct((wide, half), jnp.float32),
            jax.ShapeDtypeStruct((n_col, part, wide), jnp.float32),
            jax.ShapeDtypeStruct((n_col, part, wide), jnp.float32),
            jax.ShapeDtypeStruct((wide, width), jnp.float32),
        ),
        in_specs=[smem, smem, hbm, hbm, hbm, hbm],
        out_specs=(vmem, hbm, hbm, vmem),
        scratch_shapes=scratch,
        compiler_params=pltpu.CompilerParams(collective_id=3, has_side_effects=True, vmem_limit_bytes=63 * 2**20),
        name="fused",
    )(order, weights, inverse, own_l, own_u, given)


def body(inverse, lower, upper, diag_inverse, weights, pattern):
    n = lax.axis_size("row")
    n_col = lax.axis_size("col")
    n_groups = lax.axis_size("groups")
    _, local, _, supers, width = lower.shape
    inverse = inverse[0]
    unit = min(width, local)
    blocks = local // unit
    weights = weights[0]
    given = diag_inverse[0]
    order, over = scan_call(pattern, n * n_col * local // width, n_groups)

    def cut(factor):
        return jnp.transpose(factor[0].reshape(blocks, unit, 2, supers, width), (3, 0, 2, 1, 4))

    own_l = cut(lower)
    own_u = cut(upper)

    flat_l = own_l.reshape(supers * blocks, 2, unit, width)
    flat_u = own_u.reshape(supers * blocks, 2, unit, width)

    def usual():
        return fused_call(order, weights, inverse, flat_l, flat_u, given, (n, n_col, blocks))

    def rare():
        order, full = plan_call(pattern, (n, n_col), unit, width, blocks)
        lall, uall, row = stream_call(order, weights, inverse, flat_l, own_u, (n, n_col))
        return (row,) + tuple(column_call(full, weights, inverse, lall, uall, given, (n_col, supers, blocks)))

    row, mine, other, diag = lax.cond(over[0] <= 0, usual, rare)
    column, diagonal = close_call(mine, other, diag, n, n_col)
    row_density = jnp.transpose(row).reshape(-1, supers, width)
    return (column.reshape(-1, supers, width), row_density, diagonal.reshape(supers, width, width))


def solution(mesh):
    return jax.shard_map(
        body,
        mesh=mesh,
        in_specs=(
            P(("groups", "pole"), None, "row", "col"),
            P(("groups", "pole"), ("col", "row"), None, None, None),
            P(("groups", "pole"), ("row", "col"), None, None, None),
            P(("groups", "pole"), None, None, None, None),
            P(("groups", "pole"), None),
            P("groups", None),
        ),
        out_specs=(
            P(("groups", "row", "col", "pole"), None, None),
            P(("groups", "col", "row", "pole"), None, None),
            P("groups", None, None),
        ),
        check_vma=False,
    )
```

```python
import functools
import math

import jax
import jax.numpy as jnp
from jax import lax
from jax.experimental import pallas as pl
from jax.experimental.pallas import tpu as pltpu
from jax.sharding import PartitionSpec as P

MESH = pl.DeviceIdType.MESH
RING = 6
SLOTS = 2
TOP = 32767.0


def full_caps(n, per):
    return [per * d for d in range(n)]


def room(caps):
    n = len(caps)
    return max(caps[z] + caps[n - 1 - z] for z in range(n)) + 1


def stepped(caps, count):
    total = jnp.int32(0)
    for d in range(1, len(caps)):
        total = total + jnp.where(count >= d, caps[d] - caps[d - 1], 0)
    return total


class Streams:
    def __init__(self, caps, first, n, order, lown, lin, stage, send_sem, recv_sem, out_sem, lall):
        self.caps, self.first, self.n = caps, first, n
        self.order, self.lown, self.lin, self.stage = order, lown, lin, stage
        self.send_sem, self.recv_sem, self.out_sem, self.lall = send_sem, recv_sem, out_sem, lall
        self.per = lown.shape[0]
        self.size = lin.shape[0]
        self.z = lax.axis_index("row")
        z = self.z
        self.sent = (jnp.where(z > 0, stepped(caps, n - z), 0), jnp.where(z < n - 1, stepped(caps, z + 1), 0))
        self.taken = (stepped(caps, n - 1 - z), stepped(caps, z))
        self.events = max(caps) - first

    def place(self, way, c):
        return c if way == 0 else self.size - 1 - c

    def remote(self, way, c):
        slot = lax.rem(c, RING)
        place = self.place(way, c)
        return pltpu.make_async_remote_copy(
            src_ref=self.stage.at[way, slot],
            dst_ref=self.lin.at[place],
            send_sem=self.send_sem.at[way, slot],
            recv_sem=self.recv_sem.at[place],
            device_id={"row": self.z - 1 if way == 0 else self.z + 1},
            device_id_type=MESH,
        )

    def kept(self, way, c):
        place = self.place(way, c)
        return pltpu.make_async_copy(self.lin.at[place], self.lall.at[self.per + place], self.out_sem.at[place])

    def begin(self):
        for way in range(2):
            @pl.when(self.sent[way] > 0)
            def _():
                for c in range(self.first):
                    if c >= RING:
                        self.remote(way, c - RING).wait_send()
                    self.stage[way, c % RING] = self.lown[self.order[c]]
                    self.remote(way, c).start()

    def forward(self, d):
        c = d + self.first
        for way in range(2):
            @pl.when(c < self.sent[way])
            def _():
                @pl.when(d < self.taken[way])
                def _():
                    self.remote(way, d).wait_recv()
                    self.kept(way, d).start()

                @pl.when(c >= RING)
                def _():
                    self.remote(way, c - RING).wait_send()

                count = self.order[self.per + way]
                mine = self.lown[self.order[jnp.clip(c - count, 0, self.per - 1)]]
                arrived = self.lin[self.place(way, jnp.clip(d, 0, jnp.maximum(self.taken[way] - 1, 0)))]
                self.stage[way, lax.rem(c, RING)] = jnp.where(d < count, arrived, mine)
                self.remote(way, c).start()

    def drain(self):
        def step(c, carry):
            for way in range(2):
                @pl.when(jnp.logical_and(c < self.taken[way], c + self.first >= self.sent[way]))
                def _():
                    self.remote(way, c).wait_recv()
                    self.kept(way, c).start()

                @pl.when(jnp.logical_and(c < self.sent[way], c + RING >= self.sent[way]))
                def _():
                    self.remote(way, c).wait_send()
            return carry

        lax.fori_loop(0, max(self.caps), step, 0)

        def last(c, carry):
            for way in range(2):
                @pl.when(c < self.taken[way])
                def _():
                    self.kept(way, c).wait()
            return carry

        lax.fori_loop(0, max(self.caps), last, 0)


def greet(targets):
    barrier = pltpu.get_barrier_semaphore()
    total = jnp.int32(0)
    for axis, size, near in targets:
        me = lax.axis_index(axis)
        if near:
            for step in (-1, 1):
                there = jnp.logical_and(me + step >= 0, me + step < size)

                @pl.when(there)
                def _():
                    pl.semaphore_signal(barrier, inc=1, device_id={axis: me + step}, device_id_type=MESH)

                total = total + there.astype(jnp.int32)
        else:
            for d in range(1, size):
                pl.semaphore_signal(barrier, inc=1, device_id={axis: lax.rem(me + d, size)}, device_id_type=MESH)
            total = total + (size - 1)
    pl.semaphore_wait(barrier, total)


def packed(value):
    most = jnp.max(jnp.abs(value), axis=0, keepdims=True)
    factor = jnp.where(most > 0, TOP / jnp.maximum(most, 1e-30), 0.0)
    return jnp.round(value * factor).astype(jnp.int32).astype(jnp.int16), most * (1.0 / TOP)


def unpacked(code, scale):
    return code.astype(jnp.int32).astype(jnp.float32) * scale


def stream_kernel(cfg, order, weights, inverse, own_l, own_u, lall, uall, row_out, *scratch):
    (acc, lhs, abuf, ubuf, lown, lin, stage, prec, qstage, qrecv, mstage, mrecv,
     a_sem, u_send, u_recv, l_sem, s_send, s_recv, s_out, p_send, p_recv, q_send, q_recv, m_send, m_recv) = scratch
    n, n_col, caps = cfg
    per = lown.shape[0]
    supers, kbs, _, unit, width = ubuf.shape
    blocks = kbs // n_col
    half = acc.shape[2]
    tile = 2 * half
    z = lax.axis_index("row")
    x = lax.axis_index("col")
    p = lax.axis_index("pole")

    lcopy = pltpu.make_async_copy(own_l, lown, l_sem.at[0])
    lcopy.start()
    ucopy = pltpu.make_async_copy(own_u, ubuf.at[:, pl.ds(0, blocks)], l_sem.at[1])
    ucopy.start()

    def a_copy(t):
        kb = t // n
        origin = lax.rem(x - kb // blocks + n_col, n_col)
        row = (origin * blocks + lax.rem(kb, blocks)) * unit
        return pltpu.make_async_copy(
            inverse.at[:, pl.ds(pl.multiple_of(row, unit), unit), pl.ds(pl.multiple_of(lax.rem(t, n) * tile, tile), tile)],
            abuf.at[lax.rem(t, 3)],
            a_sem.at[lax.rem(t, 3)],
        )

    a_copy(0).start()
    a_copy(1).start()
    greet((("row", n, True), ("col", n_col, False), ("pole", 2, False)))

    def u_remote(d, b):
        return pltpu.make_async_remote_copy(
            src_ref=own_u.at[:, b],
            dst_ref=ubuf.at[:, d * blocks + b],
            send_sem=u_send.at[d * blocks + b],
            recv_sem=u_recv.at[d * blocks + b],
            device_id={"col": lax.rem(x + d, n_col)},
            device_id_type=MESH,
        )

    for b in range(blocks):
        for d in range(1, n_col):
            u_remote(d, b).start()

    lcopy.wait()
    streams = Streams(caps, blocks, n, order, lown, lin, stage, s_send, s_recv, s_out, lall)
    streams.begin()
    lout = pltpu.make_async_copy(lown, lall.at[pl.ds(0, per)], l_sem.at[0])
    lout.start()
    ucopy.wait()

    tiles = kbs * n
    early = blocks * n
    events = streams.events
    events_early = events * 5 // 18
    events_late = events - events_early
    late = tiles - early

    def due(t):
        if late == 0:
            return t * events // early
        return jnp.where(t < early, t * events_early // early, events_early + (t - early) * events_late // late)

    def row_tile(t, carry):
        kb = t // n
        j = lax.rem(t, n)

        @pl.when(j == 0)
        def _():
            @pl.when(kb >= blocks)
            def _():
                u_remote(kb // blocks, lax.rem(kb, blocks)).wait_recv()

            for s in range(supers):
                kept = order[per + 2 + kb * supers + s] > 0
                real = jnp.where(kept, ubuf[s, kb, 0].astype(jnp.float32), 0.0)
                imag = jnp.where(kept, ubuf[s, kb, 1].astype(jnp.float32), 0.0)
                span = slice(s * width, (s + 1) * width)
                for i, value in enumerate((weights[1] * real + weights[0] * imag, weights[0] * real - weights[1] * imag)):
                    turned = jnp.transpose(value)
                    high = turned.astype(jnp.bfloat16)
                    lhs[0, span, i * unit:(i + 1) * unit] = high
                    lhs[1, span, i * unit:(i + 1) * unit] = (turned - high.astype(jnp.float32)).astype(jnp.bfloat16)

        @pl.when(t + 2 < tiles)
        def _():
            a_copy(t + 2).start()

        a_copy(t).wait()
        slot = lax.rem(t, 3)
        for q in range(2):
            right = abuf[slot, :, :, q * half:(q + 1) * half].reshape(2 * unit, half)
            total = jnp.dot(lhs[0], right, preferred_element_type=jnp.float32) + jnp.dot(
                lhs[1], right, preferred_element_type=jnp.float32
            )
            before = acc[2 * j + q]
            acc[2 * j + q] = total + jnp.where(kb == 0, jnp.zeros_like(before), before)

        now = due(t)

        def some(d, carry):
            streams.forward(d)
            return carry

        lax.fori_loop(now, due(t + 1), some, 0)
        return carry

    lax.fori_loop(0, tiles, row_tile, 0)

    uout = pltpu.make_async_copy(ubuf, uall, l_sem.at[1])
    uout.start()

    def p_remote(ch):
        return pltpu.make_async_remote_copy(
            src_ref=acc.at[2 * ch + 1 - p],
            dst_ref=prec.at[ch],
            send_sem=p_send.at[ch],
            recv_sem=p_recv.at[ch],
            device_id={"pole": 1 - p},
            device_id_type=MESH,
        )

    for i in range((n + 1) // 2):
        p_remote(n - 1 - i).start()
        if i != n - 1 - i:
            p_remote(i).start()

    def q_remote(way, i):
        to = {"row": z + 1 if way == 0 else z - 1}
        return (
            pltpu.make_async_remote_copy(
                src_ref=qstage.at[way, i], dst_ref=qrecv.at[way, i], send_sem=q_send.at[way, i], recv_sem=q_recv.at[way, i],
                device_id=to, device_id_type=MESH,
            ),
            pltpu.make_async_remote_copy(
                src_ref=mstage.at[way, i], dst_ref=mrecv.at[way, i], send_sem=m_send.at[way, i], recv_sem=m_recv.at[way, i],
                device_id=to, device_id_type=MESH,
            ),
        )

    def arrived(way, i):
        for copy in q_remote(way, i):
            copy.wait_recv()
        return unpacked(qrecv[way, i], mrecv[way, i, :1])

    def row_step(i, carry):
        for way in range(2):
            ch = n - 1 - i if way == 0 else i

            @pl.when(z < ch if way == 0 else z > ch)
            def _():
                p_remote(ch).wait_recv()
                acc[2 * ch + p] = acc[2 * ch + p] + prec[ch]

                @pl.when(z > 0 if way == 0 else z < n - 1)
                def _():
                    acc[2 * ch + p] = acc[2 * ch + p] + arrived(way, i)

                code, scale = packed(acc[2 * ch + p])
                qstage[way, i] = code
                mstage[way, i] = jnp.broadcast_to(scale, mstage.shape[2:])
                for copy in q_remote(way, i):
                    copy.start()
        return carry

    lax.fori_loop(0, n - 1, row_step, 0)

    p_remote(z).wait_recv()
    row_out[...] = acc[2 * z + p] + prec[z]

    @pl.when(z > 0)
    def _():
        row_out[...] = row_out[...] + arrived(0, n - 1 - z)

    @pl.when(z < n - 1)
    def _():
        row_out[...] = row_out[...] + arrived(1, z)

    row_out[...] = -row_out[...]
    streams.drain()

    def finish(i, carry):
        for way in range(2):
            ch = n - 1 - i if way == 0 else i

            @pl.when(z < ch if way == 0 else z > ch)
            def _():
                for copy in q_remote(way, i):
                    copy.wait_send()
        return carry

    lax.fori_loop(0, n - 1, finish, 0)
    for ch in range(n):
        p_remote(ch).wait_send()
    for d in range(1, n_col):
        for b in range(blocks):
            u_remote(d, b).wait_send()
    lout.wait()
    uout.wait()


def stream_call(order, weights, inverse, own_l, own_u, sizes):
    n, n_col = sizes
    _, rows, cols = inverse.shape
    per, _, unit, width = own_l.shape
    supers, blocks = own_u.shape[:2]
    wide = supers * width
    caps = full_caps(n, per)
    kbs = blocks * n_col
    half = cols // n // 2
    space = room(caps)
    dma = pltpu.SemaphoreType.DMA
    scratch = [
        pltpu.VMEM((2 * n, wide, half), jnp.float32),
        pltpu.VMEM((2, wide, 2 * unit), jnp.bfloat16),
        pltpu.VMEM((3, 2, unit, 2 * half), jnp.bfloat16),
        pltpu.VMEM((supers, kbs, 2, unit, width), jnp.bfloat16),
        pltpu.VMEM((per, 2, unit, width), jnp.bfloat16),
        pltpu.VMEM((space, 2, unit, width), jnp.bfloat16),
        pltpu.VMEM((2, RING, 2, unit, width), jnp.bfloat16),
        pltpu.VMEM((n, wide, half), jnp.float32),
        pltpu.VMEM((2, n - 1, wide, half), jnp.int16),
        pltpu.VMEM((2, n - 1, wide, half), jnp.int16),
        pltpu.VMEM((2, n - 1, 8, half), jnp.float32),
        pltpu.VMEM((2, n - 1, 8, half), jnp.float32),
        dma((3,)), dma((kbs,)), dma((kbs,)), dma((2,)),
        dma((2, RING)), dma((space,)), dma((space,)),
        dma((n,)), dma((n,)),
        dma((2, n - 1)), dma((2, n - 1)), dma((2, n - 1)), dma((2, n - 1)),
    ]
    smem = pl.BlockSpec(memory_space=pltpu.SMEM)
    vmem = pl.BlockSpec(memory_space=pltpu.VMEM)
    hbm = pl.BlockSpec(memory_space=pl.ANY)
    return pl.pallas_call(
        functools.partial(stream_kernel, (n, n_col, caps)),
        out_shape=(
            jax.ShapeDtypeStruct((per + space, 2, unit, width), jnp.bfloat16),
            jax.ShapeDtypeStruct((supers, kbs, 2, unit, width), jnp.bfloat16),
            jax.ShapeDtypeStruct((wide, half), jnp.float32),
        ),
        in_specs=[smem, smem, hbm, hbm, hbm],
        out_specs=(hbm, hbm, vmem),
        scratch_shapes=scratch,
        compiler_params=pltpu.CompilerParams(collective_id=0, has_side_effects=True, vmem_limit_bytes=62 * 2**20),
        name="streams",
    )(order, weights, inverse, own_l, own_u)


def column_kernel(cfg, meta, weights, a_ref, *rest):
    supers, n_col, blocks = cfg
    l_refs = rest[:supers]
    u_ref, given, mine, other, diag, acc = rest[supers:]
    k = pl.program_id(0)
    steps = pl.num_programs(0)
    _, rows, double = acc.shape
    width = double // 2
    unit = a_ref.shape[2]
    base = 2 * supers * steps
    piece = rows

    @pl.when(k == 0)
    def _():
        acc[...] = jnp.zeros_like(acc)

    for s in range(supers):
        @pl.when(meta[k * supers + s] > 0)
        def _():
            real = l_refs[s][0, 0]
            imag = l_refs[s][0, 1]
            right = jnp.concatenate([jnp.concatenate([real, imag], axis=1), jnp.concatenate([-imag, real], axis=1)], axis=0)

            def part(i, carry):
                span = pl.ds(pl.multiple_of(i * piece, piece), piece)
                left = jnp.concatenate([a_ref[0, span], a_ref[1, span]], axis=1)
                acc[s, span] += jnp.dot(left, right, preferred_element_type=jnp.float32)
                return carry

            lax.fori_loop(0, rows // piece, part, 0)

    @pl.when(k == steps - 1)
    def _():
        part = mine.shape[1]
        pole = meta[base]
        for s in range(supers):
            lanes = slice(s * width, (s + 1) * width)
            for c in range(n_col):
                for q in range(2):
                    span = pl.ds((2 * c + q) * part, part)
                    real = acc[s, span, :width]
                    imag = acc[s, span, width:]
                    mixed = weights[0] * imag + weights[1] * real
                    acc[s, span, :width] = mixed
                    acc[s, span, width:] = weights[0] * real - weights[1] * imag

                    @pl.when(pole == q)
                    def _():
                        mine[c, :, lanes] = mixed

                    @pl.when(pole != q)
                    def _():
                        other[c, :, lanes] = mixed

            @pl.when(meta[base + 1] > 0)
            def _():
                diag[lanes, :] = weights[0] * given[s, 1].astype(jnp.float32) + weights[1] * given[s, 0].astype(jnp.float32)

            @pl.when(meta[base + 1] == 0)
            def _():
                diag[lanes, :] = jnp.zeros((width, diag.shape[1]), jnp.float32)

        def one(kb, carry):
            for s in range(supers):
                lanes = slice(s * width, (s + 1) * width)

                @pl.when(meta[base + 2 + n_col + kb * supers + s] > 0)
                def _():
                    start = pl.multiple_of(meta[base + 2 + kb // blocks] + lax.rem(kb, blocks) * unit, unit)
                    total = jnp.zeros((width, width), jnp.float32)
                    for c in range(2):
                        value = acc[s, pl.ds(start, unit), c * width:(c + 1) * width]
                        high = value.astype(jnp.bfloat16)
                        low = (value - high.astype(jnp.float32)).astype(jnp.bfloat16)
                        turned = jnp.transpose(u_ref[s, kb, c])
                        total += jnp.dot(turned, high, preferred_element_type=jnp.float32) + jnp.dot(
                            turned, low, preferred_element_type=jnp.float32
                        )
                    diag[lanes, :] += total
            return carry

        lax.fori_loop(0, u_ref.shape[1], one, 0)


def column_call(meta, weights, inverse, lall, uall, given, sizes):
    n_col, supers, blocks = sizes
    _, rows, cols = inverse.shape
    _, _, unit, width = lall.shape
    steps = cols // unit
    part = rows // (2 * n_col)

    def slot(s):
        return lambda k, meta: (meta[supers * steps + k * supers + s], 0, 0, 0)

    whole = pl.BlockSpec(uall.shape, lambda k, meta: (0, 0, 0, 0, 0))
    out = pl.BlockSpec((n_col, part, supers * width), lambda k, meta: (0, 0, 0))
    return pl.pallas_call(
        functools.partial(column_kernel, (supers, n_col, blocks)),
        out_shape=(
            jax.ShapeDtypeStruct((n_col, part, supers * width), jnp.float32),
            jax.ShapeDtypeStruct((n_col, part, supers * width), jnp.float32),
            jax.ShapeDtypeStruct((supers * width, width), jnp.float32),
        ),
        grid_spec=pltpu.PrefetchScalarGridSpec(
            num_scalar_prefetch=1,
            grid=(steps,),
            in_specs=[
                pl.BlockSpec(memory_space=pltpu.SMEM),
                pl.BlockSpec((2, rows, unit), lambda k, meta: (0, 0, k)),
            ]
            + [pl.BlockSpec((1, 2, unit, width), slot(s)) for s in range(supers)]
            + [whole, pl.BlockSpec(given.shape, lambda k, meta: (0, 0, 0, 0))],
            out_specs=(out, out, pl.BlockSpec((supers * width, width), lambda k, meta: (0, 0))),
            scratch_shapes=[pltpu.VMEM((supers, rows, 2 * width), jnp.float32)],
        ),
        compiler_params=pltpu.CompilerParams(vmem_limit_bytes=60 * 2**20),
        name="columns",
    )(meta, weights, inverse, *([lall] * supers), uall, given)


def close_kernel(cfg, mine, other, diag, column, total, *scratch):
    (here, prec, kept, qstage, qrecv, mstage, mrecv, dpole, dvalue, xcode, xscale, zcode, zscale, zin, zinscale, gcode, gscale,
     h_sem, p_send, p_recv, q_send, q_recv, m_send, m_recv, dp_send, dp_recv, x_send, x_recv, xs_send, xs_recv,
     z_send, z_recv, zs_send, zs_recv, g_send, g_recv, gs_send, gs_recv, gp_send, gp_recv) = scratch
    n, n_col = cfg
    z = lax.axis_index("row")
    x = lax.axis_index("col")
    p = lax.axis_index("pole")
    high = diag.shape[0] // 2
    slab = high // n
    supers, _, width = column.shape

    def remote(src, dst, send, recv, to):
        return pltpu.make_async_remote_copy(
            src_ref=src, dst_ref=dst, send_sem=send, recv_sem=recv, device_id=to, device_id_type=MESH
        )

    def p_remote(d):
        return remote(other.at[lax.rem(x + d, n_col)], prec.at[d], p_send.at[d], p_recv.at[d], {"pole": 1 - p})

    def h_copy(d):
        return pltpu.make_async_copy(mine.at[lax.rem(x + d, n_col)], here.at[d], h_sem.at[d])

    def dp_remote():
        return remote(diag.at[pl.ds(pl.multiple_of((1 - p) * high, 8), high)], dpole, dp_send.at[0], dp_recv.at[0], {"pole": 1 - p})

    def x_remote(d):
        to = {"col": lax.rem(x + d, n_col)}
        return (
            remote(xcode.at[0], xcode.at[d], x_send.at[d], x_recv.at[d], to),
            remote(xscale.at[0], xscale.at[d], xs_send.at[d], xs_recv.at[d], to),
        )

    def q_remote(d):
        to = {"col": lax.rem(x + d, n_col)}
        return (
            remote(qstage.at[d], qrecv.at[d], q_send.at[d], q_recv.at[d], to),
            remote(mstage.at[d], mrecv.at[d], m_send.at[d], m_recv.at[d], to),
        )

    def z_remote(d):
        to = {"row": lax.rem(z + d, n)}
        return (
            remote(zcode.at[d], zin.at[d], z_send.at[d], z_recv.at[d], to),
            remote(zscale.at[d], zinscale.at[d], zs_send.at[d], zs_recv.at[d], to),
        )

    def g_remote(d):
        to = {"row": lax.rem(z + d, n)}
        return (
            remote(gcode.at[0], gcode.at[d], g_send.at[d], g_recv.at[d], to),
            remote(gscale.at[0], gscale.at[d], gs_send.at[d], gs_recv.at[d], to),
        )

    def rows_of(place):
        return pl.ds(pl.multiple_of(p * high + place * slab, 8), slab)

    def gp_remote():
        span = pl.ds(pl.multiple_of(p * high, 8), high)
        return remote(total.at[span], total.at[span], gp_send.at[0], gp_recv.at[0], {"pole": 1 - p})

    def put(code_ref, scale_ref, d, value):
        code, scale = packed(value)
        code_ref[d] = code
        scale_ref[d] = jnp.broadcast_to(scale, scale_ref.shape[1:])

    def get(code_ref, scale_ref, d):
        return unpacked(code_ref[d], scale_ref[d, :1])

    for d in range(n_col):
        h_copy(d).start()
    greet((("row", n, False), ("col", n_col, False), ("pole", 2, False)))
    dp_remote().start()
    for d in range(1, n_col):
        p_remote(d).start()
    p_remote(0).start()

    dp_remote().wait_recv()
    put(xcode, xscale, 0, diag[pl.ds(pl.multiple_of(p * high, 8), high)] + dpole[...])
    for d in range(1, n_col):
        for copy in x_remote(d):
            copy.start()

    for d in range(1, n_col):
        p_remote(d).wait_recv()
        h_copy(d).wait()
        put(qstage, mstage, d, here[d] + prec[d])
        for copy in q_remote(d):
            copy.start()

    for d in range(1, n_col):
        for copy in x_remote(d):
            copy.wait_recv()
    value = jnp.zeros((high, width), jnp.float32)
    for origin in range(n_col):
        d = lax.rem(x - origin + n_col, n_col)
        value = value + get(xcode, xscale, d)
    dvalue[...] = value
    for d in range(1, n):
        to = lax.rem(z + d, n)
        put(zcode, zscale, d, dvalue[pl.ds(pl.multiple_of(to * slab, 8), slab)])
        for copy in z_remote(d):
            copy.start()
    p_remote(0).wait_recv()
    h_copy(0).wait()
    kept[...] = here[0] + prec[0]
    value = dvalue[pl.ds(pl.multiple_of(z * slab, 8), slab)]
    for d in range(1, n):
        for copy in z_remote(d):
            copy.wait_recv()
        value = value + get(zin, zinscale, d)
    put(gcode, gscale, 0, value)
    for d in range(1, n):
        for copy in g_remote(d):
            copy.start()
    total[rows_of(z)] = get(gcode, gscale, 0)
    for d in range(1, n):
        for copy in g_remote(d):
            copy.wait_recv()
        total[rows_of(lax.rem(z - d + n, n))] = get(gcode, gscale, d)
    gp_remote().start()

    for d in range(1, n_col):
        for copy in q_remote(d):
            copy.wait_recv()
        kept[...] = kept[...] + get(qrecv, mrecv, d)
    for s in range(supers):
        column[s] = -kept[:, s * width:(s + 1) * width]

    gp_remote().wait_send()
    span = pl.ds(pl.multiple_of((1 - p) * high, 8), high)
    remote(total.at[span], total.at[span], gp_send.at[0], gp_recv.at[0], {"pole": 1 - p}).wait_recv()
    dp_remote().wait_send()
    for d in range(n_col):
        p_remote(d).wait_send()
    for d in range(1, n):
        for copy in z_remote(d) + g_remote(d):
            copy.wait_send()
    for d in range(1, n_col):
        for copy in x_remote(d) + q_remote(d):
            copy.wait_send()


def close_call(mine, other, diag, n, n_col):
    _, part, wide = mine.shape
    tall, width = diag.shape
    supers = wide // width
    high = tall // 2
    slab = high // n
    dma = pltpu.SemaphoreType.DMA
    vmem = pl.BlockSpec(memory_space=pltpu.VMEM)
    hbm = pl.BlockSpec(memory_space=pl.ANY)
    return pl.pallas_call(
        functools.partial(close_kernel, (n, n_col)),
        out_shape=(
            jax.ShapeDtypeStruct((supers, part, width), jnp.float32),
            jax.ShapeDtypeStruct((tall, width), jnp.float32),
        ),
        in_specs=[hbm, hbm, vmem],
        out_specs=(vmem, vmem),
        scratch_shapes=[
            pltpu.VMEM((n_col, part, wide), jnp.float32),
            pltpu.VMEM((n_col, part, wide), jnp.float32),
            pltpu.VMEM((part, wide), jnp.float32),
            pltpu.VMEM((n_col, part, wide), jnp.int16),
            pltpu.VMEM((n_col, part, wide), jnp.int16),
            pltpu.VMEM((n_col, 8, wide), jnp.float32),
            pltpu.VMEM((n_col, 8, wide), jnp.float32),
            pltpu.VMEM((high, width), jnp.float32),
            pltpu.VMEM((high, width), jnp.float32),
            pltpu.VMEM((n_col, high, width), jnp.int16),
            pltpu.VMEM((n_col, 8, width), jnp.float32),
            pltpu.VMEM((n, slab, width), jnp.int16),
            pltpu.VMEM((n, 8, width), jnp.float32),
            pltpu.VMEM((n, slab, width), jnp.int16),
            pltpu.VMEM((n, 8, width), jnp.float32),
            pltpu.VMEM((n, slab, width), jnp.int16),
            pltpu.VMEM((n, 8, width), jnp.float32),
            dma((n_col,)), dma((n_col,)), dma((n_col,)), dma((n_col,)), dma((n_col,)), dma((n_col,)), dma((n_col,)),
            dma((1,)), dma((1,)), dma((n_col,)), dma((n_col,)), dma((n_col,)), dma((n_col,)),
            dma((n,)), dma((n,)), dma((n,)), dma((n,)), dma((n,)), dma((n,)), dma((n,)), dma((n,)), dma((1,)), dma((1,)),
        ],
        compiler_params=pltpu.CompilerParams(collective_id=2, has_side_effects=True, vmem_limit_bytes=40 * 2**20),
        name="close",
    )(mine, other, diag)


def plan_kernel(cfg, pattern, order, full, keep, count):
    n, n_col, blocks, unit, width = cfg
    supers, entries = pattern.shape
    z = lax.axis_index("row")
    x = lax.axis_index("col")
    p = lax.axis_index("pole")
    per = supers * blocks
    units = n * n_col * blocks
    steps = n * blocks
    split = width // unit

    def clear(i, carry):
        keep[i] = 0
        return carry

    lax.fori_loop(0, supers * units, clear, 0)

    def mark(i, carry):
        s = i // entries
        at = s * units + pattern[s, lax.rem(i, entries)] * split
        for r in range(split):
            keep[at + r] = 1
        return carry

    lax.fori_loop(0, supers * entries, mark, 0)

    def number(i, carry):
        total = jnp.int32(0)
        for s in range(supers):
            for b in range(blocks):
                total = total + keep[s * units + i * blocks + b]
        count[i] = total
        return carry

    lax.fori_loop(0, n * n_col, number, 0)

    def pack(r, rank):
        s = r // blocks
        k = keep[s * units + (x * n + z) * blocks + lax.rem(r, blocks)]
        order[r] = 0

        @pl.when(k > 0)
        def _():
            order[rank] = r

        return rank + k

    lax.fori_loop(0, per, pack, jnp.int32(0))

    def around(i, sums):
        k = count[x * n + i]
        return sums[0] + jnp.where(i > z, k, 0), sums[1] + jnp.where(i < z, k, 0)

    above, below = lax.fori_loop(0, n, around, (jnp.int32(0), jnp.int32(0)))
    order[per] = above
    order[per + 1] = below

    base = 2 * supers * steps
    full[base] = p
    full[base + 1] = jnp.logical_and(z == 0, x == 0).astype(jnp.int32)
    for d in range(n_col):
        full[base + 2 + d] = lax.rem(x - d + n_col, n_col) * blocks * unit

    def rows(i, carry):
        kb = i // supers
        origin = lax.rem(x - kb // blocks + n_col, n_col)
        k = keep[lax.rem(i, supers) * units + (z * n_col + origin) * blocks + lax.rem(kb, blocks)]
        order[per + 2 + i] = k
        full[base + 2 + n_col + i] = k
        return carry

    lax.fori_loop(0, n_col * blocks * supers, rows, 0)

    def device(at, before):
        here = count[x * n + at]
        after = jnp.int32(0)
        for i in range(n):
            after = after + jnp.where(i > at, count[x * n + i], 0)

        def pair(r, rank):
            s = r // blocks
            b = lax.rem(r, blocks)
            k = keep[s * units + (x * n + at) * blocks + b]
            down = blocks * (at - z - 1) + rank + jnp.where(rank < blocks, 0, after)
            up = blocks * (z - 1 - at) + rank + jnp.where(rank < blocks, 0, before)
            to = (at * blocks + b) * supers + s
            place = jnp.where(at == z, r, jnp.where(at > z, per + down, per + room(full_caps(n, per)) - 1 - up))
            full[to] = k
            full[supers * steps + to] = jnp.where(k > 0, place, 0)
            return rank + k

        lax.fori_loop(0, per, pair, jnp.int32(0))
        return before + here

    lax.fori_loop(0, n, device, jnp.int32(0))


def plan_call(pattern, sizes, unit, width, blocks):
    n, n_col = sizes
    supers, _ = pattern.shape
    per = supers * blocks
    table = 2 * supers * n * blocks + 2 + n_col + n_col * blocks * supers
    smem = pl.BlockSpec(memory_space=pltpu.SMEM)
    return pl.pallas_call(
        functools.partial(plan_kernel, (n, n_col, blocks, unit, width)),
        out_shape=(
            jax.ShapeDtypeStruct((per + 2 + n_col * blocks * supers,), jnp.int32),
            jax.ShapeDtypeStruct((table,), jnp.int32),
        ),
        in_specs=[smem],
        out_specs=(smem, smem),
        scratch_shapes=[pltpu.SMEM((supers * n * n_col * blocks,), jnp.int32), pltpu.SMEM((n * n_col,), jnp.int32)],
        name="plan",
    )(pattern)


def scan_kernel(cfg, pattern, order, over, flags, send, recv):
    n_groups, = cfg
    supers, entries = pattern.shape
    g = lax.axis_index("groups")
    lane = lax.broadcasted_iota(jnp.int32, order.shape, 1)
    row = lax.broadcasted_iota(jnp.int32, order.shape, 0)
    rank = jnp.zeros(order.shape, jnp.int32)
    table = jnp.full(order.shape, -1, jnp.int32)
    for s in range(supers):
        hit = jnp.zeros(order.shape, jnp.int32)
        for j in range(entries):
            hit = jnp.where(lane == pattern[s, j], 1, hit)
        table = jnp.where(jnp.where(row == rank, hit, 0) > 0, s, table)
        rank = rank + hit
    order[...] = table
    bad = jnp.max(jnp.where(rank > SLOTS, 1.0, 0.0))
    flags[0] = jnp.full(flags.shape[1:], bad, jnp.float32)

    def copy(d):
        return pltpu.make_async_remote_copy(
            src_ref=flags.at[0], dst_ref=flags.at[d], send_sem=send.at[d], recv_sem=recv.at[d],
            device_id={"groups": lax.rem(g + d, n_groups)}, device_id_type=MESH,
        )

    greet((("groups", n_groups, False),))
    for d in range(1, n_groups):
        copy(d).start()
    for d in range(1, n_groups):
        copy(d).wait_send()
        copy(d).wait_recv()
    over[0] = jnp.max(flags[...])


def scan_call(pattern, owners, n_groups):
    smem = pl.BlockSpec(memory_space=pltpu.SMEM)
    dma = pltpu.SemaphoreType.DMA
    return pl.pallas_call(
        functools.partial(scan_kernel, (n_groups,)),
        out_shape=(
            jax.ShapeDtypeStruct((8, -(-owners // 128) * 128), jnp.int32),
            jax.ShapeDtypeStruct((1,), jnp.float32),
        ),
        in_specs=[smem],
        out_specs=(pl.BlockSpec(memory_space=pltpu.VMEM), smem),
        scratch_shapes=[pltpu.VMEM((n_groups, 8, 128), jnp.float32), dma((n_groups,)), dma((n_groups,))],
        compiler_params=pltpu.CompilerParams(collective_id=1, has_side_effects=True),
        name="scan",
    )(pattern)


def fused_kernel(cfg, order, weights, inverse, own_l, own_u, given, row_out, mine, other, diag, *scratch):
    (acc, cacc, lhs, rhs, abuf, cbuf, uslots, lin, qstage, qrecv, mstage, mrecv,
     a_sem, c_sem, u_send, u_recv, o_sem, l_send, l_recv, p_send, p_recv, q_send, q_recv, m_send, m_recv, w_sem) = scratch[:26]
    n, n_col, supers = cfg
    z = lax.axis_index("row")
    x = lax.axis_index("col")
    p = lax.axis_index("pole")
    kbs, _, _, unit, width = uslots.shape
    blocks = kbs // n_col
    remote_blocks = (n - 1) * blocks
    half = acc.shape[2]
    tile = 2 * half
    rows = cacc.shape[1]
    apart = len(scratch) > 26
    prec = scratch[26] if apart else cacc
    given_here = scratch[27] if apart else rhs.at[0]
    wide = supers * width

    def lower_owner(k, j):
        return order[j, (x * n * blocks + k) * unit // width]

    def upper_owner(kb, j):
        origin = lax.rem(x - kb // blocks + n_col, n_col)
        return order[j, ((z * n_col + origin) * blocks + lax.rem(kb, blocks)) * unit // width]

    def place_of(ch):
        if not apart:
            fit = rows // wide
            return cacc.at[ch // fit, pl.ds(pl.multiple_of(lax.rem(ch, fit) * wide, wide), wide)]
        return prec.at[ch]

    def a_copy(t):
        kb = t // n
        origin = lax.rem(x - kb // blocks + n_col, n_col)
        row = (origin * blocks + lax.rem(kb, blocks)) * unit
        return pltpu.make_async_copy(
            inverse.at[:, pl.ds(pl.multiple_of(row, unit), unit), pl.ds(pl.multiple_of(lax.rem(t, n) * tile, tile), tile)],
            abuf.at[lax.rem(t, 2)],
            a_sem.at[lax.rem(t, 2)],
        )

    per = supers * blocks
    own = [
        pltpu.make_async_copy(source.at[c], lin.at[pl.ds(i * per, per), c], o_sem.at[2 * i + c])
        for i, source in enumerate((own_l, own_u))
        for c in range(2)
    ]
    for copy in own:
        copy.start()
    a_copy(0).start()
    for copy in own:
        copy.wait()
    for b in range(blocks):
        for j in range(SLOTS):
            chosen = jnp.maximum(lower_owner(z * blocks + b, j), 0)
            lin[(remote_blocks + b) * SLOTS + j] = lin[chosen * blocks + b]
            chosen = jnp.maximum(upper_owner(b, j), 0)
            uslots[b, j] = lin[per + chosen * blocks + b]
    greet((("row", n, True), ("col", n_col, False), ("pole", 2, False)))

    def u_remote(d, b):
        return pltpu.make_async_remote_copy(
            src_ref=uslots.at[b], dst_ref=uslots.at[d * blocks + b],
            send_sem=u_send.at[d * blocks + b], recv_sem=u_recv.at[d * blocks + b],
            device_id={"col": lax.rem(x + d, n_col)}, device_id_type=MESH,
        )

    sent = (jnp.where(z > 0, (n - z) * blocks, 0), jnp.where(z < n - 1, (z + 1) * blocks, 0))
    taken = ((n - 1 - z) * blocks, z * blocks)

    def l_place(way, c):
        return c if way == 0 else remote_blocks - 1 - c

    def l_remote(way, c, source):
        return pltpu.make_async_remote_copy(
            src_ref=lin.at[pl.ds(source * SLOTS, SLOTS)], dst_ref=lin.at[pl.ds(l_place(way, c) * SLOTS, SLOTS)],
            send_sem=l_send.at[way, c], recv_sem=l_recv.at[l_place(way, c)],
            device_id={"row": z - 1 if way == 0 else z + 1}, device_id_type=MESH,
        )

    for b in range(blocks):
        for d in range(1, n_col):
            u_remote(d, b).start()
        for way in range(2):
            @pl.when(sent[way] > 0)
            def _():
                l_remote(way, b, remote_blocks + b).start()

    def forward(c):
        for way in range(2):
            @pl.when(c + blocks < sent[way])
            def _():
                l_remote(way, c, l_place(way, c)).wait_recv()
                l_remote(way, c + blocks, l_place(way, c)).start()

    tiles = kbs * n
    events = (n - 2) * blocks
    events_early = events * 5 // 8

    def row_tile(t, carry):
        kb = t // n
        j = lax.rem(t, n)

        @pl.when(t + 1 < tiles)
        def _():
            a_copy(t + 1).start()

        @pl.when(j == 0)
        def _():
            @pl.when(kb >= blocks)
            def _():
                u_remote(kb // blocks, lax.rem(kb, blocks)).wait_recv()

            owner = [upper_owner(kb, j) for j in range(SLOTS)]
            for j in range(SLOTS):
                real = uslots[kb, j, 0].astype(jnp.float32)
                imag = uslots[kb, j, 1].astype(jnp.float32)
                for i, value in enumerate((weights[1] * real + weights[0] * imag, weights[0] * real - weights[1] * imag)):
                    turned = jnp.transpose(value)
                    for s in range(supers):
                        span = slice(s * width, (s + 1) * width)
                        lanes = slice(i * unit, (i + 1) * unit)
                        kept = jnp.where(owner[j] == s, turned, 0.0)
                        high = kept.astype(jnp.bfloat16)
                        low = (kept - high.astype(jnp.float32)).astype(jnp.bfloat16)
                        down = slice(wide + s * width, wide + (s + 1) * width)
                        if j == 0:
                            lhs[span, lanes] = high
                            lhs[down, lanes] = low
                        else:
                            lhs[span, lanes] = jnp.where(owner[j] == s, high, lhs[span, lanes])
                            lhs[down, lanes] = jnp.where(owner[j] == s, low, lhs[down, lanes])

        a_copy(t).wait()
        slot = lax.rem(t, 2)
        for q in range(2):
            right = abuf[slot, :, :, q * half:(q + 1) * half].reshape(2 * unit, half)
            total = jnp.dot(lhs[...], right, preferred_element_type=jnp.float32)
            before = acc[2 * j + q]
            acc[2 * j + q] = total[:wide] + total[wide:] + jnp.where(kb == 0, jnp.zeros_like(before), before)

        def some(c, carry):
            forward(c)
            return carry

        lax.fori_loop(t * events_early // tiles, (t + 1) * events_early // tiles, some, 0)
        return carry

    lax.fori_loop(0, tiles, row_tile, 0)

    def p_remote(ch):
        return pltpu.make_async_remote_copy(
            src_ref=acc.at[2 * ch + 1 - p], dst_ref=place_of(ch), send_sem=p_send.at[ch], recv_sem=p_recv.at[ch],
            device_id={"pole": 1 - p}, device_id_type=MESH,
        )

    def p_start(i, carry):
        p_remote(i).start()
        return carry

    lax.fori_loop(0, n, p_start, 0)

    steps = n * blocks

    def block_of(q):
        r = q - blocks
        few = jnp.minimum(taken[0], taken[1])
        up = jnp.where(r < 2 * few, lax.rem(r, 2), jnp.where(taken[0] > taken[1], 0, 1))
        c = jnp.where(r < 2 * few, r // 2, r - few)
        c = jnp.maximum(c, 0)
        place = jnp.where(q < blocks, remote_blocks + q, jnp.where(up == 0, c, remote_blocks - 1 - c))
        device = jnp.where(up == 0, z + 1 + c // blocks, z - 1 - c // blocks)
        column = jnp.where(q < blocks, z * blocks + q, device * blocks + lax.rem(c, blocks))
        return place, column, up, c

    def c_copy(v):
        q = v // 2
        _, column, _, _ = block_of(q)
        return pltpu.make_async_copy(
            inverse.at[:, pl.ds(pl.multiple_of(lax.rem(v, 2) * (rows // 2), rows // 2), rows // 2), pl.ds(pl.multiple_of(column * unit, unit), unit)],
            cbuf.at[lax.rem(v, 2)],
            c_sem.at[lax.rem(v, 2)],
        )

    c_copy(0).start()

    def p_add(ch, carry):
        p_remote(ch).wait_recv()
        acc[2 * ch + p] = acc[2 * ch + p] + place_of(ch)[...]
        return carry

    lax.fori_loop(0, n, p_add, 0)

    def q_remote(way, i):
        to = {"row": z + 1 if way == 0 else z - 1}
        return (
            pltpu.make_async_remote_copy(
                src_ref=qstage.at[way, i], dst_ref=qrecv.at[way, i], send_sem=q_send.at[way, i], recv_sem=q_recv.at[way, i],
                device_id=to, device_id_type=MESH,
            ),
            pltpu.make_async_remote_copy(
                src_ref=mstage.at[way, i], dst_ref=mrecv.at[way, i], send_sem=m_send.at[way, i], recv_sem=m_recv.at[way, i],
                device_id=to, device_id_type=MESH,
            ),
        )

    def arrived(way, i):
        for copy in q_remote(way, i):
            copy.wait_recv()
        return unpacked(qrecv[way, i], mrecv[way, i, :1])

    def wave(w):
        for way in range(2):
            i = w - z if way == 0 else w - (n - 1 - z)
            ch = n - 1 - i if way == 0 else i

            @pl.when(jnp.logical_and(i >= 0, z < ch if way == 0 else z > ch))
            def _():
                @pl.when(z > 0 if way == 0 else z < n - 1)
                def _():
                    acc[2 * ch + p] = acc[2 * ch + p] + arrived(way, i)

                code, scale = packed(acc[2 * ch + p])
                qstage[way, i] = code
                mstage[way, i] = jnp.broadcast_to(scale, mstage.shape[2:])
                for copy in q_remote(way, i):
                    copy.start()

    def row_end():
        @pl.when(z > 0)
        def _():
            acc[2 * z + p] = acc[2 * z + p] + arrived(0, n - 1 - z)

        @pl.when(z < n - 1)
        def _():
            acc[2 * z + p] = acc[2 * z + p] + arrived(1, z)

        for s in range(supers):
            row_out[s] = -jnp.transpose(acc[2 * z + p, s * width:(s + 1) * width, :])

    gap = max(1, steps // (n - 1))

    def column_step(q, carry):
        w = q // gap

        @pl.when(jnp.logical_and(lax.rem(q, gap) == 0, w < n - 1))
        def _():
            wave(w)

        e = events_early + q // 2

        @pl.when(jnp.logical_and(lax.rem(q, 2) == 0, e < events))
        def _():
            forward(e)

        @pl.when(q == steps - 1)
        def _():
            row_end()

        place, column, up, c = block_of(q)
        for way in range(2):
            @pl.when(jnp.logical_and(jnp.logical_and(q >= blocks, up == way), c + blocks >= sent[way]))
            def _():
                l_remote(way, c, remote_blocks).wait_recv()

        owner = [lower_owner(column, j) for j in range(SLOTS)]
        for s in range(supers):
            real = jnp.zeros((unit, width), jnp.bfloat16)
            imag = jnp.zeros((unit, width), jnp.bfloat16)
            for j in range(SLOTS):
                real = jnp.where(owner[j] == s, lin[place * SLOTS + j, 0], real)
                imag = jnp.where(owner[j] == s, lin[place * SLOTS + j, 1], imag)
            put_pair(rhs, s, real, imag)

        for h in range(2):
            v = 2 * q + h

            @pl.when(v + 1 < 2 * steps)
            def _():
                c_copy(v + 1).start()

            c_copy(v).wait()
            left = jnp.concatenate([cbuf[h, 0], cbuf[h, 1]], axis=1)
            span = slice(h * (rows // 2), (h + 1) * (rows // 2))
            for s in range(supers):
                total = jnp.dot(left, get_pair(rhs, s, width), preferred_element_type=jnp.float32)
                before = cacc[s, span]
                cacc[s, span] = total + jnp.where(q == 0, jnp.zeros_like(before), before)
        return carry

    lax.fori_loop(0, steps, column_step, 0)

    gcopy = pltpu.make_async_copy(given, given_here, o_sem.at[0])
    gcopy.start()

    part = mine.shape[1]

    def writes(s, c):
        lanes = pl.ds(s * width, width)
        return (
            pltpu.make_async_copy(cacc.at[s, pl.ds(pl.multiple_of((2 * c + p) * part, part), part), pl.ds(0, width)], mine.at[c, :, lanes], w_sem.at[0, s, c]),
            pltpu.make_async_copy(cacc.at[s, pl.ds(pl.multiple_of((2 * c + 1 - p) * part, part), part), pl.ds(0, width)], other.at[c, :, lanes], w_sem.at[1, s, c]),
        )

    gcopy.wait()
    origin_flag = jnp.where(jnp.logical_and(z == 0, x == 0), 1.0, 0.0)
    for s in range(supers):
        def mix(i, carry):
            span = pl.ds(pl.multiple_of(i * 2 * part, 2 * part), 2 * part)
            real = cacc[s, span, :width]
            imag = cacc[s, span, width:]
            cacc[s, span, :width] = weights[0] * imag + weights[1] * real
            cacc[s, span, width:] = weights[0] * real - weights[1] * imag
            return carry

        lax.fori_loop(0, n_col, mix, 0)
        for c in range(n_col):
            for copy in writes(s, c):
                copy.start()
        diag[s * width:(s + 1) * width, :] = origin_flag * (
            weights[0] * given_here[s, 1].astype(jnp.float32) + weights[1] * given_here[s, 0].astype(jnp.float32)
        )

    def one(kb, carry):
        start = pl.multiple_of((lax.rem(x - kb // blocks + n_col, n_col) * blocks + lax.rem(kb, blocks)) * unit, unit)
        owner = [upper_owner(kb, j) for j in range(SLOTS)]
        for s in range(supers):
            rights = []
            lefts = []
            for c in range(2):
                value = cacc[s, pl.ds(start, unit), c * width:(c + 1) * width]
                high = value.astype(jnp.bfloat16)
                low = (value - high.astype(jnp.float32)).astype(jnp.bfloat16)
                rights.append(jnp.concatenate([high, low], axis=1))
                chosen = jnp.zeros((unit, width), jnp.bfloat16)
                for j in range(SLOTS):
                    chosen = jnp.where(owner[j] == s, uslots[kb, j, c], chosen)
                lefts.append(jnp.transpose(chosen))
            total = jnp.dot(
                jnp.concatenate(lefts, axis=1), jnp.concatenate(rights, axis=0), preferred_element_type=jnp.float32
            )
            diag[s * width:(s + 1) * width, :] += total[:, :width] + total[:, width:]
        return carry

    lax.fori_loop(0, kbs, one, 0)

    for s in range(supers):
        for c in range(n_col):
            for copy in writes(s, c):
                copy.wait()

    def finish(i, carry):
        for way in range(2):
            ch = n - 1 - i if way == 0 else i

            @pl.when(z < ch if way == 0 else z > ch)
            def _():
                for copy in q_remote(way, i):
                    copy.wait_send()
        return carry

    lax.fori_loop(0, n - 1, finish, 0)

    def l_finish(c, carry):
        for way in range(2):
            @pl.when(c < sent[way])
            def _():
                l_remote(way, c, remote_blocks).wait_send()
        return carry

    lax.fori_loop(0, remote_blocks, l_finish, 0)

    def p_finish(ch, carry):
        p_remote(ch).wait_send()
        return carry

    lax.fori_loop(0, n, p_finish, 0)
    for d in range(1, n_col):
        for b in range(blocks):
            u_remote(d, b).wait_send()


def put_pair(rhs, s, real, imag):
    for i, value in enumerate((real, imag, -imag, real)):
        rhs[i // 2, s, i % 2] = value


def get_pair(rhs, s, width):
    return jnp.concatenate(
        [jnp.concatenate([rhs[i, s, 0], rhs[i, s, 1]], axis=1) for i in range(2)], axis=0
    )


def fused_call(order, weights, inverse, own_l, own_u, given, sizes):
    n, n_col, blocks = sizes
    _, rows, cols = inverse.shape
    _, per, unit, width = own_l.shape
    supers = per // blocks
    wide = supers * width
    kbs = blocks * n_col
    half = cols // n // 2
    part = rows // (2 * n_col)
    dma = pltpu.SemaphoreType.DMA
    shared = unit == width and half == 2 * width and n <= supers * (rows // wide)
    scratch = [
        pltpu.VMEM((2 * n, wide, half), jnp.float32),
        pltpu.VMEM((supers, rows, 2 * width), jnp.float32),
        pltpu.VMEM((2 * wide, 2 * unit), jnp.bfloat16),
        pltpu.VMEM((2, supers, 2, unit, width), jnp.bfloat16),
        pltpu.VMEM((2, 2, unit, 2 * half), jnp.bfloat16),
        pltpu.VMEM((2, 2, rows // 2, unit), jnp.bfloat16),
        pltpu.VMEM((kbs, SLOTS, 2, unit, width), jnp.bfloat16),
        pltpu.VMEM((n * blocks * SLOTS, 2, unit, width), jnp.bfloat16),
        pltpu.VMEM((2, n - 1, wide, half), jnp.int16),
        pltpu.VMEM((2, n - 1, wide, half), jnp.int16),
        pltpu.VMEM((2, n - 1, 8, half), jnp.float32),
        pltpu.VMEM((2, n - 1, 8, half), jnp.float32),
        dma((2,)), dma((2,)), dma((kbs,)), dma((kbs,)), dma((4,)),
        dma((2, n * blocks)), dma((n * blocks,)),
        dma((n,)), dma((n,)),
        dma((2, n - 1)), dma((2, n - 1)), dma((2, n - 1)), dma((2, n - 1)),
        dma((2, supers, n_col)),
    ]
    if not shared:
        scratch.append(pltpu.VMEM((n, wide, half), jnp.float32))
        scratch.append(pltpu.VMEM(given.shape, jnp.bfloat16))
    smem = pl.BlockSpec(memory_space=pltpu.SMEM)
    vmem = pl.BlockSpec(memory_space=pltpu.VMEM)
    hbm = pl.BlockSpec(memory_space=pl.ANY)
    return pl.pallas_call(
        functools.partial(fused_kernel, (n, n_col, supers)),
        out_shape=(
            jax.ShapeDtypeStruct((supers, half, width), jnp.float32),
            jax.ShapeDtypeStruct((n_col, part, wide), jnp.float32),
            jax.ShapeDtypeStruct((n_col, part, wide), jnp.float32),
            jax.ShapeDtypeStruct((wide, width), jnp.float32),
        ),
        in_specs=[smem, smem, hbm, hbm, hbm, hbm],
        out_specs=(vmem, hbm, hbm, vmem),
        scratch_shapes=scratch,
        compiler_params=pltpu.CompilerParams(collective_id=3, has_side_effects=True, vmem_limit_bytes=63 * 2**20),
        name="fused",
    )(order, weights, inverse, own_l, own_u, given)


def body(inverse, lower, upper, diag_inverse, weights, pattern):
    n = lax.axis_size("row")
    n_col = lax.axis_size("col")
    n_groups = lax.axis_size("groups")
    _, local, _, supers, width = lower.shape
    inverse = inverse[0]
    unit = min(width, local)
    blocks = local // unit
    weights = weights[0]
    given = diag_inverse[0]
    order, over = scan_call(pattern, n * n_col * local // width, n_groups)

    def flat(factor):
        return jnp.transpose(factor[0], (1, 2, 0, 3)).reshape(2, supers * blocks, unit, width)

    def usual():
        return fused_call(order, weights, inverse, flat(lower), flat(upper), given, (n, n_col, blocks))

    def rare():
        order, full = plan_call(pattern, (n, n_col), unit, width, blocks)
        own_l = jnp.transpose(flat(lower), (1, 0, 2, 3))
        own_u = jnp.transpose(flat(upper), (1, 0, 2, 3)).reshape(supers, blocks, 2, unit, width)
        lall, uall, row = stream_call(order, weights, inverse, own_l, own_u, (n, n_col))
        row = jnp.transpose(row.reshape(supers, width, -1), (0, 2, 1))
        return (row,) + tuple(column_call(full, weights, inverse, lall, uall, given, (n_col, supers, blocks)))

    row, mine, other, diag = lax.cond(over[0] <= 0, usual, rare)
    column, diagonal = close_call(mine, other, diag, n, n_col)
    return (jnp.transpose(column, (1, 0, 2)), jnp.transpose(row, (1, 0, 2)), diagonal.reshape(supers, width, width))


def solution(mesh):
    return jax.shard_map(
        body,
        mesh=mesh,
        in_specs=(
            P(("groups", "pole"), None, "row", "col"),
            P(("groups", "pole"), ("col", "row"), None, None, None),
            P(("groups", "pole"), ("row", "col"), None, None, None),
            P(("groups", "pole"), None, None, None, None),
            P(("groups", "pole"), None),
            P("groups", None),
        ),
        out_specs=(
            P(("groups", "row", "col", "pole"), None, None),
            P(("groups", "col", "row", "pole"), None, None),
            P("groups", None, None),
        ),
        check_vma=False,
    )
```

```python
import functools
import math

import jax
import jax.numpy as jnp
from jax import lax
from jax.experimental import pallas as pl
from jax.experimental.pallas import tpu as pltpu
from jax.sharding import PartitionSpec as P

MESH = pl.DeviceIdType.MESH
RING = 6
SLOTS = 2
TOP = 32767.0


def full_caps(n, per):
    return [per * d for d in range(n)]


def room(caps):
    n = len(caps)
    return max(caps[z] + caps[n - 1 - z] for z in range(n)) + 1


def stepped(caps, count):
    total = jnp.int32(0)
    for d in range(1, len(caps)):
        total = total + jnp.where(count >= d, caps[d] - caps[d - 1], 0)
    return total


class Streams:
    def __init__(self, caps, first, n, order, lown, lin, stage, send_sem, recv_sem, out_sem, lall):
        self.caps, self.first, self.n = caps, first, n
        self.order, self.lown, self.lin, self.stage = order, lown, lin, stage
        self.send_sem, self.recv_sem, self.out_sem, self.lall = send_sem, recv_sem, out_sem, lall
        self.per = lown.shape[0]
        self.size = lin.shape[0]
        self.z = lax.axis_index("row")
        z = self.z
        self.sent = (jnp.where(z > 0, stepped(caps, n - z), 0), jnp.where(z < n - 1, stepped(caps, z + 1), 0))
        self.taken = (stepped(caps, n - 1 - z), stepped(caps, z))
        self.events = max(caps) - first

    def place(self, way, c):
        return c if way == 0 else self.size - 1 - c

    def remote(self, way, c):
        slot = lax.rem(c, RING)
        place = self.place(way, c)
        return pltpu.make_async_remote_copy(
            src_ref=self.stage.at[way, slot],
            dst_ref=self.lin.at[place],
            send_sem=self.send_sem.at[way, slot],
            recv_sem=self.recv_sem.at[place],
            device_id={"row": self.z - 1 if way == 0 else self.z + 1},
            device_id_type=MESH,
        )

    def kept(self, way, c):
        place = self.place(way, c)
        return pltpu.make_async_copy(self.lin.at[place], self.lall.at[self.per + place], self.out_sem.at[place])

    def begin(self):
        for way in range(2):
            @pl.when(self.sent[way] > 0)
            def _():
                for c in range(self.first):
                    if c >= RING:
                        self.remote(way, c - RING).wait_send()
                    self.stage[way, c % RING] = self.lown[self.order[c]]
                    self.remote(way, c).start()

    def forward(self, d):
        c = d + self.first
        for way in range(2):
            @pl.when(c < self.sent[way])
            def _():
                @pl.when(d < self.taken[way])
                def _():
                    self.remote(way, d).wait_recv()
                    self.kept(way, d).start()

                @pl.when(c >= RING)
                def _():
                    self.remote(way, c - RING).wait_send()

                count = self.order[self.per + way]
                mine = self.lown[self.order[jnp.clip(c - count, 0, self.per - 1)]]
                arrived = self.lin[self.place(way, jnp.clip(d, 0, jnp.maximum(self.taken[way] - 1, 0)))]
                self.stage[way, lax.rem(c, RING)] = jnp.where(d < count, arrived, mine)
                self.remote(way, c).start()

    def drain(self):
        def step(c, carry):
            for way in range(2):
                @pl.when(jnp.logical_and(c < self.taken[way], c + self.first >= self.sent[way]))
                def _():
                    self.remote(way, c).wait_recv()
                    self.kept(way, c).start()

                @pl.when(jnp.logical_and(c < self.sent[way], c + RING >= self.sent[way]))
                def _():
                    self.remote(way, c).wait_send()
            return carry

        lax.fori_loop(0, max(self.caps), step, 0)

        def last(c, carry):
            for way in range(2):
                @pl.when(c < self.taken[way])
                def _():
                    self.kept(way, c).wait()
            return carry

        lax.fori_loop(0, max(self.caps), last, 0)


def greet(targets):
    barrier = pltpu.get_barrier_semaphore()
    total = jnp.int32(0)
    for axis, size, near in targets:
        me = lax.axis_index(axis)
        if near:
            for step in (-1, 1):
                there = jnp.logical_and(me + step >= 0, me + step < size)

                @pl.when(there)
                def _():
                    pl.semaphore_signal(barrier, inc=1, device_id={axis: me + step}, device_id_type=MESH)

                total = total + there.astype(jnp.int32)
        else:
            for d in range(1, size):
                pl.semaphore_signal(barrier, inc=1, device_id={axis: lax.rem(me + d, size)}, device_id_type=MESH)
            total = total + (size - 1)
    pl.semaphore_wait(barrier, total)


def packed(value):
    most = jnp.max(jnp.abs(value), axis=0, keepdims=True)
    factor = jnp.where(most > 0, TOP / jnp.maximum(most, 1e-30), 0.0)
    return jnp.round(value * factor).astype(jnp.int32).astype(jnp.int16), most * (1.0 / TOP)


def unpacked(code, scale):
    return code.astype(jnp.int32).astype(jnp.float32) * scale


def stream_kernel(cfg, order, weights, inverse, own_l, own_u, lall, uall, row_out, *scratch):
    (acc, lhs, abuf, ubuf, lown, lin, stage, prec, qstage, qrecv, mstage, mrecv,
     a_sem, u_send, u_recv, l_sem, s_send, s_recv, s_out, p_send, p_recv, q_send, q_recv, m_send, m_recv) = scratch
    n, n_col, caps = cfg
    per = lown.shape[0]
    supers, kbs, _, unit, width = ubuf.shape
    blocks = kbs // n_col
    half = acc.shape[2]
    tile = 2 * half
    z = lax.axis_index("row")
    x = lax.axis_index("col")
    p = lax.axis_index("pole")

    lcopy = pltpu.make_async_copy(own_l, lown, l_sem.at[0])
    lcopy.start()
    ucopy = pltpu.make_async_copy(own_u, ubuf.at[:, pl.ds(0, blocks)], l_sem.at[1])
    ucopy.start()

    def a_copy(t):
        kb = t // n
        origin = lax.rem(x - kb // blocks + n_col, n_col)
        row = (origin * blocks + lax.rem(kb, blocks)) * unit
        return pltpu.make_async_copy(
            inverse.at[:, pl.ds(pl.multiple_of(row, unit), unit), pl.ds(pl.multiple_of(lax.rem(t, n) * tile, tile), tile)],
            abuf.at[lax.rem(t, 3)],
            a_sem.at[lax.rem(t, 3)],
        )

    a_copy(0).start()
    a_copy(1).start()
    greet((("row", n, True), ("col", n_col, False), ("pole", 2, False)))

    def u_remote(d, b):
        return pltpu.make_async_remote_copy(
            src_ref=own_u.at[:, b],
            dst_ref=ubuf.at[:, d * blocks + b],
            send_sem=u_send.at[d * blocks + b],
            recv_sem=u_recv.at[d * blocks + b],
            device_id={"col": lax.rem(x + d, n_col)},
            device_id_type=MESH,
        )

    for b in range(blocks):
        for d in range(1, n_col):
            u_remote(d, b).start()

    lcopy.wait()
    streams = Streams(caps, blocks, n, order, lown, lin, stage, s_send, s_recv, s_out, lall)
    streams.begin()
    lout = pltpu.make_async_copy(lown, lall.at[pl.ds(0, per)], l_sem.at[0])
    lout.start()
    ucopy.wait()

    tiles = kbs * n
    early = blocks * n
    events = streams.events
    events_early = events * 5 // 18
    events_late = events - events_early
    late = tiles - early

    def due(t):
        if late == 0:
            return t * events // early
        return jnp.where(t < early, t * events_early // early, events_early + (t - early) * events_late // late)

    def row_tile(t, carry):
        kb = t // n
        j = lax.rem(t, n)

        @pl.when(j == 0)
        def _():
            @pl.when(kb >= blocks)
            def _():
                u_remote(kb // blocks, lax.rem(kb, blocks)).wait_recv()

            for s in range(supers):
                kept = order[per + 2 + kb * supers + s] > 0
                real = jnp.where(kept, ubuf[s, kb, 0].astype(jnp.float32), 0.0)
                imag = jnp.where(kept, ubuf[s, kb, 1].astype(jnp.float32), 0.0)
                span = slice(s * width, (s + 1) * width)
                for i, value in enumerate((weights[1] * real + weights[0] * imag, weights[0] * real - weights[1] * imag)):
                    turned = jnp.transpose(value)
                    high = turned.astype(jnp.bfloat16)
                    lhs[0, span, i * unit:(i + 1) * unit] = high
                    lhs[1, span, i * unit:(i + 1) * unit] = (turned - high.astype(jnp.float32)).astype(jnp.bfloat16)

        @pl.when(t + 2 < tiles)
        def _():
            a_copy(t + 2).start()

        a_copy(t).wait()
        slot = lax.rem(t, 3)
        for q in range(2):
            right = abuf[slot, :, :, q * half:(q + 1) * half].reshape(2 * unit, half)
            total = jnp.dot(lhs[0], right, preferred_element_type=jnp.float32) + jnp.dot(
                lhs[1], right, preferred_element_type=jnp.float32
            )
            before = acc[2 * j + q]
            acc[2 * j + q] = total + jnp.where(kb == 0, jnp.zeros_like(before), before)

        now = due(t)

        def some(d, carry):
            streams.forward(d)
            return carry

        lax.fori_loop(now, due(t + 1), some, 0)
        return carry

    lax.fori_loop(0, tiles, row_tile, 0)

    uout = pltpu.make_async_copy(ubuf, uall, l_sem.at[1])
    uout.start()

    def p_remote(ch):
        return pltpu.make_async_remote_copy(
            src_ref=acc.at[2 * ch + 1 - p],
            dst_ref=prec.at[ch],
            send_sem=p_send.at[ch],
            recv_sem=p_recv.at[ch],
            device_id={"pole": 1 - p},
            device_id_type=MESH,
        )

    for i in range((n + 1) // 2):
        p_remote(n - 1 - i).start()
        if i != n - 1 - i:
            p_remote(i).start()

    def q_remote(way, i):
        to = {"row": z + 1 if way == 0 else z - 1}
        return (
            pltpu.make_async_remote_copy(
                src_ref=qstage.at[way, i], dst_ref=qrecv.at[way, i], send_sem=q_send.at[way, i], recv_sem=q_recv.at[way, i],
                device_id=to, device_id_type=MESH,
            ),
            pltpu.make_async_remote_copy(
                src_ref=mstage.at[way, i], dst_ref=mrecv.at[way, i], send_sem=m_send.at[way, i], recv_sem=m_recv.at[way, i],
                device_id=to, device_id_type=MESH,
            ),
        )

    def arrived(way, i):
        for copy in q_remote(way, i):
            copy.wait_recv()
        return unpacked(qrecv[way, i], mrecv[way, i, :1])

    def row_step(i, carry):
        for way in range(2):
            ch = n - 1 - i if way == 0 else i

            @pl.when(z < ch if way == 0 else z > ch)
            def _():
                p_remote(ch).wait_recv()
                acc[2 * ch + p] = acc[2 * ch + p] + prec[ch]

                @pl.when(z > 0 if way == 0 else z < n - 1)
                def _():
                    acc[2 * ch + p] = acc[2 * ch + p] + arrived(way, i)

                code, scale = packed(acc[2 * ch + p])
                qstage[way, i] = code
                mstage[way, i] = jnp.broadcast_to(scale, mstage.shape[2:])
                for copy in q_remote(way, i):
                    copy.start()
        return carry

    lax.fori_loop(0, n - 1, row_step, 0)

    p_remote(z).wait_recv()
    row_out[...] = acc[2 * z + p] + prec[z]

    @pl.when(z > 0)
    def _():
        row_out[...] = row_out[...] + arrived(0, n - 1 - z)

    @pl.when(z < n - 1)
    def _():
        row_out[...] = row_out[...] + arrived(1, z)

    row_out[...] = -row_out[...]
    streams.drain()

    def finish(i, carry):
        for way in range(2):
            ch = n - 1 - i if way == 0 else i

            @pl.when(z < ch if way == 0 else z > ch)
            def _():
                for copy in q_remote(way, i):
                    copy.wait_send()
        return carry

    lax.fori_loop(0, n - 1, finish, 0)
    for ch in range(n):
        p_remote(ch).wait_send()
    for d in range(1, n_col):
        for b in range(blocks):
            u_remote(d, b).wait_send()
    lout.wait()
    uout.wait()


def stream_call(order, weights, inverse, own_l, own_u, sizes):
    n, n_col = sizes
    _, rows, cols = inverse.shape
    per, _, unit, width = own_l.shape
    supers, blocks = own_u.shape[:2]
    wide = supers * width
    caps = full_caps(n, per)
    kbs = blocks * n_col
    half = cols // n // 2
    space = room(caps)
    dma = pltpu.SemaphoreType.DMA
    scratch = [
        pltpu.VMEM((2 * n, wide, half), jnp.float32),
        pltpu.VMEM((2, wide, 2 * unit), jnp.bfloat16),
        pltpu.VMEM((3, 2, unit, 2 * half), jnp.bfloat16),
        pltpu.VMEM((supers, kbs, 2, unit, width), jnp.bfloat16),
        pltpu.VMEM((per, 2, unit, width), jnp.bfloat16),
        pltpu.VMEM((space, 2, unit, width), jnp.bfloat16),
        pltpu.VMEM((2, RING, 2, unit, width), jnp.bfloat16),
        pltpu.VMEM((n, wide, half), jnp.float32),
        pltpu.VMEM((2, n - 1, wide, half), jnp.int16),
        pltpu.VMEM((2, n - 1, wide, half), jnp.int16),
        pltpu.VMEM((2, n - 1, 8, half), jnp.float32),
        pltpu.VMEM((2, n - 1, 8, half), jnp.float32),
        dma((3,)), dma((kbs,)), dma((kbs,)), dma((2,)),
        dma((2, RING)), dma((space,)), dma((space,)),
        dma((n,)), dma((n,)),
        dma((2, n - 1)), dma((2, n - 1)), dma((2, n - 1)), dma((2, n - 1)),
    ]
    smem = pl.BlockSpec(memory_space=pltpu.SMEM)
    vmem = pl.BlockSpec(memory_space=pltpu.VMEM)
    hbm = pl.BlockSpec(memory_space=pl.ANY)
    return pl.pallas_call(
        functools.partial(stream_kernel, (n, n_col, caps)),
        out_shape=(
            jax.ShapeDtypeStruct((per + space, 2, unit, width), jnp.bfloat16),
            jax.ShapeDtypeStruct((supers, kbs, 2, unit, width), jnp.bfloat16),
            jax.ShapeDtypeStruct((wide, half), jnp.float32),
        ),
        in_specs=[smem, smem, hbm, hbm, hbm],
        out_specs=(hbm, hbm, vmem),
        scratch_shapes=scratch,
        compiler_params=pltpu.CompilerParams(collective_id=0, has_side_effects=True, vmem_limit_bytes=62 * 2**20),
        name="streams",
    )(order, weights, inverse, own_l, own_u)


def column_kernel(cfg, meta, weights, a_ref, *rest):
    supers, n_col, blocks = cfg
    l_refs = rest[:supers]
    u_ref, given, mine, other, diag, acc = rest[supers:]
    k = pl.program_id(0)
    steps = pl.num_programs(0)
    _, rows, double = acc.shape
    width = double // 2
    unit = a_ref.shape[2]
    base = 2 * supers * steps
    piece = rows

    @pl.when(k == 0)
    def _():
        acc[...] = jnp.zeros_like(acc)

    for s in range(supers):
        @pl.when(meta[k * supers + s] > 0)
        def _():
            real = l_refs[s][0, 0]
            imag = l_refs[s][0, 1]
            right = jnp.concatenate([jnp.concatenate([real, imag], axis=1), jnp.concatenate([-imag, real], axis=1)], axis=0)

            def part(i, carry):
                span = pl.ds(pl.multiple_of(i * piece, piece), piece)
                left = jnp.concatenate([a_ref[0, span], a_ref[1, span]], axis=1)
                acc[s, span] += jnp.dot(left, right, preferred_element_type=jnp.float32)
                return carry

            lax.fori_loop(0, rows // piece, part, 0)

    @pl.when(k == steps - 1)
    def _():
        part = mine.shape[1]
        pole = meta[base]
        for s in range(supers):
            lanes = slice(s * width, (s + 1) * width)
            for c in range(n_col):
                for q in range(2):
                    span = pl.ds((2 * c + q) * part, part)
                    real = acc[s, span, :width]
                    imag = acc[s, span, width:]
                    mixed = weights[0] * imag + weights[1] * real
                    acc[s, span, :width] = mixed
                    acc[s, span, width:] = weights[0] * real - weights[1] * imag

                    @pl.when(pole == q)
                    def _():
                        mine[c, :, lanes] = mixed

                    @pl.when(pole != q)
                    def _():
                        other[c, :, lanes] = mixed

            @pl.when(meta[base + 1] > 0)
            def _():
                diag[lanes, :] = weights[0] * given[s, 1].astype(jnp.float32) + weights[1] * given[s, 0].astype(jnp.float32)

            @pl.when(meta[base + 1] == 0)
            def _():
                diag[lanes, :] = jnp.zeros((width, diag.shape[1]), jnp.float32)

        def one(kb, carry):
            for s in range(supers):
                lanes = slice(s * width, (s + 1) * width)

                @pl.when(meta[base + 2 + n_col + kb * supers + s] > 0)
                def _():
                    start = pl.multiple_of(meta[base + 2 + kb // blocks] + lax.rem(kb, blocks) * unit, unit)
                    total = jnp.zeros((width, width), jnp.float32)
                    for c in range(2):
                        value = acc[s, pl.ds(start, unit), c * width:(c + 1) * width]
                        high = value.astype(jnp.bfloat16)
                        low = (value - high.astype(jnp.float32)).astype(jnp.bfloat16)
                        turned = jnp.transpose(u_ref[s, kb, c])
                        total += jnp.dot(turned, high, preferred_element_type=jnp.float32) + jnp.dot(
                            turned, low, preferred_element_type=jnp.float32
                        )
                    diag[lanes, :] += total
            return carry

        lax.fori_loop(0, u_ref.shape[1], one, 0)


def column_call(meta, weights, inverse, lall, uall, given, sizes):
    n_col, supers, blocks = sizes
    _, rows, cols = inverse.shape
    _, _, unit, width = lall.shape
    steps = cols // unit
    part = rows // (2 * n_col)

    def slot(s):
        return lambda k, meta: (meta[supers * steps + k * supers + s], 0, 0, 0)

    whole = pl.BlockSpec(uall.shape, lambda k, meta: (0, 0, 0, 0, 0))
    out = pl.BlockSpec((n_col, part, supers * width), lambda k, meta: (0, 0, 0))
    return pl.pallas_call(
        functools.partial(column_kernel, (supers, n_col, blocks)),
        out_shape=(
            jax.ShapeDtypeStruct((n_col, part, supers * width), jnp.float32),
            jax.ShapeDtypeStruct((n_col, part, supers * width), jnp.float32),
            jax.ShapeDtypeStruct((supers * width, width), jnp.float32),
        ),
        grid_spec=pltpu.PrefetchScalarGridSpec(
            num_scalar_prefetch=1,
            grid=(steps,),
            in_specs=[
                pl.BlockSpec(memory_space=pltpu.SMEM),
                pl.BlockSpec((2, rows, unit), lambda k, meta: (0, 0, k)),
            ]
            + [pl.BlockSpec((1, 2, unit, width), slot(s)) for s in range(supers)]
            + [whole, pl.BlockSpec(given.shape, lambda k, meta: (0, 0, 0, 0))],
            out_specs=(out, out, pl.BlockSpec((supers * width, width), lambda k, meta: (0, 0))),
            scratch_shapes=[pltpu.VMEM((supers, rows, 2 * width), jnp.float32)],
        ),
        compiler_params=pltpu.CompilerParams(vmem_limit_bytes=60 * 2**20),
        name="columns",
    )(meta, weights, inverse, *([lall] * supers), uall, given)


def close_kernel(cfg, mine, other, diag, column, total, *scratch):
    (here, prec, kept, qstage, qrecv, mstage, mrecv, dpole, dvalue, xcode, xscale, zcode, zscale, zin, zinscale, gcode, gscale,
     h_sem, p_send, p_recv, q_send, q_recv, m_send, m_recv, dp_send, dp_recv, x_send, x_recv, xs_send, xs_recv,
     z_send, z_recv, zs_send, zs_recv, g_send, g_recv, gs_send, gs_recv, gp_send, gp_recv) = scratch
    n, n_col = cfg
    z = lax.axis_index("row")
    x = lax.axis_index("col")
    p = lax.axis_index("pole")
    high = diag.shape[0] // 2
    slab = high // n
    supers, _, width = column.shape

    def remote(src, dst, send, recv, to):
        return pltpu.make_async_remote_copy(
            src_ref=src, dst_ref=dst, send_sem=send, recv_sem=recv, device_id=to, device_id_type=MESH
        )

    def p_remote(d):
        return remote(other.at[lax.rem(x + d, n_col)], prec.at[d], p_send.at[d], p_recv.at[d], {"pole": 1 - p})

    def h_copy(d):
        return pltpu.make_async_copy(mine.at[lax.rem(x + d, n_col)], here.at[d], h_sem.at[d])

    def dp_remote():
        return remote(diag.at[pl.ds(pl.multiple_of((1 - p) * high, 8), high)], dpole, dp_send.at[0], dp_recv.at[0], {"pole": 1 - p})

    def x_remote(d):
        to = {"col": lax.rem(x + d, n_col)}
        return (
            remote(xcode.at[0], xcode.at[d], x_send.at[d], x_recv.at[d], to),
            remote(xscale.at[0], xscale.at[d], xs_send.at[d], xs_recv.at[d], to),
        )

    def q_remote(d):
        to = {"col": lax.rem(x + d, n_col)}
        return (
            remote(qstage.at[d], qrecv.at[d], q_send.at[d], q_recv.at[d], to),
            remote(mstage.at[d], mrecv.at[d], m_send.at[d], m_recv.at[d], to),
        )

    def z_remote(d):
        to = {"row": lax.rem(z + d, n)}
        return (
            remote(zcode.at[d], zin.at[d], z_send.at[d], z_recv.at[d], to),
            remote(zscale.at[d], zinscale.at[d], zs_send.at[d], zs_recv.at[d], to),
        )

    def g_remote(d):
        to = {"row": lax.rem(z + d, n)}
        return (
            remote(gcode.at[0], gcode.at[d], g_send.at[d], g_recv.at[d], to),
            remote(gscale.at[0], gscale.at[d], gs_send.at[d], gs_recv.at[d], to),
        )

    def rows_of(place):
        return pl.ds(pl.multiple_of(p * high + place * slab, 8), slab)

    def gp_remote():
        span = pl.ds(pl.multiple_of(p * high, 8), high)
        return remote(total.at[span], total.at[span], gp_send.at[0], gp_recv.at[0], {"pole": 1 - p})

    def put(code_ref, scale_ref, d, value):
        code, scale = packed(value)
        code_ref[d] = code
        scale_ref[d] = jnp.broadcast_to(scale, scale_ref.shape[1:])

    def get(code_ref, scale_ref, d):
        return unpacked(code_ref[d], scale_ref[d, :1])

    for d in range(n_col):
        h_copy(d).start()
    greet((("row", n, False), ("col", n_col, False), ("pole", 2, False)))
    dp_remote().start()
    for d in range(1, n_col):
        p_remote(d).start()
    p_remote(0).start()

    dp_remote().wait_recv()
    put(xcode, xscale, 0, diag[pl.ds(pl.multiple_of(p * high, 8), high)] + dpole[...])
    for d in range(1, n_col):
        for copy in x_remote(d):
            copy.start()

    for d in range(1, n_col):
        p_remote(d).wait_recv()
        h_copy(d).wait()
        put(qstage, mstage, d, here[d] + prec[d])
        for copy in q_remote(d):
            copy.start()

    for d in range(1, n_col):
        for copy in x_remote(d):
            copy.wait_recv()
    value = jnp.zeros((high, width), jnp.float32)
    for origin in range(n_col):
        d = lax.rem(x - origin + n_col, n_col)
        value = value + get(xcode, xscale, d)
    dvalue[...] = value
    for d in range(1, n):
        to = lax.rem(z + d, n)
        put(zcode, zscale, d, dvalue[pl.ds(pl.multiple_of(to * slab, 8), slab)])
        for copy in z_remote(d):
            copy.start()
    p_remote(0).wait_recv()
    h_copy(0).wait()
    kept[...] = here[0] + prec[0]
    value = dvalue[pl.ds(pl.multiple_of(z * slab, 8), slab)]
    for d in range(1, n):
        for copy in z_remote(d):
            copy.wait_recv()
        value = value + get(zin, zinscale, d)
    put(gcode, gscale, 0, value)
    for d in range(1, n):
        for copy in g_remote(d):
            copy.start()
    total[rows_of(z)] = get(gcode, gscale, 0)
    for d in range(1, n):
        for copy in g_remote(d):
            copy.wait_recv()
        total[rows_of(lax.rem(z - d + n, n))] = get(gcode, gscale, d)
    gp_remote().start()

    for d in range(1, n_col):
        for copy in q_remote(d):
            copy.wait_recv()
        kept[...] = kept[...] + get(qrecv, mrecv, d)
    for s in range(supers):
        column[s] = -kept[:, s * width:(s + 1) * width]

    gp_remote().wait_send()
    span = pl.ds(pl.multiple_of((1 - p) * high, 8), high)
    remote(total.at[span], total.at[span], gp_send.at[0], gp_recv.at[0], {"pole": 1 - p}).wait_recv()
    dp_remote().wait_send()
    for d in range(n_col):
        p_remote(d).wait_send()
    for d in range(1, n):
        for copy in z_remote(d) + g_remote(d):
            copy.wait_send()
    for d in range(1, n_col):
        for copy in x_remote(d) + q_remote(d):
            copy.wait_send()


def close_call(mine, other, diag, n, n_col):
    _, part, wide = mine.shape
    tall, width = diag.shape
    supers = wide // width
    high = tall // 2
    slab = high // n
    dma = pltpu.SemaphoreType.DMA
    vmem = pl.BlockSpec(memory_space=pltpu.VMEM)
    hbm = pl.BlockSpec(memory_space=pl.ANY)
    return pl.pallas_call(
        functools.partial(close_kernel, (n, n_col)),
        out_shape=(
            jax.ShapeDtypeStruct((supers, part, width), jnp.float32),
            jax.ShapeDtypeStruct((tall, width), jnp.float32),
        ),
        in_specs=[hbm, hbm, vmem],
        out_specs=(vmem, vmem),
        scratch_shapes=[
            pltpu.VMEM((n_col, part, wide), jnp.float32),
            pltpu.VMEM((n_col, part, wide), jnp.float32),
            pltpu.VMEM((part, wide), jnp.float32),
            pltpu.VMEM((n_col, part, wide), jnp.int16),
            pltpu.VMEM((n_col, part, wide), jnp.int16),
            pltpu.VMEM((n_col, 8, wide), jnp.float32),
            pltpu.VMEM((n_col, 8, wide), jnp.float32),
            pltpu.VMEM((high, width), jnp.float32),
            pltpu.VMEM((high, width), jnp.float32),
            pltpu.VMEM((n_col, high, width), jnp.int16),
            pltpu.VMEM((n_col, 8, width), jnp.float32),
            pltpu.VMEM((n, slab, width), jnp.int16),
            pltpu.VMEM((n, 8, width), jnp.float32),
            pltpu.VMEM((n, slab, width), jnp.int16),
            pltpu.VMEM((n, 8, width), jnp.float32),
            pltpu.VMEM((n, slab, width), jnp.int16),
            pltpu.VMEM((n, 8, width), jnp.float32),
            dma((n_col,)), dma((n_col,)), dma((n_col,)), dma((n_col,)), dma((n_col,)), dma((n_col,)), dma((n_col,)),
            dma((1,)), dma((1,)), dma((n_col,)), dma((n_col,)), dma((n_col,)), dma((n_col,)),
            dma((n,)), dma((n,)), dma((n,)), dma((n,)), dma((n,)), dma((n,)), dma((n,)), dma((n,)), dma((1,)), dma((1,)),
        ],
        compiler_params=pltpu.CompilerParams(collective_id=2, has_side_effects=True, vmem_limit_bytes=40 * 2**20),
        name="close",
    )(mine, other, diag)


def plan_kernel(cfg, pattern, order, full, keep, count):
    n, n_col, blocks, unit, width = cfg
    supers, entries = pattern.shape
    z = lax.axis_index("row")
    x = lax.axis_index("col")
    p = lax.axis_index("pole")
    per = supers * blocks
    units = n * n_col * blocks
    steps = n * blocks
    split = width // unit

    def clear(i, carry):
        keep[i] = 0
        return carry

    lax.fori_loop(0, supers * units, clear, 0)

    def mark(i, carry):
        s = i // entries
        at = s * units + pattern[s, lax.rem(i, entries)] * split
        for r in range(split):
            keep[at + r] = 1
        return carry

    lax.fori_loop(0, supers * entries, mark, 0)

    def number(i, carry):
        total = jnp.int32(0)
        for s in range(supers):
            for b in range(blocks):
                total = total + keep[s * units + i * blocks + b]
        count[i] = total
        return carry

    lax.fori_loop(0, n * n_col, number, 0)

    def pack(r, rank):
        s = r // blocks
        k = keep[s * units + (x * n + z) * blocks + lax.rem(r, blocks)]
        order[r] = 0

        @pl.when(k > 0)
        def _():
            order[rank] = r

        return rank + k

    lax.fori_loop(0, per, pack, jnp.int32(0))

    def around(i, sums):
        k = count[x * n + i]
        return sums[0] + jnp.where(i > z, k, 0), sums[1] + jnp.where(i < z, k, 0)

    above, below = lax.fori_loop(0, n, around, (jnp.int32(0), jnp.int32(0)))
    order[per] = above
    order[per + 1] = below

    base = 2 * supers * steps
    full[base] = p
    full[base + 1] = jnp.logical_and(z == 0, x == 0).astype(jnp.int32)
    for d in range(n_col):
        full[base + 2 + d] = lax.rem(x - d + n_col, n_col) * blocks * unit

    def rows(i, carry):
        kb = i // supers
        origin = lax.rem(x - kb // blocks + n_col, n_col)
        k = keep[lax.rem(i, supers) * units + (z * n_col + origin) * blocks + lax.rem(kb, blocks)]
        order[per + 2 + i] = k
        full[base + 2 + n_col + i] = k
        return carry

    lax.fori_loop(0, n_col * blocks * supers, rows, 0)

    def device(at, before):
        here = count[x * n + at]
        after = jnp.int32(0)
        for i in range(n):
            after = after + jnp.where(i > at, count[x * n + i], 0)

        def pair(r, rank):
            s = r // blocks
            b = lax.rem(r, blocks)
            k = keep[s * units + (x * n + at) * blocks + b]
            down = blocks * (at - z - 1) + rank + jnp.where(rank < blocks, 0, after)
            up = blocks * (z - 1 - at) + rank + jnp.where(rank < blocks, 0, before)
            to = (at * blocks + b) * supers + s
            place = jnp.where(at == z, r, jnp.where(at > z, per + down, per + room(full_caps(n, per)) - 1 - up))
            full[to] = k
            full[supers * steps + to] = jnp.where(k > 0, place, 0)
            return rank + k

        lax.fori_loop(0, per, pair, jnp.int32(0))
        return before + here

    lax.fori_loop(0, n, device, jnp.int32(0))


def plan_call(pattern, sizes, unit, width, blocks):
    n, n_col = sizes
    supers, _ = pattern.shape
    per = supers * blocks
    table = 2 * supers * n * blocks + 2 + n_col + n_col * blocks * supers
    smem = pl.BlockSpec(memory_space=pltpu.SMEM)
    return pl.pallas_call(
        functools.partial(plan_kernel, (n, n_col, blocks, unit, width)),
        out_shape=(
            jax.ShapeDtypeStruct((per + 2 + n_col * blocks * supers,), jnp.int32),
            jax.ShapeDtypeStruct((table,), jnp.int32),
        ),
        in_specs=[smem],
        out_specs=(smem, smem),
        scratch_shapes=[pltpu.SMEM((supers * n * n_col * blocks,), jnp.int32), pltpu.SMEM((n * n_col,), jnp.int32)],
        name="plan",
    )(pattern)


def scan_kernel(cfg, pattern, order, over, flags, send, recv):
    n_groups, = cfg
    supers, entries = pattern.shape
    g = lax.axis_index("groups")
    lane = lax.broadcasted_iota(jnp.int32, order.shape, 1)
    row = lax.broadcasted_iota(jnp.int32, order.shape, 0)
    rank = jnp.zeros(order.shape, jnp.int32)
    table = jnp.full(order.shape, -1, jnp.int32)
    for s in range(supers):
        hit = jnp.zeros(order.shape, jnp.int32)
        for j in range(entries):
            hit = jnp.where(lane == pattern[s, j], 1, hit)
        table = jnp.where(jnp.where(row == rank, hit, 0) > 0, s, table)
        rank = rank + hit
    order[...] = table
    bad = jnp.max(jnp.where(rank > SLOTS, 1.0, 0.0))
    flags[0] = jnp.full(flags.shape[1:], bad, jnp.float32)

    def copy(d):
        return pltpu.make_async_remote_copy(
            src_ref=flags.at[0], dst_ref=flags.at[d], send_sem=send.at[d], recv_sem=recv.at[d],
            device_id={"groups": lax.rem(g + d, n_groups)}, device_id_type=MESH,
        )

    greet((("groups", n_groups, False),))
    for d in range(1, n_groups):
        copy(d).start()
    for d in range(1, n_groups):
        copy(d).wait_send()
        copy(d).wait_recv()
    over[0] = jnp.max(flags[...])


def scan_call(pattern, owners, n_groups):
    smem = pl.BlockSpec(memory_space=pltpu.SMEM)
    dma = pltpu.SemaphoreType.DMA
    return pl.pallas_call(
        functools.partial(scan_kernel, (n_groups,)),
        out_shape=(
            jax.ShapeDtypeStruct((8, -(-owners // 128) * 128), jnp.int32),
            jax.ShapeDtypeStruct((1,), jnp.float32),
        ),
        in_specs=[smem],
        out_specs=(pl.BlockSpec(memory_space=pltpu.VMEM), smem),
        scratch_shapes=[pltpu.VMEM((n_groups, 8, 128), jnp.float32), dma((n_groups,)), dma((n_groups,))],
        compiler_params=pltpu.CompilerParams(collective_id=1, has_side_effects=True),
        name="scan",
    )(pattern)


def fused_kernel(cfg, order, weights, inverse, own_l, own_u, given, row_out, mine, other, diag, *scratch):
    (acc, cacc, lhs, rhs, abuf, cbuf, uslots, lin, qstage, qrecv, mstage, mrecv,
     a_sem, c_sem, u_send, u_recv, o_sem, l_send, l_recv, p_send, p_recv, q_send, q_recv, m_send, m_recv, w_sem) = scratch[:26]
    n, n_col, supers = cfg
    z = lax.axis_index("row")
    x = lax.axis_index("col")
    p = lax.axis_index("pole")
    kbs, _, _, unit, width = uslots.shape
    blocks = kbs // n_col
    remote_blocks = (n - 1) * blocks
    half = acc.shape[2]
    tile = 2 * half
    rows = cacc.shape[1]
    apart = len(scratch) > 26
    prec = scratch[26] if apart else cacc

    def given_at(s, c):
        return scratch[27].at[s, c] if apart else cbuf.at[0, c, pl.ds(s * width, width)]

    wide = supers * width

    def lower_owner(k, j):
        return order[j, (x * n * blocks + k) * unit // width]

    def upper_owner(kb, j):
        origin = lax.rem(x - kb // blocks + n_col, n_col)
        return order[j, ((z * n_col + origin) * blocks + lax.rem(kb, blocks)) * unit // width]

    def place_of(ch):
        if not apart:
            fit = rows // wide
            return cacc.at[ch // fit, pl.ds(pl.multiple_of(lax.rem(ch, fit) * wide, wide), wide)]
        return prec.at[ch]

    def a_copy(t):
        kb = t // n
        origin = lax.rem(x - kb // blocks + n_col, n_col)
        row = (origin * blocks + lax.rem(kb, blocks)) * unit
        return pltpu.make_async_copy(
            inverse.at[:, pl.ds(pl.multiple_of(row, unit), unit), pl.ds(pl.multiple_of(lax.rem(t, n) * tile, tile), tile)],
            abuf.at[lax.rem(t, 2)],
            a_sem.at[lax.rem(t, 2)],
        )

    per = supers * blocks
    own = [
        pltpu.make_async_copy(source.at[c], lin.at[pl.ds(i * per, per), c], o_sem.at[2 * i + c])
        for i, source in enumerate((own_l, own_u))
        for c in range(2)
    ]
    for copy in own:
        copy.start()
    a_copy(0).start()
    for copy in own:
        copy.wait()
    for b in range(blocks):
        for j in range(SLOTS):
            chosen = jnp.maximum(lower_owner(z * blocks + b, j), 0)
            lin[(remote_blocks + b) * SLOTS + j] = lin[chosen * blocks + b]
            chosen = jnp.maximum(upper_owner(b, j), 0)
            uslots[b, j] = lin[per + chosen * blocks + b]
    greet((("row", n, True), ("col", n_col, False), ("pole", 2, False)))

    def u_remote(d, b):
        return pltpu.make_async_remote_copy(
            src_ref=uslots.at[b], dst_ref=uslots.at[d * blocks + b],
            send_sem=u_send.at[d * blocks + b], recv_sem=u_recv.at[d * blocks + b],
            device_id={"col": lax.rem(x + d, n_col)}, device_id_type=MESH,
        )

    sent = (jnp.where(z > 0, (n - z) * blocks, 0), jnp.where(z < n - 1, (z + 1) * blocks, 0))
    taken = ((n - 1 - z) * blocks, z * blocks)

    def l_place(way, c):
        return c if way == 0 else remote_blocks - 1 - c

    def l_remote(way, c, source):
        return pltpu.make_async_remote_copy(
            src_ref=lin.at[pl.ds(source * SLOTS, SLOTS)], dst_ref=lin.at[pl.ds(l_place(way, c) * SLOTS, SLOTS)],
            send_sem=l_send.at[way, c], recv_sem=l_recv.at[l_place(way, c)],
            device_id={"row": z - 1 if way == 0 else z + 1}, device_id_type=MESH,
        )

    for b in range(blocks):
        for d in range(1, n_col):
            u_remote(d, b).start()
        for way in range(2):
            @pl.when(sent[way] > 0)
            def _():
                l_remote(way, b, remote_blocks + b).start()

    def forward(c):
        for way in range(2):
            @pl.when(c + blocks < sent[way])
            def _():
                l_remote(way, c, l_place(way, c)).wait_recv()
                l_remote(way, c + blocks, l_place(way, c)).start()

    tiles = kbs * n
    events = (n - 2) * blocks
    events_early = events * 5 // 8

    def row_tile(t, carry):
        kb = t // n
        j = lax.rem(t, n)

        @pl.when(t + 1 < tiles)
        def _():
            a_copy(t + 1).start()

        @pl.when(j == 0)
        def _():
            @pl.when(kb >= blocks)
            def _():
                u_remote(kb // blocks, lax.rem(kb, blocks)).wait_recv()

            owner = [upper_owner(kb, j) for j in range(SLOTS)]
            for j in range(SLOTS):
                real = uslots[kb, j, 0].astype(jnp.float32)
                imag = uslots[kb, j, 1].astype(jnp.float32)
                for i, value in enumerate((weights[1] * real + weights[0] * imag, weights[0] * real - weights[1] * imag)):
                    turned = jnp.transpose(value)
                    for s in range(supers):
                        span = slice(s * width, (s + 1) * width)
                        lanes = slice(i * unit, (i + 1) * unit)
                        kept = jnp.where(owner[j] == s, turned, 0.0)
                        high = kept.astype(jnp.bfloat16)
                        low = (kept - high.astype(jnp.float32)).astype(jnp.bfloat16)
                        down = slice(wide + s * width, wide + (s + 1) * width)
                        if j == 0:
                            lhs[span, lanes] = high
                            lhs[down, lanes] = low
                        else:
                            lhs[span, lanes] = jnp.where(owner[j] == s, high, lhs[span, lanes])
                            lhs[down, lanes] = jnp.where(owner[j] == s, low, lhs[down, lanes])

        a_copy(t).wait()
        slot = lax.rem(t, 2)
        total = jnp.dot(lhs[...], abuf[slot].reshape(2 * unit, tile), preferred_element_type=jnp.float32)
        for q in range(2):
            lanes = slice(q * half, (q + 1) * half)
            before = acc[2 * j + q]
            acc[2 * j + q] = total[:wide, lanes] + total[wide:, lanes] + jnp.where(kb == 0, jnp.zeros_like(before), before)

        def some(c, carry):
            forward(c)
            return carry

        lax.fori_loop(t * events_early // tiles, (t + 1) * events_early // tiles, some, 0)
        return carry

    lax.fori_loop(0, tiles, row_tile, 0)

    def p_remote(ch):
        return pltpu.make_async_remote_copy(
            src_ref=acc.at[2 * ch + 1 - p], dst_ref=place_of(ch), send_sem=p_send.at[ch], recv_sem=p_recv.at[ch],
            device_id={"pole": 1 - p}, device_id_type=MESH,
        )

    def p_start(i, carry):
        p_remote(i).start()
        return carry

    lax.fori_loop(0, n, p_start, 0)

    for d in range(1, n_col):
        for b in range(blocks):
            u_remote(d, b).wait_send()
    steps = n * blocks
    turning = unit == width and kbs <= steps

    def block_of(q):
        r = q - blocks
        few = jnp.minimum(taken[0], taken[1])
        up = jnp.where(r < 2 * few, lax.rem(r, 2), jnp.where(taken[0] > taken[1], 0, 1))
        c = jnp.where(r < 2 * few, r // 2, r - few)
        c = jnp.maximum(c, 0)
        place = jnp.where(q < blocks, remote_blocks + q, jnp.where(up == 0, c, remote_blocks - 1 - c))
        device = jnp.where(up == 0, z + 1 + c // blocks, z - 1 - c // blocks)
        column = jnp.where(q < blocks, z * blocks + q, device * blocks + lax.rem(c, blocks))
        return place, column, up, c

    def c_copy(v):
        q = v // 2
        _, column, _, _ = block_of(q)
        return pltpu.make_async_copy(
            inverse.at[:, pl.ds(pl.multiple_of(lax.rem(v, 2) * (rows // 2), rows // 2), rows // 2), pl.ds(pl.multiple_of(column * unit, unit), unit)],
            cbuf.at[lax.rem(v, 2)],
            c_sem.at[lax.rem(v, 2)],
        )

    c_copy(0).start()

    def p_add(ch, carry):
        p_remote(ch).wait_recv()
        acc[2 * ch + p] = acc[2 * ch + p] + place_of(ch)[...]
        return carry

    lax.fori_loop(0, n, p_add, 0)

    def q_remote(way, i):
        to = {"row": z + 1 if way == 0 else z - 1}
        return (
            pltpu.make_async_remote_copy(
                src_ref=qstage.at[way, i], dst_ref=qrecv.at[way, i], send_sem=q_send.at[way, i], recv_sem=q_recv.at[way, i],
                device_id=to, device_id_type=MESH,
            ),
            pltpu.make_async_remote_copy(
                src_ref=mstage.at[way, i], dst_ref=mrecv.at[way, i], send_sem=m_send.at[way, i], recv_sem=m_recv.at[way, i],
                device_id=to, device_id_type=MESH,
            ),
        )

    def arrived(way, i):
        for copy in q_remote(way, i):
            copy.wait_recv()
        return unpacked(qrecv[way, i], mrecv[way, i, :1])

    def wave(w):
        for way in range(2):
            i = w - z if way == 0 else w - (n - 1 - z)
            ch = n - 1 - i if way == 0 else i

            @pl.when(jnp.logical_and(i >= 0, z < ch if way == 0 else z > ch))
            def _():
                @pl.when(z > 0 if way == 0 else z < n - 1)
                def _():
                    acc[2 * ch + p] = acc[2 * ch + p] + arrived(way, i)

                code, scale = packed(acc[2 * ch + p])
                qstage[way, i] = code
                mstage[way, i] = jnp.broadcast_to(scale, mstage.shape[2:])
                for copy in q_remote(way, i):
                    copy.start()

    def row_end():
        @pl.when(z > 0)
        def _():
            acc[2 * z + p] = acc[2 * z + p] + arrived(0, n - 1 - z)

        @pl.when(z < n - 1)
        def _():
            acc[2 * z + p] = acc[2 * z + p] + arrived(1, z)

        for s in range(supers):
            row_out[s] = -jnp.transpose(acc[2 * z + p, s * width:(s + 1) * width, :])

    gap = max(1, steps // (n - 1))

    def column_step(q, carry):
        w = q // gap

        @pl.when(jnp.logical_and(lax.rem(q, gap) == 0, w < n - 1))
        def _():
            wave(w)

        e = events_early + q // 2

        @pl.when(jnp.logical_and(lax.rem(q, 2) == 0, e < events))
        def _():
            forward(e)

        place, column, up, c = block_of(q)
        for way in range(2):
            @pl.when(jnp.logical_and(jnp.logical_and(q >= blocks, up == way), c + blocks >= sent[way]))
            def _():
                l_remote(way, c, remote_blocks).wait_recv()

        if turning:
            @pl.when(q < kbs)
            def _():
                for j in range(SLOTS):
                    for c in range(2):
                        uslots[q, j, c] = jnp.transpose(uslots[q, j, c])

        owner = [lower_owner(column, j) for j in range(SLOTS)]
        for s in range(supers):
            real = jnp.zeros((unit, width), jnp.bfloat16)
            imag = jnp.zeros((unit, width), jnp.bfloat16)
            for j in range(SLOTS):
                real = jnp.where(owner[j] == s, lin[place * SLOTS + j, 0], real)
                imag = jnp.where(owner[j] == s, lin[place * SLOTS + j, 1], imag)
            for i, value in enumerate((real, imag, -imag, real)):
                rhs[i // 2 * unit:(i // 2 + 1) * unit, (2 * s + i % 2) * width:(2 * s + i % 2 + 1) * width] = value

        for h in range(2):
            v = 2 * q + h

            @pl.when(v + 1 < 2 * steps)
            def _():
                c_copy(v + 1).start()

            c_copy(v).wait()
            left = jnp.concatenate([cbuf[h, 0], cbuf[h, 1]], axis=1)
            span = slice(h * (rows // 2), (h + 1) * (rows // 2))
            total = jnp.dot(left, rhs[...], preferred_element_type=jnp.float32)
            for s in range(supers):
                before = cacc[s, span]
                cacc[s, span] = total[:, 2 * s * width:2 * (s + 1) * width] + jnp.where(q == 0, jnp.zeros_like(before), before)
        return carry

    lax.fori_loop(0, steps, column_step, 0)


    gcopies = [
        pltpu.make_async_copy(given.at[s, c], given_at(s, c), o_sem.at[2 * s + c]) for s in range(supers) for c in range(2)
    ]
    for copy in gcopies:
        copy.start()
    part = mine.shape[1]

    def writes(s, c):
        lanes = pl.ds(s * width, width)
        return (
            pltpu.make_async_copy(cacc.at[s, pl.ds(pl.multiple_of((2 * c + p) * part, part), part), pl.ds(0, width)], mine.at[c, :, lanes], w_sem.at[0, s, c]),
            pltpu.make_async_copy(cacc.at[s, pl.ds(pl.multiple_of((2 * c + 1 - p) * part, part), part), pl.ds(0, width)], other.at[c, :, lanes], w_sem.at[1, s, c]),
        )

    for copy in gcopies:
        copy.wait()
    origin_flag = jnp.where(jnp.logical_and(z == 0, x == 0), 1.0, 0.0)
    for s in range(supers):
        def mix(i, carry):
            span = pl.ds(pl.multiple_of(i * 2 * part, 2 * part), 2 * part)
            real = cacc[s, span, :width]
            imag = cacc[s, span, width:]
            cacc[s, span, :width] = weights[0] * imag + weights[1] * real
            cacc[s, span, width:] = weights[0] * real - weights[1] * imag
            return carry

        lax.fori_loop(0, n_col, mix, 0)
        for c in range(n_col):
            for copy in writes(s, c):
                copy.start()
        diag[s * width:(s + 1) * width, :] = origin_flag * (
            weights[0] * given_at(s, 1)[...].astype(jnp.float32) + weights[1] * given_at(s, 0)[...].astype(jnp.float32)
        )

    def one(kb, carry):
        start = pl.multiple_of((lax.rem(x - kb // blocks + n_col, n_col) * blocks + lax.rem(kb, blocks)) * unit, unit)
        owner = [upper_owner(kb, j) for j in range(SLOTS)]
        for s in range(supers):
            rights = []
            lefts = []
            for c in range(2):
                value = cacc[s, pl.ds(start, unit), c * width:(c + 1) * width]
                high = value.astype(jnp.bfloat16)
                low = (value - high.astype(jnp.float32)).astype(jnp.bfloat16)
                rights.append(jnp.concatenate([high, low], axis=1))
                chosen = jnp.zeros((unit, width), jnp.bfloat16)
                for j in range(SLOTS):
                    chosen = jnp.where(owner[j] == s, uslots[kb, j, c], chosen)
                lefts.append(chosen if turning else jnp.transpose(chosen))
            total = jnp.dot(
                jnp.concatenate(lefts, axis=1), jnp.concatenate(rights, axis=0), preferred_element_type=jnp.float32
            )
            diag[s * width:(s + 1) * width, :] += total[:, :width] + total[:, width:]
        return carry

    lax.fori_loop(0, kbs, one, 0)
    row_end()

    for s in range(supers):
        for c in range(n_col):
            for copy in writes(s, c):
                copy.wait()

    def finish(i, carry):
        for way in range(2):
            ch = n - 1 - i if way == 0 else i

            @pl.when(z < ch if way == 0 else z > ch)
            def _():
                for copy in q_remote(way, i):
                    copy.wait_send()
        return carry

    lax.fori_loop(0, n - 1, finish, 0)

    def l_finish(c, carry):
        for way in range(2):
            @pl.when(c < sent[way])
            def _():
                l_remote(way, c, remote_blocks).wait_send()
        return carry

    lax.fori_loop(0, remote_blocks, l_finish, 0)

    def p_finish(ch, carry):
        p_remote(ch).wait_send()
        return carry

    lax.fori_loop(0, n, p_finish, 0)


def fused_call(order, weights, inverse, own_l, own_u, given, sizes):
    n, n_col, blocks = sizes
    _, rows, cols = inverse.shape
    _, per, unit, width = own_l.shape
    supers = per // blocks
    wide = supers * width
    kbs = blocks * n_col
    half = cols // n // 2
    part = rows // (2 * n_col)
    dma = pltpu.SemaphoreType.DMA
    shared = unit == width and rows // 2 >= wide and half == 2 * width and n <= supers * (rows // wide)
    scratch = [
        pltpu.VMEM((2 * n, wide, half), jnp.float32),
        pltpu.VMEM((supers, rows, 2 * width), jnp.float32),
        pltpu.VMEM((2 * wide, 2 * unit), jnp.bfloat16),
        pltpu.VMEM((2 * unit, 2 * wide), jnp.bfloat16),
        pltpu.VMEM((2, 2, unit, 2 * half), jnp.bfloat16),
        pltpu.VMEM((2, 2, rows // 2, unit), jnp.bfloat16),
        pltpu.VMEM((kbs, SLOTS, 2, unit, width), jnp.bfloat16),
        pltpu.VMEM((n * blocks * SLOTS, 2, unit, width), jnp.bfloat16),
        pltpu.VMEM((2, n - 1, wide, half), jnp.int16),
        pltpu.VMEM((2, n - 1, wide, half), jnp.int16),
        pltpu.VMEM((2, n - 1, 8, half), jnp.float32),
        pltpu.VMEM((2, n - 1, 8, half), jnp.float32),
        dma((2,)), dma((2,)), dma((kbs,)), dma((kbs,)), dma((max(4, 2 * supers),)),
        dma((2, n * blocks)), dma((n * blocks,)),
        dma((n,)), dma((n,)),
        dma((2, n - 1)), dma((2, n - 1)), dma((2, n - 1)), dma((2, n - 1)),
        dma((2, supers, n_col)),
    ]
    if not shared:
        scratch.append(pltpu.VMEM((n, wide, half), jnp.float32))
        scratch.append(pltpu.VMEM(given.shape, jnp.bfloat16))
    smem = pl.BlockSpec(memory_space=pltpu.SMEM)
    vmem = pl.BlockSpec(memory_space=pltpu.VMEM)
    hbm = pl.BlockSpec(memory_space=pl.ANY)
    return pl.pallas_call(
        functools.partial(fused_kernel, (n, n_col, supers)),
        out_shape=(
            jax.ShapeDtypeStruct((supers, half, width), jnp.float32),
            jax.ShapeDtypeStruct((n_col, part, wide), jnp.float32),
            jax.ShapeDtypeStruct((n_col, part, wide), jnp.float32),
            jax.ShapeDtypeStruct((wide, width), jnp.float32),
        ),
        in_specs=[smem, smem, hbm, hbm, hbm, hbm],
        out_specs=(vmem, hbm, hbm, vmem),
        scratch_shapes=scratch,
        compiler_params=pltpu.CompilerParams(collective_id=3, has_side_effects=True, vmem_limit_bytes=63 * 2**20),
        name="fused",
    )(order, weights, inverse, own_l, own_u, given)


def body(inverse, lower, upper, diag_inverse, weights, pattern):
    n = lax.axis_size("row")
    n_col = lax.axis_size("col")
    n_groups = lax.axis_size("groups")
    _, local, _, supers, width = lower.shape
    inverse = inverse[0]
    unit = min(width, local)
    blocks = local // unit
    weights = weights[0]
    given = diag_inverse[0]
    order, over = scan_call(pattern, n * n_col * local // width, n_groups)

    def flat(factor):
        return jnp.transpose(factor[0], (1, 2, 0, 3)).reshape(2, supers * blocks, unit, width)

    def usual():
        return fused_call(order, weights, inverse, flat(lower), flat(upper), given, (n, n_col, blocks))

    def rare():
        order, full = plan_call(pattern, (n, n_col), unit, width, blocks)
        own_l = jnp.transpose(flat(lower), (1, 0, 2, 3))
        own_u = jnp.transpose(flat(upper), (1, 0, 2, 3)).reshape(supers, blocks, 2, unit, width)
        lall, uall, row = stream_call(order, weights, inverse, own_l, own_u, (n, n_col))
        row = jnp.transpose(row.reshape(supers, width, -1), (0, 2, 1))
        return (row,) + tuple(column_call(full, weights, inverse, lall, uall, given, (n_col, supers, blocks)))

    row, mine, other, diag = lax.cond(over[0] <= 0, usual, rare)
    column, diagonal = close_call(mine, other, diag, n, n_col)
    return (jnp.transpose(column, (1, 0, 2)), jnp.transpose(row, (1, 0, 2)), diagonal.reshape(supers, width, width))


def solution(mesh):
    return jax.shard_map(
        body,
        mesh=mesh,
        in_specs=(
            P(("groups", "pole"), None, "row", "col"),
            P(("groups", "pole"), ("col", "row"), None, None, None),
            P(("groups", "pole"), ("row", "col"), None, None, None),
            P(("groups", "pole"), None, None, None, None),
            P(("groups", "pole"), None),
            P("groups", None),
        ),
        out_specs=(
            P(("groups", "row", "col", "pole"), None, None),
            P(("groups", "col", "row", "pole"), None, None),
            P("groups", None, None),
        ),
        check_vma=False,
    )
```

```python
import functools
import math

import jax
import jax.numpy as jnp
from jax import lax
from jax.experimental import pallas as pl
from jax.experimental.pallas import tpu as pltpu
from jax.sharding import PartitionSpec as P

MESH = pl.DeviceIdType.MESH
RING = 6
SLOTS = 2
TOP = 32767.0


def full_caps(n, per):
    return [per * d for d in range(n)]


def room(caps):
    n = len(caps)
    return max(caps[z] + caps[n - 1 - z] for z in range(n)) + 1


def stepped(caps, count):
    total = jnp.int32(0)
    for d in range(1, len(caps)):
        total = total + jnp.where(count >= d, caps[d] - caps[d - 1], 0)
    return total


class Streams:
    def __init__(self, caps, first, n, order, lown, lin, stage, send_sem, recv_sem, out_sem, lall):
        self.caps, self.first, self.n = caps, first, n
        self.order, self.lown, self.lin, self.stage = order, lown, lin, stage
        self.send_sem, self.recv_sem, self.out_sem, self.lall = send_sem, recv_sem, out_sem, lall
        self.per = lown.shape[0]
        self.size = lin.shape[0]
        self.z = lax.axis_index("row")
        z = self.z
        self.sent = (jnp.where(z > 0, stepped(caps, n - z), 0), jnp.where(z < n - 1, stepped(caps, z + 1), 0))
        self.taken = (stepped(caps, n - 1 - z), stepped(caps, z))
        self.events = max(caps) - first

    def place(self, way, c):
        return c if way == 0 else self.size - 1 - c

    def remote(self, way, c):
        slot = lax.rem(c, RING)
        place = self.place(way, c)
        return pltpu.make_async_remote_copy(
            src_ref=self.stage.at[way, slot],
            dst_ref=self.lin.at[place],
            send_sem=self.send_sem.at[way, slot],
            recv_sem=self.recv_sem.at[place],
            device_id={"row": self.z - 1 if way == 0 else self.z + 1},
            device_id_type=MESH,
        )

    def kept(self, way, c):
        place = self.place(way, c)
        return pltpu.make_async_copy(self.lin.at[place], self.lall.at[self.per + place], self.out_sem.at[place])

    def begin(self):
        for way in range(2):
            @pl.when(self.sent[way] > 0)
            def _():
                for c in range(self.first):
                    if c >= RING:
                        self.remote(way, c - RING).wait_send()
                    self.stage[way, c % RING] = self.lown[self.order[c]]
                    self.remote(way, c).start()

    def forward(self, d):
        c = d + self.first
        for way in range(2):
            @pl.when(c < self.sent[way])
            def _():
                @pl.when(d < self.taken[way])
                def _():
                    self.remote(way, d).wait_recv()
                    self.kept(way, d).start()

                @pl.when(c >= RING)
                def _():
                    self.remote(way, c - RING).wait_send()

                count = self.order[self.per + way]
                mine = self.lown[self.order[jnp.clip(c - count, 0, self.per - 1)]]
                arrived = self.lin[self.place(way, jnp.clip(d, 0, jnp.maximum(self.taken[way] - 1, 0)))]
                self.stage[way, lax.rem(c, RING)] = jnp.where(d < count, arrived, mine)
                self.remote(way, c).start()

    def drain(self):
        def step(c, carry):
            for way in range(2):
                @pl.when(jnp.logical_and(c < self.taken[way], c + self.first >= self.sent[way]))
                def _():
                    self.remote(way, c).wait_recv()
                    self.kept(way, c).start()

                @pl.when(jnp.logical_and(c < self.sent[way], c + RING >= self.sent[way]))
                def _():
                    self.remote(way, c).wait_send()
            return carry

        lax.fori_loop(0, max(self.caps), step, 0)

        def last(c, carry):
            for way in range(2):
                @pl.when(c < self.taken[way])
                def _():
                    self.kept(way, c).wait()
            return carry

        lax.fori_loop(0, max(self.caps), last, 0)


def greet(targets):
    barrier = pltpu.get_barrier_semaphore()
    total = jnp.int32(0)
    for axis, size, near in targets:
        me = lax.axis_index(axis)
        if near:
            for step in (-1, 1):
                there = jnp.logical_and(me + step >= 0, me + step < size)

                @pl.when(there)
                def _():
                    pl.semaphore_signal(barrier, inc=1, device_id={axis: me + step}, device_id_type=MESH)

                total = total + there.astype(jnp.int32)
        else:
            for d in range(1, size):
                pl.semaphore_signal(barrier, inc=1, device_id={axis: lax.rem(me + d, size)}, device_id_type=MESH)
            total = total + (size - 1)
    pl.semaphore_wait(barrier, total)


def packed(value):
    most = jnp.max(jnp.abs(value), axis=0, keepdims=True)
    factor = jnp.where(most > 0, TOP / jnp.maximum(most, 1e-30), 0.0)
    return jnp.round(value * factor).astype(jnp.int32).astype(jnp.int16), most * (1.0 / TOP)


def unpacked(code, scale):
    return code.astype(jnp.int32).astype(jnp.float32) * scale


def stream_kernel(cfg, order, weights, inverse, own_l, own_u, lall, uall, row_out, *scratch):
    (acc, lhs, abuf, ubuf, lown, lin, stage, prec, qstage, qrecv, mstage, mrecv,
     a_sem, u_send, u_recv, l_sem, s_send, s_recv, s_out, p_send, p_recv, q_send, q_recv, m_send, m_recv) = scratch
    n, n_col, caps = cfg
    per = lown.shape[0]
    supers, kbs, _, unit, width = ubuf.shape
    blocks = kbs // n_col
    half = acc.shape[2]
    tile = 2 * half
    z = lax.axis_index("row")
    x = lax.axis_index("col")
    p = lax.axis_index("pole")

    lcopy = pltpu.make_async_copy(own_l, lown, l_sem.at[0])
    lcopy.start()
    ucopy = pltpu.make_async_copy(own_u, ubuf.at[:, pl.ds(0, blocks)], l_sem.at[1])
    ucopy.start()

    def a_copy(t):
        kb = t // n
        origin = lax.rem(x - kb // blocks + n_col, n_col)
        row = (origin * blocks + lax.rem(kb, blocks)) * unit
        return pltpu.make_async_copy(
            inverse.at[:, pl.ds(pl.multiple_of(row, unit), unit), pl.ds(pl.multiple_of(lax.rem(t, n) * tile, tile), tile)],
            abuf.at[lax.rem(t, 3)],
            a_sem.at[lax.rem(t, 3)],
        )

    a_copy(0).start()
    a_copy(1).start()
    greet((("row", n, True), ("col", n_col, False), ("pole", 2, False)))

    def u_remote(d, b):
        return pltpu.make_async_remote_copy(
            src_ref=own_u.at[:, b],
            dst_ref=ubuf.at[:, d * blocks + b],
            send_sem=u_send.at[d * blocks + b],
            recv_sem=u_recv.at[d * blocks + b],
            device_id={"col": lax.rem(x + d, n_col)},
            device_id_type=MESH,
        )

    for b in range(blocks):
        for d in range(1, n_col):
            u_remote(d, b).start()

    lcopy.wait()
    streams = Streams(caps, blocks, n, order, lown, lin, stage, s_send, s_recv, s_out, lall)
    streams.begin()
    lout = pltpu.make_async_copy(lown, lall.at[pl.ds(0, per)], l_sem.at[0])
    lout.start()
    ucopy.wait()

    tiles = kbs * n
    early = blocks * n
    events = streams.events
    events_early = events * 5 // 18
    events_late = events - events_early
    late = tiles - early

    def due(t):
        if late == 0:
            return t * events // early
        return jnp.where(t < early, t * events_early // early, events_early + (t - early) * events_late // late)

    def row_tile(t, carry):
        kb = t // n
        j = lax.rem(t, n)

        @pl.when(j == 0)
        def _():
            @pl.when(kb >= blocks)
            def _():
                u_remote(kb // blocks, lax.rem(kb, blocks)).wait_recv()

            for s in range(supers):
                kept = order[per + 2 + kb * supers + s] > 0
                real = jnp.where(kept, ubuf[s, kb, 0].astype(jnp.float32), 0.0)
                imag = jnp.where(kept, ubuf[s, kb, 1].astype(jnp.float32), 0.0)
                span = slice(s * width, (s + 1) * width)
                for i, value in enumerate((weights[1] * real + weights[0] * imag, weights[0] * real - weights[1] * imag)):
                    turned = jnp.transpose(value)
                    high = turned.astype(jnp.bfloat16)
                    lhs[0, span, i * unit:(i + 1) * unit] = high
                    lhs[1, span, i * unit:(i + 1) * unit] = (turned - high.astype(jnp.float32)).astype(jnp.bfloat16)

        @pl.when(t + 2 < tiles)
        def _():
            a_copy(t + 2).start()

        a_copy(t).wait()
        slot = lax.rem(t, 3)
        for q in range(2):
            right = abuf[slot, :, :, q * half:(q + 1) * half].reshape(2 * unit, half)
            total = jnp.dot(lhs[0], right, preferred_element_type=jnp.float32) + jnp.dot(
                lhs[1], right, preferred_element_type=jnp.float32
            )
            before = acc[2 * j + q]
            acc[2 * j + q] = total + jnp.where(kb == 0, jnp.zeros_like(before), before)

        now = due(t)

        def some(d, carry):
            streams.forward(d)
            return carry

        lax.fori_loop(now, due(t + 1), some, 0)
        return carry

    lax.fori_loop(0, tiles, row_tile, 0)

    uout = pltpu.make_async_copy(ubuf, uall, l_sem.at[1])
    uout.start()

    def p_remote(ch):
        return pltpu.make_async_remote_copy(
            src_ref=acc.at[2 * ch + 1 - p],
            dst_ref=prec.at[ch],
            send_sem=p_send.at[ch],
            recv_sem=p_recv.at[ch],
            device_id={"pole": 1 - p},
            device_id_type=MESH,
        )

    for i in range((n + 1) // 2):
        p_remote(n - 1 - i).start()
        if i != n - 1 - i:
            p_remote(i).start()

    def q_remote(way, i):
        to = {"row": z + 1 if way == 0 else z - 1}
        return (
            pltpu.make_async_remote_copy(
                src_ref=qstage.at[way, i], dst_ref=qrecv.at[way, i], send_sem=q_send.at[way, i], recv_sem=q_recv.at[way, i],
                device_id=to, device_id_type=MESH,
            ),
            pltpu.make_async_remote_copy(
                src_ref=mstage.at[way, i], dst_ref=mrecv.at[way, i], send_sem=m_send.at[way, i], recv_sem=m_recv.at[way, i],
                device_id=to, device_id_type=MESH,
            ),
        )

    def arrived(way, i):
        for copy in q_remote(way, i):
            copy.wait_recv()
        return unpacked(qrecv[way, i], mrecv[way, i, :1])

    def row_step(i, carry):
        for way in range(2):
            ch = n - 1 - i if way == 0 else i

            @pl.when(z < ch if way == 0 else z > ch)
            def _():
                p_remote(ch).wait_recv()
                acc[2 * ch + p] = acc[2 * ch + p] + prec[ch]

                @pl.when(z > 0 if way == 0 else z < n - 1)
                def _():
                    acc[2 * ch + p] = acc[2 * ch + p] + arrived(way, i)

                code, scale = packed(acc[2 * ch + p])
                qstage[way, i] = code
                mstage[way, i] = jnp.broadcast_to(scale, mstage.shape[2:])
                for copy in q_remote(way, i):
                    copy.start()
        return carry

    lax.fori_loop(0, n - 1, row_step, 0)

    p_remote(z).wait_recv()
    row_out[...] = acc[2 * z + p] + prec[z]

    @pl.when(z > 0)
    def _():
        row_out[...] = row_out[...] + arrived(0, n - 1 - z)

    @pl.when(z < n - 1)
    def _():
        row_out[...] = row_out[...] + arrived(1, z)

    row_out[...] = -row_out[...]
    streams.drain()

    def finish(i, carry):
        for way in range(2):
            ch = n - 1 - i if way == 0 else i

            @pl.when(z < ch if way == 0 else z > ch)
            def _():
                for copy in q_remote(way, i):
                    copy.wait_send()
        return carry

    lax.fori_loop(0, n - 1, finish, 0)
    for ch in range(n):
        p_remote(ch).wait_send()
    for d in range(1, n_col):
        for b in range(blocks):
            u_remote(d, b).wait_send()
    lout.wait()
    uout.wait()


def stream_call(order, weights, inverse, own_l, own_u, sizes):
    n, n_col = sizes
    _, rows, cols = inverse.shape
    per, _, unit, width = own_l.shape
    supers, blocks = own_u.shape[:2]
    wide = supers * width
    caps = full_caps(n, per)
    kbs = blocks * n_col
    half = cols // n // 2
    space = room(caps)
    dma = pltpu.SemaphoreType.DMA
    scratch = [
        pltpu.VMEM((2 * n, wide, half), jnp.float32),
        pltpu.VMEM((2, wide, 2 * unit), jnp.bfloat16),
        pltpu.VMEM((3, 2, unit, 2 * half), jnp.bfloat16),
        pltpu.VMEM((supers, kbs, 2, unit, width), jnp.bfloat16),
        pltpu.VMEM((per, 2, unit, width), jnp.bfloat16),
        pltpu.VMEM((space, 2, unit, width), jnp.bfloat16),
        pltpu.VMEM((2, RING, 2, unit, width), jnp.bfloat16),
        pltpu.VMEM((n, wide, half), jnp.float32),
        pltpu.VMEM((2, n - 1, wide, half), jnp.int16),
        pltpu.VMEM((2, n - 1, wide, half), jnp.int16),
        pltpu.VMEM((2, n - 1, 8, half), jnp.float32),
        pltpu.VMEM((2, n - 1, 8, half), jnp.float32),
        dma((3,)), dma((kbs,)), dma((kbs,)), dma((2,)),
        dma((2, RING)), dma((space,)), dma((space,)),
        dma((n,)), dma((n,)),
        dma((2, n - 1)), dma((2, n - 1)), dma((2, n - 1)), dma((2, n - 1)),
    ]
    smem = pl.BlockSpec(memory_space=pltpu.SMEM)
    vmem = pl.BlockSpec(memory_space=pltpu.VMEM)
    hbm = pl.BlockSpec(memory_space=pl.ANY)
    return pl.pallas_call(
        functools.partial(stream_kernel, (n, n_col, caps)),
        out_shape=(
            jax.ShapeDtypeStruct((per + space, 2, unit, width), jnp.bfloat16),
            jax.ShapeDtypeStruct((supers, kbs, 2, unit, width), jnp.bfloat16),
            jax.ShapeDtypeStruct((wide, half), jnp.float32),
        ),
        in_specs=[smem, smem, hbm, hbm, hbm],
        out_specs=(hbm, hbm, vmem),
        scratch_shapes=scratch,
        compiler_params=pltpu.CompilerParams(collective_id=0, has_side_effects=True, vmem_limit_bytes=62 * 2**20),
        name="streams",
    )(order, weights, inverse, own_l, own_u)


def column_kernel(cfg, meta, weights, a_ref, *rest):
    supers, n_col, blocks = cfg
    l_refs = rest[:supers]
    u_ref, given, mine, other, diag, acc = rest[supers:]
    k = pl.program_id(0)
    steps = pl.num_programs(0)
    _, rows, double = acc.shape
    width = double // 2
    unit = a_ref.shape[2]
    base = 2 * supers * steps
    piece = rows

    @pl.when(k == 0)
    def _():
        acc[...] = jnp.zeros_like(acc)

    for s in range(supers):
        @pl.when(meta[k * supers + s] > 0)
        def _():
            real = l_refs[s][0, 0]
            imag = l_refs[s][0, 1]
            right = jnp.concatenate([jnp.concatenate([real, imag], axis=1), jnp.concatenate([-imag, real], axis=1)], axis=0)

            def part(i, carry):
                span = pl.ds(pl.multiple_of(i * piece, piece), piece)
                left = jnp.concatenate([a_ref[0, span], a_ref[1, span]], axis=1)
                acc[s, span] += jnp.dot(left, right, preferred_element_type=jnp.float32)
                return carry

            lax.fori_loop(0, rows // piece, part, 0)

    @pl.when(k == steps - 1)
    def _():
        part = mine.shape[1]
        pole = meta[base]
        for s in range(supers):
            lanes = slice(s * width, (s + 1) * width)
            for c in range(n_col):
                for q in range(2):
                    span = pl.ds((2 * c + q) * part, part)
                    real = acc[s, span, :width]
                    imag = acc[s, span, width:]
                    mixed = weights[0] * imag + weights[1] * real
                    acc[s, span, :width] = mixed
                    acc[s, span, width:] = weights[0] * real - weights[1] * imag

                    @pl.when(pole == q)
                    def _():
                        mine[c, :, lanes] = mixed

                    @pl.when(pole != q)
                    def _():
                        other[c, :, lanes] = mixed

            @pl.when(meta[base + 1] > 0)
            def _():
                diag[lanes, :] = weights[0] * given[s, 1].astype(jnp.float32) + weights[1] * given[s, 0].astype(jnp.float32)

            @pl.when(meta[base + 1] == 0)
            def _():
                diag[lanes, :] = jnp.zeros((width, diag.shape[1]), jnp.float32)

        def one(kb, carry):
            for s in range(supers):
                lanes = slice(s * width, (s + 1) * width)

                @pl.when(meta[base + 2 + n_col + kb * supers + s] > 0)
                def _():
                    start = pl.multiple_of(meta[base + 2 + kb // blocks] + lax.rem(kb, blocks) * unit, unit)
                    total = jnp.zeros((width, width), jnp.float32)
                    for c in range(2):
                        value = acc[s, pl.ds(start, unit), c * width:(c + 1) * width]
                        high = value.astype(jnp.bfloat16)
                        low = (value - high.astype(jnp.float32)).astype(jnp.bfloat16)
                        turned = jnp.transpose(u_ref[s, kb, c])
                        total += jnp.dot(turned, high, preferred_element_type=jnp.float32) + jnp.dot(
                            turned, low, preferred_element_type=jnp.float32
                        )
                    diag[lanes, :] += total
            return carry

        lax.fori_loop(0, u_ref.shape[1], one, 0)


def column_call(meta, weights, inverse, lall, uall, given, sizes):
    n_col, supers, blocks = sizes
    _, rows, cols = inverse.shape
    _, _, unit, width = lall.shape
    steps = cols // unit
    part = rows // (2 * n_col)

    def slot(s):
        return lambda k, meta: (meta[supers * steps + k * supers + s], 0, 0, 0)

    whole = pl.BlockSpec(uall.shape, lambda k, meta: (0, 0, 0, 0, 0))
    out = pl.BlockSpec((n_col, part, supers * width), lambda k, meta: (0, 0, 0))
    return pl.pallas_call(
        functools.partial(column_kernel, (supers, n_col, blocks)),
        out_shape=(
            jax.ShapeDtypeStruct((n_col, part, supers * width), jnp.float32),
            jax.ShapeDtypeStruct((n_col, part, supers * width), jnp.float32),
            jax.ShapeDtypeStruct((supers * width, width), jnp.float32),
        ),
        grid_spec=pltpu.PrefetchScalarGridSpec(
            num_scalar_prefetch=1,
            grid=(steps,),
            in_specs=[
                pl.BlockSpec(memory_space=pltpu.SMEM),
                pl.BlockSpec((2, rows, unit), lambda k, meta: (0, 0, k)),
            ]
            + [pl.BlockSpec((1, 2, unit, width), slot(s)) for s in range(supers)]
            + [whole, pl.BlockSpec(given.shape, lambda k, meta: (0, 0, 0, 0))],
            out_specs=(out, out, pl.BlockSpec((supers * width, width), lambda k, meta: (0, 0))),
            scratch_shapes=[pltpu.VMEM((supers, rows, 2 * width), jnp.float32)],
        ),
        compiler_params=pltpu.CompilerParams(vmem_limit_bytes=60 * 2**20),
        name="columns",
    )(meta, weights, inverse, *([lall] * supers), uall, given)


def close_kernel(cfg, mine, other, diag, row, column, total, row_out, *scratch):
    (here, prec, qstage, qrecv, mstage, mrecv, dpole, dvalue, xcode, xscale, zcode, zscale, zin, zinscale, gcode, gscale,
     r_sem, h_sem, p_send, p_recv, q_send, q_recv, m_send, m_recv, dp_send, dp_recv, x_send, x_recv, xs_send, xs_recv,
     z_send, z_recv, zs_send, zs_recv, g_send, g_recv, gs_send, gs_recv, gp_send, gp_recv) = scratch
    n, n_col = cfg
    z = lax.axis_index("row")
    x = lax.axis_index("col")
    p = lax.axis_index("pole")
    high = diag.shape[0] // 2
    slab = high // n
    supers, _, width = column.shape

    def remote(src, dst, send, recv, to):
        return pltpu.make_async_remote_copy(
            src_ref=src, dst_ref=dst, send_sem=send, recv_sem=recv, device_id=to, device_id_type=MESH
        )

    def lanes(s):
        return pl.ds(s * width, width)

    def p_remote(d, s):
        return remote(other.at[lax.rem(x + d, n_col), :, lanes(s)], prec.at[d, s], p_send.at[d, s], p_recv.at[d, s], {"pole": 1 - p})

    def h_copy(d, s):
        return pltpu.make_async_copy(mine.at[lax.rem(x + d, n_col), :, lanes(s)], here.at[d, s], h_sem.at[d, s])

    def dp_remote():
        return remote(diag.at[pl.ds(pl.multiple_of((1 - p) * high, 8), high)], dpole, dp_send.at[0], dp_recv.at[0], {"pole": 1 - p})

    def x_remote(d):
        to = {"col": lax.rem(x + d, n_col)}
        return (
            remote(xcode.at[0], xcode.at[d], x_send.at[d], x_recv.at[d], to),
            remote(xscale.at[0], xscale.at[d], xs_send.at[d], xs_recv.at[d], to),
        )

    def q_remote(d, s):
        to = {"col": lax.rem(x + d, n_col)}
        return (
            remote(qstage.at[d, s], qrecv.at[d, s], q_send.at[d, s], q_recv.at[d, s], to),
            remote(mstage.at[d, s], mrecv.at[d, s], m_send.at[d, s], m_recv.at[d, s], to),
        )

    def z_remote(d):
        to = {"row": lax.rem(z + d, n)}
        return (
            remote(zcode.at[d], zin.at[d], z_send.at[d], z_recv.at[d], to),
            remote(zscale.at[d], zinscale.at[d], zs_send.at[d], zs_recv.at[d], to),
        )

    def g_remote(d):
        to = {"row": lax.rem(z + d, n)}
        return (
            remote(gcode.at[0], gcode.at[d], g_send.at[d], g_recv.at[d], to),
            remote(gscale.at[0], gscale.at[d], gs_send.at[d], gs_recv.at[d], to),
        )

    def rows_of(place):
        return pl.ds(pl.multiple_of(p * high + place * slab, 8), slab)

    def gp_remote():
        span = pl.ds(pl.multiple_of(p * high, 8), high)
        return remote(total.at[span], total.at[span], gp_send.at[0], gp_recv.at[0], {"pole": 1 - p})

    def put(code_ref, scale_ref, d, value):
        code, scale = packed(value)
        code_ref[d] = code
        scale_ref[d] = jnp.broadcast_to(scale, (8, width))

    def get(code_ref, scale_ref, d):
        return unpacked(code_ref[d], scale_ref[d, :1])

    others = range(1, n_col)
    r_copy = pltpu.make_async_copy(row, row_out, r_sem.at[0])
    for s in range(supers):
        for d in range(n_col):
            h_copy(d, s).start()
    greet((("row", n, False), ("col", n_col, False), ("pole", 2, False)))
    dp_remote().start()
    for s in range(supers):
        for d in others:
            p_remote(d, s).start()
    for s in range(supers):
        p_remote(0, s).start()
    r_copy.start()

    dp_remote().wait_recv()
    dvalue[...] = diag[pl.ds(pl.multiple_of(p * high, 8), high)] + dpole[...]
    for d in range(1, n):
        to = lax.rem(z + d, n)
        put(zcode, zscale, d, dvalue[pl.ds(pl.multiple_of(to * slab, 8), slab)])
        for copy in z_remote(d):
            copy.start()

    def send(s):
        for d in others:
            p_remote(d, s).wait_recv()
            h_copy(d, s).wait()
            put(qstage, mstage, (d, s), here[d, s] + prec[d, s])
            for copy in q_remote(d, s):
                copy.start()

    send(0)
    value = dvalue[pl.ds(pl.multiple_of(z * slab, 8), slab)]
    for d in range(1, n):
        for copy in z_remote(d):
            copy.wait_recv()
        value = value + get(zin, zinscale, d)
    put(xcode, xscale, 0, value)
    for d in others:
        for copy in x_remote(d):
            copy.start()
    for s in range(1, supers):
        send(s)
    for s in range(supers):
        p_remote(0, s).wait_recv()
        h_copy(0, s).wait()
        column[s] = -(here[0, s] + prec[0, s])
    for d in others:
        for copy in x_remote(d):
            copy.wait_recv()
    value = jnp.zeros((slab, width), jnp.float32)
    for origin in range(n_col):
        value = value + get(xcode, xscale, lax.rem(x - origin + n_col, n_col))
    put(gcode, gscale, 0, value)
    for d in range(1, n):
        for copy in g_remote(d):
            copy.start()
    total[rows_of(z)] = get(gcode, gscale, 0)
    for d in range(1, n):
        for copy in g_remote(d):
            copy.wait_recv()
        total[rows_of(lax.rem(z - d + n, n))] = get(gcode, gscale, d)
    gp_remote().start()

    for s in range(supers):
        for d in others:
            for copy in q_remote(d, s):
                copy.wait_recv()
            column[s] = column[s] - unpacked(qrecv[d, s], mrecv[d, s, :1])

    gp_remote().wait_send()
    span = pl.ds(pl.multiple_of((1 - p) * high, 8), high)
    remote(total.at[span], total.at[span], gp_send.at[0], gp_recv.at[0], {"pole": 1 - p}).wait_recv()
    dp_remote().wait_send()
    for s in range(supers):
        for d in range(n_col):
            p_remote(d, s).wait_send()
    for d in range(1, n):
        for copy in z_remote(d) + g_remote(d):
            copy.wait_send()
    for d in others:
        for copy in x_remote(d):
            copy.wait_send()
        for s in range(supers):
            for copy in q_remote(d, s):
                copy.wait_send()
    r_copy.wait()


def close_call(mine, other, diag, row, n, n_col):
    _, part, wide = mine.shape
    tall, width = diag.shape
    supers = wide // width
    high = tall // 2
    slab = high // n
    dma = pltpu.SemaphoreType.DMA
    vmem = pl.BlockSpec(memory_space=pltpu.VMEM)
    hbm = pl.BlockSpec(memory_space=pl.ANY)
    return pl.pallas_call(
        functools.partial(close_kernel, (n, n_col)),
        out_shape=(
            jax.ShapeDtypeStruct((supers, part, width), jnp.float32),
            jax.ShapeDtypeStruct((tall, width), jnp.float32),
            jax.ShapeDtypeStruct(row.shape, jnp.float32),
        ),
        in_specs=[hbm, hbm, vmem, hbm],
        out_specs=(vmem, vmem, vmem),
        scratch_shapes=[
            pltpu.VMEM((n_col, supers, part, width), jnp.float32),
            pltpu.VMEM((n_col, supers, part, width), jnp.float32),
            pltpu.VMEM((n_col, supers, part, width), jnp.int16),
            pltpu.VMEM((n_col, supers, part, width), jnp.int16),
            pltpu.VMEM((n_col, supers, 8, width), jnp.float32),
            pltpu.VMEM((n_col, supers, 8, width), jnp.float32),
            pltpu.VMEM((high, width), jnp.float32),
            pltpu.VMEM((high, width), jnp.float32),
            pltpu.VMEM((n_col, slab, width), jnp.int16),
            pltpu.VMEM((n_col, 8, width), jnp.float32),
            pltpu.VMEM((n, slab, width), jnp.int16),
            pltpu.VMEM((n, 8, width), jnp.float32),
            pltpu.VMEM((n, slab, width), jnp.int16),
            pltpu.VMEM((n, 8, width), jnp.float32),
            pltpu.VMEM((n, slab, width), jnp.int16),
            pltpu.VMEM((n, 8, width), jnp.float32),
            dma((1,)), *[dma((n_col, supers)) for _ in range(7)],
            dma((1,)), dma((1,)), dma((n_col,)), dma((n_col,)), dma((n_col,)), dma((n_col,)),
            dma((n,)), dma((n,)), dma((n,)), dma((n,)), dma((n,)), dma((n,)), dma((n,)), dma((n,)), dma((1,)), dma((1,)),
        ],
        compiler_params=pltpu.CompilerParams(collective_id=2, has_side_effects=True, vmem_limit_bytes=40 * 2**20),
        name="close",
    )(mine, other, diag, row)


def plan_kernel(cfg, pattern, order, full, keep, count):
    n, n_col, blocks, unit, width = cfg
    supers, entries = pattern.shape
    z = lax.axis_index("row")
    x = lax.axis_index("col")
    p = lax.axis_index("pole")
    per = supers * blocks
    units = n * n_col * blocks
    steps = n * blocks
    split = width // unit

    def clear(i, carry):
        keep[i] = 0
        return carry

    lax.fori_loop(0, supers * units, clear, 0)

    def mark(i, carry):
        s = i // entries
        at = s * units + pattern[s, lax.rem(i, entries)] * split
        for r in range(split):
            keep[at + r] = 1
        return carry

    lax.fori_loop(0, supers * entries, mark, 0)

    def number(i, carry):
        total = jnp.int32(0)
        for s in range(supers):
            for b in range(blocks):
                total = total + keep[s * units + i * blocks + b]
        count[i] = total
        return carry

    lax.fori_loop(0, n * n_col, number, 0)

    def pack(r, rank):
        s = r // blocks
        k = keep[s * units + (x * n + z) * blocks + lax.rem(r, blocks)]
        order[r] = 0

        @pl.when(k > 0)
        def _():
            order[rank] = r

        return rank + k

    lax.fori_loop(0, per, pack, jnp.int32(0))

    def around(i, sums):
        k = count[x * n + i]
        return sums[0] + jnp.where(i > z, k, 0), sums[1] + jnp.where(i < z, k, 0)

    above, below = lax.fori_loop(0, n, around, (jnp.int32(0), jnp.int32(0)))
    order[per] = above
    order[per + 1] = below

    base = 2 * supers * steps
    full[base] = p
    full[base + 1] = jnp.logical_and(z == 0, x == 0).astype(jnp.int32)
    for d in range(n_col):
        full[base + 2 + d] = lax.rem(x - d + n_col, n_col) * blocks * unit

    def rows(i, carry):
        kb = i // supers
        origin = lax.rem(x - kb // blocks + n_col, n_col)
        k = keep[lax.rem(i, supers) * units + (z * n_col + origin) * blocks + lax.rem(kb, blocks)]
        order[per + 2 + i] = k
        full[base + 2 + n_col + i] = k
        return carry

    lax.fori_loop(0, n_col * blocks * supers, rows, 0)

    def device(at, before):
        here = count[x * n + at]
        after = jnp.int32(0)
        for i in range(n):
            after = after + jnp.where(i > at, count[x * n + i], 0)

        def pair(r, rank):
            s = r // blocks
            b = lax.rem(r, blocks)
            k = keep[s * units + (x * n + at) * blocks + b]
            down = blocks * (at - z - 1) + rank + jnp.where(rank < blocks, 0, after)
            up = blocks * (z - 1 - at) + rank + jnp.where(rank < blocks, 0, before)
            to = (at * blocks + b) * supers + s
            place = jnp.where(at == z, r, jnp.where(at > z, per + down, per + room(full_caps(n, per)) - 1 - up))
            full[to] = k
            full[supers * steps + to] = jnp.where(k > 0, place, 0)
            return rank + k

        lax.fori_loop(0, per, pair, jnp.int32(0))
        return before + here

    lax.fori_loop(0, n, device, jnp.int32(0))


def plan_call(pattern, sizes, unit, width, blocks):
    n, n_col = sizes
    supers, _ = pattern.shape
    per = supers * blocks
    table = 2 * supers * n * blocks + 2 + n_col + n_col * blocks * supers
    smem = pl.BlockSpec(memory_space=pltpu.SMEM)
    return pl.pallas_call(
        functools.partial(plan_kernel, (n, n_col, blocks, unit, width)),
        out_shape=(
            jax.ShapeDtypeStruct((per + 2 + n_col * blocks * supers,), jnp.int32),
            jax.ShapeDtypeStruct((table,), jnp.int32),
        ),
        in_specs=[smem],
        out_specs=(smem, smem),
        scratch_shapes=[pltpu.SMEM((supers * n * n_col * blocks,), jnp.int32), pltpu.SMEM((n * n_col,), jnp.int32)],
        name="plan",
    )(pattern)


def scan_kernel(cfg, pattern, order, over, flags, send, recv):
    n_groups, = cfg
    supers, entries = pattern.shape
    g = lax.axis_index("groups")
    lane = lax.broadcasted_iota(jnp.int32, order.shape, 1)
    row = lax.broadcasted_iota(jnp.int32, order.shape, 0)
    rank = jnp.zeros(order.shape, jnp.int32)
    table = jnp.full(order.shape, -1, jnp.int32)
    for s in range(supers):
        hit = jnp.zeros(order.shape, jnp.int32)
        for j in range(entries):
            hit = jnp.where(lane == pattern[s, j], 1, hit)
        table = jnp.where(jnp.where(row == rank, hit, 0) > 0, s, table)
        rank = rank + hit
    order[...] = table
    bad = jnp.max(jnp.where(rank > SLOTS, 1.0, 0.0))
    flags[0] = jnp.full(flags.shape[1:], bad, jnp.float32)

    def copy(d):
        return pltpu.make_async_remote_copy(
            src_ref=flags.at[0], dst_ref=flags.at[d], send_sem=send.at[d], recv_sem=recv.at[d],
            device_id={"groups": lax.rem(g + d, n_groups)}, device_id_type=MESH,
        )

    greet((("groups", n_groups, False),))
    for d in range(1, n_groups):
        copy(d).start()
    for d in range(1, n_groups):
        copy(d).wait_send()
        copy(d).wait_recv()
    over[0] = jnp.max(flags[...])


def scan_call(pattern, owners, n_groups):
    smem = pl.BlockSpec(memory_space=pltpu.SMEM)
    dma = pltpu.SemaphoreType.DMA
    return pl.pallas_call(
        functools.partial(scan_kernel, (n_groups,)),
        out_shape=(
            jax.ShapeDtypeStruct((8, -(-owners // 128) * 128), jnp.int32),
            jax.ShapeDtypeStruct((1,), jnp.float32),
        ),
        in_specs=[smem],
        out_specs=(pl.BlockSpec(memory_space=pltpu.VMEM), smem),
        scratch_shapes=[pltpu.VMEM((n_groups, 8, 128), jnp.float32), dma((n_groups,)), dma((n_groups,))],
        compiler_params=pltpu.CompilerParams(collective_id=1, has_side_effects=True),
        name="scan",
    )(pattern)


def fused_kernel(cfg, order, weights, inverse, own_l, own_u, given, row_out, mine, other, diag, *scratch):
    (acc, cacc, lhs, rhs, abuf, cbuf, uslots, lin, qstage, qrecv, mstage, mrecv,
     a_sem, c_sem, u_send, u_recv, o_sem, l_send, l_recv, p_send, p_recv, q_send, q_recv, m_send, m_recv, w_sem) = scratch[:26]
    n, n_col, supers = cfg
    z = lax.axis_index("row")
    x = lax.axis_index("col")
    p = lax.axis_index("pole")
    kbs, _, _, unit, width = uslots.shape
    blocks = kbs // n_col
    remote_blocks = (n - 1) * blocks
    half = acc.shape[2]
    tile = 2 * half
    rows = cacc.shape[1]
    apart = len(scratch) > 26
    prec = scratch[26] if apart else cacc

    def given_at(s, c):
        return scratch[27].at[s, c] if apart else cbuf.at[0, c, pl.ds(s * width, width)]

    wide = supers * width

    def lower_owner(k, j):
        return order[j, (x * n * blocks + k) * unit // width]

    def upper_owner(kb, j):
        origin = lax.rem(x - kb // blocks + n_col, n_col)
        return order[j, ((z * n_col + origin) * blocks + lax.rem(kb, blocks)) * unit // width]

    def place_of(ch):
        if not apart:
            fit = rows // wide
            return cacc.at[ch // fit, pl.ds(pl.multiple_of(lax.rem(ch, fit) * wide, wide), wide)]
        return prec.at[ch]

    def a_copy(t):
        kb = t // n
        origin = lax.rem(x - kb // blocks + n_col, n_col)
        row = (origin * blocks + lax.rem(kb, blocks)) * unit
        return pltpu.make_async_copy(
            inverse.at[:, pl.ds(pl.multiple_of(row, unit), unit), pl.ds(pl.multiple_of(lax.rem(t, n) * tile, tile), tile)],
            abuf.at[lax.rem(t, 2)],
            a_sem.at[lax.rem(t, 2)],
        )

    per = supers * blocks
    own = [
        pltpu.make_async_copy(source.at[c], lin.at[pl.ds(i * per, per), c], o_sem.at[2 * i + c])
        for i, source in enumerate((own_l, own_u))
        for c in range(2)
    ]
    for copy in own:
        copy.start()
    a_copy(0).start()
    for copy in own:
        copy.wait()
    for b in range(blocks):
        for j in range(SLOTS):
            chosen = jnp.maximum(lower_owner(z * blocks + b, j), 0)
            lin[(remote_blocks + b) * SLOTS + j] = lin[chosen * blocks + b]
            chosen = jnp.maximum(upper_owner(b, j), 0)
            uslots[b, j] = lin[per + chosen * blocks + b]
    greet((("row", n, True), ("col", n_col, False), ("pole", 2, False)))

    def u_remote(d, b):
        return pltpu.make_async_remote_copy(
            src_ref=uslots.at[b], dst_ref=uslots.at[d * blocks + b],
            send_sem=u_send.at[d * blocks + b], recv_sem=u_recv.at[d * blocks + b],
            device_id={"col": lax.rem(x + d, n_col)}, device_id_type=MESH,
        )

    sent = (jnp.where(z > 0, (n - z) * blocks, 0), jnp.where(z < n - 1, (z + 1) * blocks, 0))
    taken = ((n - 1 - z) * blocks, z * blocks)

    def l_place(way, c):
        return c if way == 0 else remote_blocks - 1 - c

    def l_remote(way, c, source):
        return pltpu.make_async_remote_copy(
            src_ref=lin.at[pl.ds(source * SLOTS, SLOTS)], dst_ref=lin.at[pl.ds(l_place(way, c) * SLOTS, SLOTS)],
            send_sem=l_send.at[way, c], recv_sem=l_recv.at[l_place(way, c)],
            device_id={"row": z - 1 if way == 0 else z + 1}, device_id_type=MESH,
        )

    for b in range(blocks):
        for d in range(1, n_col):
            u_remote(d, b).start()
        for way in range(2):
            @pl.when(sent[way] > 0)
            def _():
                l_remote(way, b, remote_blocks + b).start()

    def forward(c):
        for way in range(2):
            @pl.when(c + blocks < sent[way])
            def _():
                l_remote(way, c, l_place(way, c)).wait_recv()
                l_remote(way, c + blocks, l_place(way, c)).start()

    tiles = kbs * n
    events = (n - 2) * blocks
    events_early = events * 5 // 8

    def row_tile(t, carry):
        kb = t // n
        j = lax.rem(t, n)

        @pl.when(t + 1 < tiles)
        def _():
            a_copy(t + 1).start()

        @pl.when(j == 0)
        def _():
            @pl.when(kb >= blocks)
            def _():
                u_remote(kb // blocks, lax.rem(kb, blocks)).wait_recv()

            owner = [upper_owner(kb, j) for j in range(SLOTS)]
            for j in range(SLOTS):
                real = uslots[kb, j, 0].astype(jnp.float32)
                imag = uslots[kb, j, 1].astype(jnp.float32)
                for i, value in enumerate((weights[1] * real + weights[0] * imag, weights[0] * real - weights[1] * imag)):
                    turned = jnp.transpose(value)
                    for s in range(supers):
                        span = slice(s * width, (s + 1) * width)
                        lanes = slice(i * unit, (i + 1) * unit)
                        kept = jnp.where(owner[j] == s, turned, 0.0)
                        high = kept.astype(jnp.bfloat16)
                        low = (kept - high.astype(jnp.float32)).astype(jnp.bfloat16)
                        down = slice(wide + s * width, wide + (s + 1) * width)
                        if j == 0:
                            lhs[span, lanes] = high
                            lhs[down, lanes] = low
                        else:
                            lhs[span, lanes] = jnp.where(owner[j] == s, high, lhs[span, lanes])
                            lhs[down, lanes] = jnp.where(owner[j] == s, low, lhs[down, lanes])

        a_copy(t).wait()
        slot = lax.rem(t, 2)
        total = jnp.dot(lhs[...], abuf[slot].reshape(2 * unit, tile), preferred_element_type=jnp.float32)
        for q in range(2):
            lanes = slice(q * half, (q + 1) * half)
            before = acc[2 * j + q]
            acc[2 * j + q] = total[:wide, lanes] + total[wide:, lanes] + jnp.where(kb == 0, jnp.zeros_like(before), before)

        def some(c, carry):
            forward(c)
            return carry

        lax.fori_loop(t * events_early // tiles, (t + 1) * events_early // tiles, some, 0)
        return carry

    lax.fori_loop(0, tiles, row_tile, 0)

    def p_remote(ch):
        return pltpu.make_async_remote_copy(
            src_ref=acc.at[2 * ch + 1 - p], dst_ref=place_of(ch), send_sem=p_send.at[ch], recv_sem=p_recv.at[ch],
            device_id={"pole": 1 - p}, device_id_type=MESH,
        )

    def p_start(i, carry):
        p_remote(i).start()
        return carry

    lax.fori_loop(0, n, p_start, 0)

    for d in range(1, n_col):
        for b in range(blocks):
            u_remote(d, b).wait_send()
    steps = n * blocks
    turning = unit == width and kbs <= steps

    def block_of(q):
        r = q - blocks
        few = jnp.minimum(taken[0], taken[1])
        up = jnp.where(r < 2 * few, lax.rem(r, 2), jnp.where(taken[0] > taken[1], 0, 1))
        c = jnp.where(r < 2 * few, r // 2, r - few)
        c = jnp.maximum(c, 0)
        place = jnp.where(q < blocks, remote_blocks + q, jnp.where(up == 0, c, remote_blocks - 1 - c))
        device = jnp.where(up == 0, z + 1 + c // blocks, z - 1 - c // blocks)
        column = jnp.where(q < blocks, z * blocks + q, device * blocks + lax.rem(c, blocks))
        return place, column, up, c

    def c_copy(v):
        q = v // 2
        _, column, _, _ = block_of(q)
        return pltpu.make_async_copy(
            inverse.at[:, pl.ds(pl.multiple_of(lax.rem(v, 2) * (rows // 2), rows // 2), rows // 2), pl.ds(pl.multiple_of(column * unit, unit), unit)],
            cbuf.at[lax.rem(v, 2)],
            c_sem.at[lax.rem(v, 2)],
        )

    c_copy(0).start()

    def p_add(ch, carry):
        p_remote(ch).wait_recv()
        acc[2 * ch + p] = acc[2 * ch + p] + place_of(ch)[...]
        return carry

    lax.fori_loop(0, n, p_add, 0)

    def q_remote(way, i):
        to = {"row": z + 1 if way == 0 else z - 1}
        return (
            pltpu.make_async_remote_copy(
                src_ref=qstage.at[way, i], dst_ref=qrecv.at[way, i], send_sem=q_send.at[way, i], recv_sem=q_recv.at[way, i],
                device_id=to, device_id_type=MESH,
            ),
            pltpu.make_async_remote_copy(
                src_ref=mstage.at[way, i], dst_ref=mrecv.at[way, i], send_sem=m_send.at[way, i], recv_sem=m_recv.at[way, i],
                device_id=to, device_id_type=MESH,
            ),
        )

    def arrived(way, i):
        for copy in q_remote(way, i):
            copy.wait_recv()
        return unpacked(qrecv[way, i], mrecv[way, i, :1])

    def wave(w):
        for way in range(2):
            i = w - z if way == 0 else w - (n - 1 - z)
            ch = n - 1 - i if way == 0 else i

            @pl.when(jnp.logical_and(i >= 0, z < ch if way == 0 else z > ch))
            def _():
                @pl.when(z > 0 if way == 0 else z < n - 1)
                def _():
                    acc[2 * ch + p] = acc[2 * ch + p] + arrived(way, i)

                code, scale = packed(acc[2 * ch + p])
                qstage[way, i] = code
                mstage[way, i] = jnp.broadcast_to(scale, mstage.shape[2:])
                for copy in q_remote(way, i):
                    copy.start()

    def row_end():
        @pl.when(z > 0)
        def _():
            acc[2 * z + p] = acc[2 * z + p] + arrived(0, n - 1 - z)

        @pl.when(z < n - 1)
        def _():
            acc[2 * z + p] = acc[2 * z + p] + arrived(1, z)

        for s in range(supers):
            row_out[s] = -jnp.transpose(acc[2 * z + p, s * width:(s + 1) * width, :])

    gap = max(1, steps // (n - 1))

    def column_step(q, carry):
        w = q // gap

        @pl.when(jnp.logical_and(lax.rem(q, gap) == 0, w < n - 1))
        def _():
            wave(w)

        e = events_early + q // 2

        @pl.when(jnp.logical_and(lax.rem(q, 2) == 0, e < events))
        def _():
            forward(e)

        place, column, up, c = block_of(q)
        for way in range(2):
            @pl.when(jnp.logical_and(jnp.logical_and(q >= blocks, up == way), c + blocks >= sent[way]))
            def _():
                l_remote(way, c, remote_blocks).wait_recv()

        if turning:
            @pl.when(q < kbs)
            def _():
                for j in range(SLOTS):
                    for c in range(2):
                        uslots[q, j, c] = jnp.transpose(uslots[q, j, c])

        owner = [lower_owner(column, j) for j in range(SLOTS)]
        for s in range(supers):
            real = jnp.zeros((unit, width), jnp.bfloat16)
            imag = jnp.zeros((unit, width), jnp.bfloat16)
            for j in range(SLOTS):
                real = jnp.where(owner[j] == s, lin[place * SLOTS + j, 0], real)
                imag = jnp.where(owner[j] == s, lin[place * SLOTS + j, 1], imag)
            for i, value in enumerate((real, imag, -imag, real)):
                rhs[i // 2 * unit:(i // 2 + 1) * unit, (2 * s + i % 2) * width:(2 * s + i % 2 + 1) * width] = value

        for h in range(2):
            v = 2 * q + h

            @pl.when(v + 1 < 2 * steps)
            def _():
                c_copy(v + 1).start()

            c_copy(v).wait()
            left = jnp.concatenate([cbuf[h, 0], cbuf[h, 1]], axis=1)
            span = slice(h * (rows // 2), (h + 1) * (rows // 2))
            total = jnp.dot(left, rhs[...], preferred_element_type=jnp.float32)
            for s in range(supers):
                before = cacc[s, span]
                cacc[s, span] = total[:, 2 * s * width:2 * (s + 1) * width] + jnp.where(q == 0, jnp.zeros_like(before), before)
        return carry

    lax.fori_loop(0, steps, column_step, 0)


    gcopies = [
        pltpu.make_async_copy(given.at[s, c], given_at(s, c), o_sem.at[2 * s + c]) for s in range(supers) for c in range(2)
    ]
    for copy in gcopies:
        copy.start()
    part = mine.shape[1]

    def writes(s, c):
        lanes = pl.ds(s * width, width)
        return (
            pltpu.make_async_copy(cacc.at[s, pl.ds(pl.multiple_of((2 * c + p) * part, part), part), pl.ds(0, width)], mine.at[c, :, lanes], w_sem.at[0, s, c]),
            pltpu.make_async_copy(cacc.at[s, pl.ds(pl.multiple_of((2 * c + 1 - p) * part, part), part), pl.ds(0, width)], other.at[c, :, lanes], w_sem.at[1, s, c]),
        )

    for copy in gcopies:
        copy.wait()
    origin_flag = jnp.where(jnp.logical_and(z == 0, x == 0), 1.0, 0.0)
    for s in range(supers):
        def mix(i, carry):
            span = pl.ds(pl.multiple_of(i * 2 * part, 2 * part), 2 * part)
            real = cacc[s, span, :width]
            imag = cacc[s, span, width:]
            cacc[s, span, :width] = weights[0] * imag + weights[1] * real
            cacc[s, span, width:] = weights[0] * real - weights[1] * imag
            return carry

        lax.fori_loop(0, n_col, mix, 0)
        for c in range(n_col):
            for copy in writes(s, c):
                copy.start()
        diag[s * width:(s + 1) * width, :] = origin_flag * (
            weights[0] * given_at(s, 1)[...].astype(jnp.float32) + weights[1] * given_at(s, 0)[...].astype(jnp.float32)
        )

    def one(kb, carry):
        start = pl.multiple_of((lax.rem(x - kb // blocks + n_col, n_col) * blocks + lax.rem(kb, blocks)) * unit, unit)
        owner = [upper_owner(kb, j) for j in range(SLOTS)]
        for s in range(supers):
            rights = []
            lefts = []
            for c in range(2):
                value = cacc[s, pl.ds(start, unit), c * width:(c + 1) * width]
                high = value.astype(jnp.bfloat16)
                low = (value - high.astype(jnp.float32)).astype(jnp.bfloat16)
                rights.append(jnp.concatenate([high, low], axis=1))
                chosen = jnp.zeros((unit, width), jnp.bfloat16)
                for j in range(SLOTS):
                    chosen = jnp.where(owner[j] == s, uslots[kb, j, c], chosen)
                lefts.append(chosen if turning else jnp.transpose(chosen))
            total = jnp.dot(
                jnp.concatenate(lefts, axis=1), jnp.concatenate(rights, axis=0), preferred_element_type=jnp.float32
            )
            diag[s * width:(s + 1) * width, :] += total[:, :width] + total[:, width:]
        return carry

    lax.fori_loop(0, kbs, one, 0)
    row_end()

    for s in range(supers):
        for c in range(n_col):
            for copy in writes(s, c):
                copy.wait()

    def finish(i, carry):
        for way in range(2):
            ch = n - 1 - i if way == 0 else i

            @pl.when(z < ch if way == 0 else z > ch)
            def _():
                for copy in q_remote(way, i):
                    copy.wait_send()
        return carry

    lax.fori_loop(0, n - 1, finish, 0)

    def l_finish(c, carry):
        for way in range(2):
            @pl.when(c < sent[way])
            def _():
                l_remote(way, c, remote_blocks).wait_send()
        return carry

    lax.fori_loop(0, remote_blocks, l_finish, 0)

    def p_finish(ch, carry):
        p_remote(ch).wait_send()
        return carry

    lax.fori_loop(0, n, p_finish, 0)


def fused_call(order, weights, inverse, own_l, own_u, given, sizes):
    n, n_col, blocks = sizes
    _, rows, cols = inverse.shape
    _, per, unit, width = own_l.shape
    supers = per // blocks
    wide = supers * width
    kbs = blocks * n_col
    half = cols // n // 2
    part = rows // (2 * n_col)
    dma = pltpu.SemaphoreType.DMA
    shared = unit == width and rows // 2 >= wide and half == 2 * width and n <= supers * (rows // wide)
    scratch = [
        pltpu.VMEM((2 * n, wide, half), jnp.float32),
        pltpu.VMEM((supers, rows, 2 * width), jnp.float32),
        pltpu.VMEM((2 * wide, 2 * unit), jnp.bfloat16),
        pltpu.VMEM((2 * unit, 2 * wide), jnp.bfloat16),
        pltpu.VMEM((2, 2, unit, 2 * half), jnp.bfloat16),
        pltpu.VMEM((2, 2, rows // 2, unit), jnp.bfloat16),
        pltpu.VMEM((kbs, SLOTS, 2, unit, width), jnp.bfloat16),
        pltpu.VMEM((n * blocks * SLOTS, 2, unit, width), jnp.bfloat16),
        pltpu.VMEM((2, n - 1, wide, half), jnp.int16),
        pltpu.VMEM((2, n - 1, wide, half), jnp.int16),
        pltpu.VMEM((2, n - 1, 8, half), jnp.float32),
        pltpu.VMEM((2, n - 1, 8, half), jnp.float32),
        dma((2,)), dma((2,)), dma((kbs,)), dma((kbs,)), dma((max(4, 2 * supers),)),
        dma((2, n * blocks)), dma((n * blocks,)),
        dma((n,)), dma((n,)),
        dma((2, n - 1)), dma((2, n - 1)), dma((2, n - 1)), dma((2, n - 1)),
        dma((2, supers, n_col)),
    ]
    if not shared:
        scratch.append(pltpu.VMEM((n, wide, half), jnp.float32))
        scratch.append(pltpu.VMEM(given.shape, jnp.bfloat16))
    smem = pl.BlockSpec(memory_space=pltpu.SMEM)
    vmem = pl.BlockSpec(memory_space=pltpu.VMEM)
    hbm = pl.BlockSpec(memory_space=pl.ANY)
    return pl.pallas_call(
        functools.partial(fused_kernel, (n, n_col, supers)),
        out_shape=(
            jax.ShapeDtypeStruct((supers, half, width), jnp.float32),
            jax.ShapeDtypeStruct((n_col, part, wide), jnp.float32),
            jax.ShapeDtypeStruct((n_col, part, wide), jnp.float32),
            jax.ShapeDtypeStruct((wide, width), jnp.float32),
        ),
        in_specs=[smem, smem, hbm, hbm, hbm, hbm],
        out_specs=(vmem, hbm, hbm, vmem),
        scratch_shapes=scratch,
        compiler_params=pltpu.CompilerParams(collective_id=3, has_side_effects=True, vmem_limit_bytes=63 * 2**20),
        name="fused",
    )(order, weights, inverse, own_l, own_u, given)


def body(inverse, lower, upper, diag_inverse, weights, pattern):
    n = lax.axis_size("row")
    n_col = lax.axis_size("col")
    n_groups = lax.axis_size("groups")
    _, local, _, supers, width = lower.shape
    inverse = inverse[0]
    unit = min(width, local)
    blocks = local // unit
    weights = weights[0]
    given = diag_inverse[0]
    order, over = scan_call(pattern, n * n_col * local // width, n_groups)

    def flat(factor):
        return jnp.transpose(factor[0], (1, 2, 0, 3)).reshape(2, supers * blocks, unit, width)

    def usual():
        return fused_call(order, weights, inverse, flat(lower), flat(upper), given, (n, n_col, blocks))

    def rare():
        order, full = plan_call(pattern, (n, n_col), unit, width, blocks)
        own_l = jnp.transpose(flat(lower), (1, 0, 2, 3))
        own_u = jnp.transpose(flat(upper), (1, 0, 2, 3)).reshape(supers, blocks, 2, unit, width)
        lall, uall, row = stream_call(order, weights, inverse, own_l, own_u, (n, n_col))
        row = jnp.transpose(row.reshape(supers, width, -1), (0, 2, 1))
        return (row,) + tuple(column_call(full, weights, inverse, lall, uall, given, (n_col, supers, blocks)))

    row, mine, other, diag = lax.cond(over[0] <= 0, usual, rare)
    column, diagonal, row = close_call(mine, other, diag, row, n, n_col)
    return (jnp.transpose(column, (1, 0, 2)), jnp.transpose(row, (1, 0, 2)), diagonal.reshape(supers, width, width))


def solution(mesh):
    return jax.shard_map(
        body,
        mesh=mesh,
        in_specs=(
            P(("groups", "pole"), None, "row", "col"),
            P(("groups", "pole"), ("col", "row"), None, None, None),
            P(("groups", "pole"), ("row", "col"), None, None, None),
            P(("groups", "pole"), None, None, None, None),
            P(("groups", "pole"), None),
            P("groups", None),
        ),
        out_specs=(
            P(("groups", "row", "col", "pole"), None, None),
            P(("groups", "col", "row", "pole"), None, None),
            P("groups", None, None),
        ),
        check_vma=False,
    )
```

```python
import functools
import math

import jax
import jax.numpy as jnp
from jax import lax
from jax.experimental import pallas as pl
from jax.experimental.pallas import tpu as pltpu
from jax.sharding import PartitionSpec as P

MESH = pl.DeviceIdType.MESH
RING = 6
SLOTS = 2
TOP = 32767.0


def full_caps(n, per):
    return [per * d for d in range(n)]


def room(caps):
    n = len(caps)
    return max(caps[z] + caps[n - 1 - z] for z in range(n)) + 1


def stepped(caps, count):
    total = jnp.int32(0)
    for d in range(1, len(caps)):
        total = total + jnp.where(count >= d, caps[d] - caps[d - 1], 0)
    return total


class Streams:
    def __init__(self, caps, first, n, order, lown, lin, stage, send_sem, recv_sem, out_sem, lall):
        self.caps, self.first, self.n = caps, first, n
        self.order, self.lown, self.lin, self.stage = order, lown, lin, stage
        self.send_sem, self.recv_sem, self.out_sem, self.lall = send_sem, recv_sem, out_sem, lall
        self.per = lown.shape[0]
        self.size = lin.shape[0]
        self.z = lax.axis_index("row")
        z = self.z
        self.sent = (jnp.where(z > 0, stepped(caps, n - z), 0), jnp.where(z < n - 1, stepped(caps, z + 1), 0))
        self.taken = (stepped(caps, n - 1 - z), stepped(caps, z))
        self.events = max(caps) - first

    def place(self, way, c):
        return c if way == 0 else self.size - 1 - c

    def remote(self, way, c):
        slot = lax.rem(c, RING)
        place = self.place(way, c)
        return pltpu.make_async_remote_copy(
            src_ref=self.stage.at[way, slot],
            dst_ref=self.lin.at[place],
            send_sem=self.send_sem.at[way, slot],
            recv_sem=self.recv_sem.at[place],
            device_id={"row": self.z - 1 if way == 0 else self.z + 1},
            device_id_type=MESH,
        )

    def kept(self, way, c):
        place = self.place(way, c)
        return pltpu.make_async_copy(self.lin.at[place], self.lall.at[self.per + place], self.out_sem.at[place])

    def begin(self):
        for way in range(2):
            @pl.when(self.sent[way] > 0)
            def _():
                for c in range(self.first):
                    if c >= RING:
                        self.remote(way, c - RING).wait_send()
                    self.stage[way, c % RING] = self.lown[self.order[c]]
                    self.remote(way, c).start()

    def forward(self, d):
        c = d + self.first
        for way in range(2):
            @pl.when(c < self.sent[way])
            def _():
                @pl.when(d < self.taken[way])
                def _():
                    self.remote(way, d).wait_recv()
                    self.kept(way, d).start()

                @pl.when(c >= RING)
                def _():
                    self.remote(way, c - RING).wait_send()

                count = self.order[self.per + way]
                mine = self.lown[self.order[jnp.clip(c - count, 0, self.per - 1)]]
                arrived = self.lin[self.place(way, jnp.clip(d, 0, jnp.maximum(self.taken[way] - 1, 0)))]
                self.stage[way, lax.rem(c, RING)] = jnp.where(d < count, arrived, mine)
                self.remote(way, c).start()

    def drain(self):
        def step(c, carry):
            for way in range(2):
                @pl.when(jnp.logical_and(c < self.taken[way], c + self.first >= self.sent[way]))
                def _():
                    self.remote(way, c).wait_recv()
                    self.kept(way, c).start()

                @pl.when(jnp.logical_and(c < self.sent[way], c + RING >= self.sent[way]))
                def _():
                    self.remote(way, c).wait_send()
            return carry

        lax.fori_loop(0, max(self.caps), step, 0)

        def last(c, carry):
            for way in range(2):
                @pl.when(c < self.taken[way])
                def _():
                    self.kept(way, c).wait()
            return carry

        lax.fori_loop(0, max(self.caps), last, 0)


def greet(targets):
    barrier = pltpu.get_barrier_semaphore()
    total = jnp.int32(0)
    for axis, size, near in targets:
        me = lax.axis_index(axis)
        if near:
            for step in (-1, 1):
                there = jnp.logical_and(me + step >= 0, me + step < size)

                @pl.when(there)
                def _():
                    pl.semaphore_signal(barrier, inc=1, device_id={axis: me + step}, device_id_type=MESH)

                total = total + there.astype(jnp.int32)
        else:
            for d in range(1, size):
                pl.semaphore_signal(barrier, inc=1, device_id={axis: lax.rem(me + d, size)}, device_id_type=MESH)
            total = total + (size - 1)
    pl.semaphore_wait(barrier, total)


def packed(value):
    most = jnp.max(jnp.abs(value), axis=0, keepdims=True)
    factor = jnp.where(most > 0, TOP / jnp.maximum(most, 1e-30), 0.0)
    return jnp.round(value * factor).astype(jnp.int32).astype(jnp.int16), most * (1.0 / TOP)


def unpacked(code, scale):
    return code.astype(jnp.int32).astype(jnp.float32) * scale


def stream_kernel(cfg, order, weights, inverse, own_l, own_u, lall, uall, row_out, *scratch):
    (acc, lhs, abuf, ubuf, lown, lin, stage, prec, qstage, qrecv, mstage, mrecv,
     a_sem, u_send, u_recv, l_sem, s_send, s_recv, s_out, p_send, p_recv, q_send, q_recv, m_send, m_recv) = scratch
    n, n_col, caps = cfg
    per = lown.shape[0]
    supers, kbs, _, unit, width = ubuf.shape
    blocks = kbs // n_col
    half = acc.shape[2]
    tile = 2 * half
    z = lax.axis_index("row")
    x = lax.axis_index("col")
    p = lax.axis_index("pole")

    lcopy = pltpu.make_async_copy(own_l, lown, l_sem.at[0])
    lcopy.start()
    ucopy = pltpu.make_async_copy(own_u, ubuf.at[:, pl.ds(0, blocks)], l_sem.at[1])
    ucopy.start()

    def a_copy(t):
        kb = t // n
        origin = lax.rem(x - kb // blocks + n_col, n_col)
        row = (origin * blocks + lax.rem(kb, blocks)) * unit
        return pltpu.make_async_copy(
            inverse.at[:, pl.ds(pl.multiple_of(row, unit), unit), pl.ds(pl.multiple_of(lax.rem(t, n) * tile, tile), tile)],
            abuf.at[lax.rem(t, 3)],
            a_sem.at[lax.rem(t, 3)],
        )

    a_copy(0).start()
    a_copy(1).start()
    greet((("row", n, True), ("col", n_col, False), ("pole", 2, False)))

    def u_remote(d, b):
        return pltpu.make_async_remote_copy(
            src_ref=own_u.at[:, b],
            dst_ref=ubuf.at[:, d * blocks + b],
            send_sem=u_send.at[d * blocks + b],
            recv_sem=u_recv.at[d * blocks + b],
            device_id={"col": lax.rem(x + d, n_col)},
            device_id_type=MESH,
        )

    for b in range(blocks):
        for d in range(1, n_col):
            u_remote(d, b).start()

    lcopy.wait()
    streams = Streams(caps, blocks, n, order, lown, lin, stage, s_send, s_recv, s_out, lall)
    streams.begin()
    lout = pltpu.make_async_copy(lown, lall.at[pl.ds(0, per)], l_sem.at[0])
    lout.start()
    ucopy.wait()

    tiles = kbs * n
    early = blocks * n
    events = streams.events
    events_early = events * 5 // 18
    events_late = events - events_early
    late = tiles - early

    def due(t):
        if late == 0:
            return t * events // early
        return jnp.where(t < early, t * events_early // early, events_early + (t - early) * events_late // late)

    def row_tile(t, carry):
        kb = t // n
        j = lax.rem(t, n)

        @pl.when(j == 0)
        def _():
            @pl.when(kb >= blocks)
            def _():
                u_remote(kb // blocks, lax.rem(kb, blocks)).wait_recv()

            for s in range(supers):
                kept = order[per + 2 + kb * supers + s] > 0
                real = jnp.where(kept, ubuf[s, kb, 0].astype(jnp.float32), 0.0)
                imag = jnp.where(kept, ubuf[s, kb, 1].astype(jnp.float32), 0.0)
                span = slice(s * width, (s + 1) * width)
                for i, value in enumerate((weights[1] * real + weights[0] * imag, weights[0] * real - weights[1] * imag)):
                    turned = jnp.transpose(value)
                    high = turned.astype(jnp.bfloat16)
                    lhs[0, span, i * unit:(i + 1) * unit] = high
                    lhs[1, span, i * unit:(i + 1) * unit] = (turned - high.astype(jnp.float32)).astype(jnp.bfloat16)

        @pl.when(t + 2 < tiles)
        def _():
            a_copy(t + 2).start()

        a_copy(t).wait()
        slot = lax.rem(t, 3)
        for q in range(2):
            right = abuf[slot, :, :, q * half:(q + 1) * half].reshape(2 * unit, half)
            total = jnp.dot(lhs[0], right, preferred_element_type=jnp.float32) + jnp.dot(
                lhs[1], right, preferred_element_type=jnp.float32
            )
            before = acc[2 * j + q]
            acc[2 * j + q] = total + jnp.where(kb == 0, jnp.zeros_like(before), before)

        now = due(t)

        def some(d, carry):
            streams.forward(d)
            return carry

        lax.fori_loop(now, due(t + 1), some, 0)
        return carry

    lax.fori_loop(0, tiles, row_tile, 0)

    uout = pltpu.make_async_copy(ubuf, uall, l_sem.at[1])
    uout.start()

    def p_remote(ch):
        return pltpu.make_async_remote_copy(
            src_ref=acc.at[2 * ch + 1 - p],
            dst_ref=prec.at[ch],
            send_sem=p_send.at[ch],
            recv_sem=p_recv.at[ch],
            device_id={"pole": 1 - p},
            device_id_type=MESH,
        )

    for i in range((n + 1) // 2):
        p_remote(n - 1 - i).start()
        if i != n - 1 - i:
            p_remote(i).start()

    def q_remote(way, i):
        to = {"row": z + 1 if way == 0 else z - 1}
        return (
            pltpu.make_async_remote_copy(
                src_ref=qstage.at[way, i], dst_ref=qrecv.at[way, i], send_sem=q_send.at[way, i], recv_sem=q_recv.at[way, i],
                device_id=to, device_id_type=MESH,
            ),
            pltpu.make_async_remote_copy(
                src_ref=mstage.at[way, i], dst_ref=mrecv.at[way, i], send_sem=m_send.at[way, i], recv_sem=m_recv.at[way, i],
                device_id=to, device_id_type=MESH,
            ),
        )

    def arrived(way, i):
        for copy in q_remote(way, i):
            copy.wait_recv()
        return unpacked(qrecv[way, i], mrecv[way, i, :1])

    def row_step(i, carry):
        for way in range(2):
            ch = n - 1 - i if way == 0 else i

            @pl.when(z < ch if way == 0 else z > ch)
            def _():
                p_remote(ch).wait_recv()
                acc[2 * ch + p] = acc[2 * ch + p] + prec[ch]

                @pl.when(z > 0 if way == 0 else z < n - 1)
                def _():
                    acc[2 * ch + p] = acc[2 * ch + p] + arrived(way, i)

                code, scale = packed(acc[2 * ch + p])
                qstage[way, i] = code
                mstage[way, i] = jnp.broadcast_to(scale, mstage.shape[2:])
                for copy in q_remote(way, i):
                    copy.start()
        return carry

    lax.fori_loop(0, n - 1, row_step, 0)

    p_remote(z).wait_recv()
    row_out[...] = acc[2 * z + p] + prec[z]

    @pl.when(z > 0)
    def _():
        row_out[...] = row_out[...] + arrived(0, n - 1 - z)

    @pl.when(z < n - 1)
    def _():
        row_out[...] = row_out[...] + arrived(1, z)

    row_out[...] = -row_out[...]
    streams.drain()

    def finish(i, carry):
        for way in range(2):
            ch = n - 1 - i if way == 0 else i

            @pl.when(z < ch if way == 0 else z > ch)
            def _():
                for copy in q_remote(way, i):
                    copy.wait_send()
        return carry

    lax.fori_loop(0, n - 1, finish, 0)
    for ch in range(n):
        p_remote(ch).wait_send()
    for d in range(1, n_col):
        for b in range(blocks):
            u_remote(d, b).wait_send()
    lout.wait()
    uout.wait()


def stream_call(order, weights, inverse, own_l, own_u, sizes):
    n, n_col = sizes
    _, rows, cols = inverse.shape
    per, _, unit, width = own_l.shape
    supers, blocks = own_u.shape[:2]
    wide = supers * width
    caps = full_caps(n, per)
    kbs = blocks * n_col
    half = cols // n // 2
    space = room(caps)
    dma = pltpu.SemaphoreType.DMA
    scratch = [
        pltpu.VMEM((2 * n, wide, half), jnp.float32),
        pltpu.VMEM((2, wide, 2 * unit), jnp.bfloat16),
        pltpu.VMEM((3, 2, unit, 2 * half), jnp.bfloat16),
        pltpu.VMEM((supers, kbs, 2, unit, width), jnp.bfloat16),
        pltpu.VMEM((per, 2, unit, width), jnp.bfloat16),
        pltpu.VMEM((space, 2, unit, width), jnp.bfloat16),
        pltpu.VMEM((2, RING, 2, unit, width), jnp.bfloat16),
        pltpu.VMEM((n, wide, half), jnp.float32),
        pltpu.VMEM((2, n - 1, wide, half), jnp.int16),
        pltpu.VMEM((2, n - 1, wide, half), jnp.int16),
        pltpu.VMEM((2, n - 1, 8, half), jnp.float32),
        pltpu.VMEM((2, n - 1, 8, half), jnp.float32),
        dma((3,)), dma((kbs,)), dma((kbs,)), dma((2,)),
        dma((2, RING)), dma((space,)), dma((space,)),
        dma((n,)), dma((n,)),
        dma((2, n - 1)), dma((2, n - 1)), dma((2, n - 1)), dma((2, n - 1)),
    ]
    smem = pl.BlockSpec(memory_space=pltpu.SMEM)
    vmem = pl.BlockSpec(memory_space=pltpu.VMEM)
    hbm = pl.BlockSpec(memory_space=pl.ANY)
    return pl.pallas_call(
        functools.partial(stream_kernel, (n, n_col, caps)),
        out_shape=(
            jax.ShapeDtypeStruct((per + space, 2, unit, width), jnp.bfloat16),
            jax.ShapeDtypeStruct((supers, kbs, 2, unit, width), jnp.bfloat16),
            jax.ShapeDtypeStruct((wide, half), jnp.float32),
        ),
        in_specs=[smem, smem, hbm, hbm, hbm],
        out_specs=(hbm, hbm, vmem),
        scratch_shapes=scratch,
        compiler_params=pltpu.CompilerParams(collective_id=0, has_side_effects=True, vmem_limit_bytes=62 * 2**20),
        name="streams",
    )(order, weights, inverse, own_l, own_u)


def column_kernel(cfg, meta, weights, a_ref, *rest):
    supers, n_col, blocks = cfg
    l_refs = rest[:supers]
    u_ref, given, mine, other, diag, acc = rest[supers:]
    k = pl.program_id(0)
    steps = pl.num_programs(0)
    _, rows, double = acc.shape
    width = double // 2
    unit = a_ref.shape[2]
    base = 2 * supers * steps
    piece = rows

    @pl.when(k == 0)
    def _():
        acc[...] = jnp.zeros_like(acc)

    for s in range(supers):
        @pl.when(meta[k * supers + s] > 0)
        def _():
            real = l_refs[s][0, 0]
            imag = l_refs[s][0, 1]
            right = jnp.concatenate([jnp.concatenate([real, imag], axis=1), jnp.concatenate([-imag, real], axis=1)], axis=0)

            def part(i, carry):
                span = pl.ds(pl.multiple_of(i * piece, piece), piece)
                left = jnp.concatenate([a_ref[0, span], a_ref[1, span]], axis=1)
                acc[s, span] += jnp.dot(left, right, preferred_element_type=jnp.float32)
                return carry

            lax.fori_loop(0, rows // piece, part, 0)

    @pl.when(k == steps - 1)
    def _():
        part = mine.shape[1]
        pole = meta[base]
        for s in range(supers):
            lanes = slice(s * width, (s + 1) * width)
            for c in range(n_col):
                for q in range(2):
                    span = pl.ds((2 * c + q) * part, part)
                    real = acc[s, span, :width]
                    imag = acc[s, span, width:]
                    mixed = weights[0] * imag + weights[1] * real
                    acc[s, span, :width] = mixed
                    acc[s, span, width:] = weights[0] * real - weights[1] * imag

                    @pl.when(pole == q)
                    def _():
                        mine[c, :, lanes] = mixed

                    @pl.when(pole != q)
                    def _():
                        other[c, :, lanes] = mixed

            @pl.when(meta[base + 1] > 0)
            def _():
                diag[lanes, :] = weights[0] * given[s, 1].astype(jnp.float32) + weights[1] * given[s, 0].astype(jnp.float32)

            @pl.when(meta[base + 1] == 0)
            def _():
                diag[lanes, :] = jnp.zeros((width, diag.shape[1]), jnp.float32)

        def one(kb, carry):
            for s in range(supers):
                lanes = slice(s * width, (s + 1) * width)

                @pl.when(meta[base + 2 + n_col + kb * supers + s] > 0)
                def _():
                    start = pl.multiple_of(meta[base + 2 + kb // blocks] + lax.rem(kb, blocks) * unit, unit)
                    total = jnp.zeros((width, width), jnp.float32)
                    for c in range(2):
                        value = acc[s, pl.ds(start, unit), c * width:(c + 1) * width]
                        high = value.astype(jnp.bfloat16)
                        low = (value - high.astype(jnp.float32)).astype(jnp.bfloat16)
                        turned = jnp.transpose(u_ref[s, kb, c])
                        total += jnp.dot(turned, high, preferred_element_type=jnp.float32) + jnp.dot(
                            turned, low, preferred_element_type=jnp.float32
                        )
                    diag[lanes, :] += total
            return carry

        lax.fori_loop(0, u_ref.shape[1], one, 0)


def column_call(meta, weights, inverse, lall, uall, given, sizes):
    n_col, supers, blocks = sizes
    _, rows, cols = inverse.shape
    _, _, unit, width = lall.shape
    steps = cols // unit
    part = rows // (2 * n_col)

    def slot(s):
        return lambda k, meta: (meta[supers * steps + k * supers + s], 0, 0, 0)

    whole = pl.BlockSpec(uall.shape, lambda k, meta: (0, 0, 0, 0, 0))
    out = pl.BlockSpec((n_col, part, supers * width), lambda k, meta: (0, 0, 0))
    return pl.pallas_call(
        functools.partial(column_kernel, (supers, n_col, blocks)),
        out_shape=(
            jax.ShapeDtypeStruct((n_col, part, supers * width), jnp.float32),
            jax.ShapeDtypeStruct((n_col, part, supers * width), jnp.float32),
            jax.ShapeDtypeStruct((supers * width, width), jnp.float32),
        ),
        grid_spec=pltpu.PrefetchScalarGridSpec(
            num_scalar_prefetch=1,
            grid=(steps,),
            in_specs=[
                pl.BlockSpec(memory_space=pltpu.SMEM),
                pl.BlockSpec((2, rows, unit), lambda k, meta: (0, 0, k)),
            ]
            + [pl.BlockSpec((1, 2, unit, width), slot(s)) for s in range(supers)]
            + [whole, pl.BlockSpec(given.shape, lambda k, meta: (0, 0, 0, 0))],
            out_specs=(out, out, pl.BlockSpec((supers * width, width), lambda k, meta: (0, 0))),
            scratch_shapes=[pltpu.VMEM((supers, rows, 2 * width), jnp.float32)],
        ),
        compiler_params=pltpu.CompilerParams(vmem_limit_bytes=60 * 2**20),
        name="columns",
    )(meta, weights, inverse, *([lall] * supers), uall, given)


def close_kernel(cfg, mine, other, diag, row, column, total, row_out, *scratch):
    (row_in, here, prec, qstage, qrecv, mstage, mrecv, dpole, dvalue, xcode, xscale, zcode, zscale, zin, zinscale, gcode, gscale,
     r_sem, h_sem, p_send, p_recv, q_send, q_recv, m_send, m_recv, dp_send, dp_recv, x_send, x_recv, xs_send, xs_recv,
     z_send, z_recv, zs_send, zs_recv, g_send, g_recv, gs_send, gs_recv, gp_send, gp_recv) = scratch
    n, n_col = cfg
    z = lax.axis_index("row")
    x = lax.axis_index("col")
    p = lax.axis_index("pole")
    high = diag.shape[0] // 2
    slab = high // n
    supers, _, width = column.shape

    def remote(src, dst, send, recv, to):
        return pltpu.make_async_remote_copy(
            src_ref=src, dst_ref=dst, send_sem=send, recv_sem=recv, device_id=to, device_id_type=MESH
        )

    def lanes(s):
        return pl.ds(s * width, width)

    def p_remote(d, s):
        return remote(other.at[lax.rem(x + d, n_col), :, lanes(s)], prec.at[d, s], p_send.at[d, s], p_recv.at[d, s], {"pole": 1 - p})

    def h_copy(d, s):
        return pltpu.make_async_copy(mine.at[lax.rem(x + d, n_col), :, lanes(s)], here.at[d, s], h_sem.at[d, s])

    def dp_remote():
        return remote(diag.at[pl.ds(pl.multiple_of((1 - p) * high, 8), high)], dpole, dp_send.at[0], dp_recv.at[0], {"pole": 1 - p})

    def x_remote(d):
        to = {"col": lax.rem(x + d, n_col)}
        return (
            remote(xcode.at[0], xcode.at[d], x_send.at[d], x_recv.at[d], to),
            remote(xscale.at[0], xscale.at[d], xs_send.at[d], xs_recv.at[d], to),
        )

    def q_remote(d, s):
        to = {"col": lax.rem(x + d, n_col)}
        return (
            remote(qstage.at[d, s], qrecv.at[d, s], q_send.at[d, s], q_recv.at[d, s], to),
            remote(mstage.at[d, s], mrecv.at[d, s], m_send.at[d, s], m_recv.at[d, s], to),
        )

    def z_remote(d):
        to = {"row": lax.rem(z + d, n)}
        return (
            remote(zcode.at[d], zin.at[d], z_send.at[d], z_recv.at[d], to),
            remote(zscale.at[d], zinscale.at[d], zs_send.at[d], zs_recv.at[d], to),
        )

    def g_remote(d):
        to = {"row": lax.rem(z + d, n)}
        return (
            remote(gcode.at[0], gcode.at[d], g_send.at[d], g_recv.at[d], to),
            remote(gscale.at[0], gscale.at[d], gs_send.at[d], gs_recv.at[d], to),
        )

    def rows_of(place):
        return pl.ds(pl.multiple_of(p * high + place * slab, 8), slab)

    def gp_remote():
        span = pl.ds(pl.multiple_of(p * high, 8), high)
        return remote(total.at[span], total.at[span], gp_send.at[0], gp_recv.at[0], {"pole": 1 - p})

    def put(code_ref, scale_ref, d, value):
        code, scale = packed(value)
        code_ref[d] = code
        scale_ref[d] = jnp.broadcast_to(scale, (8, width))

    def get(code_ref, scale_ref, d):
        return unpacked(code_ref[d], scale_ref[d, :1])

    others = range(1, n_col)
    r_copy = pltpu.make_async_copy(row, row_in, r_sem.at[0])
    for s in range(supers):
        for d in range(n_col):
            h_copy(d, s).start()
    greet((("row", n, False), ("col", n_col, False), ("pole", 2, False)))
    dp_remote().start()
    for s in range(supers):
        for d in others:
            p_remote(d, s).start()
    for s in range(supers):
        p_remote(0, s).start()
    r_copy.start()

    dp_remote().wait_recv()
    dvalue[...] = diag[pl.ds(pl.multiple_of(p * high, 8), high)] + dpole[...]
    for d in range(1, n):
        to = lax.rem(z + d, n)
        put(zcode, zscale, d, dvalue[pl.ds(pl.multiple_of(to * slab, 8), slab)])
        for copy in z_remote(d):
            copy.start()

    def send(s):
        for d in others:
            p_remote(d, s).wait_recv()
            h_copy(d, s).wait()
            put(qstage, mstage, (d, s), here[d, s] + prec[d, s])
            for copy in q_remote(d, s):
                copy.start()

    send(0)
    value = dvalue[pl.ds(pl.multiple_of(z * slab, 8), slab)]
    for d in range(1, n):
        for copy in z_remote(d):
            copy.wait_recv()
        value = value + get(zin, zinscale, d)
    put(xcode, xscale, 0, value)
    for d in others:
        for copy in x_remote(d):
            copy.start()
    for s in range(1, supers):
        send(s)
    for s in range(supers):
        p_remote(0, s).wait_recv()
        h_copy(0, s).wait()
        column[s] = -(here[0, s] + prec[0, s])
    r_copy.wait()
    for s in range(supers):
        row_out[s] = jnp.transpose(row_in[s * width:(s + 1) * width, :])
    for d in others:
        for copy in x_remote(d):
            copy.wait_recv()
    value = jnp.zeros((slab, width), jnp.float32)
    for origin in range(n_col):
        value = value + get(xcode, xscale, lax.rem(x - origin + n_col, n_col))
    put(gcode, gscale, 0, value)
    for d in range(1, n):
        for copy in g_remote(d):
            copy.start()
    total[rows_of(z)] = get(gcode, gscale, 0)
    for d in range(1, n):
        for copy in g_remote(d):
            copy.wait_recv()
        total[rows_of(lax.rem(z - d + n, n))] = get(gcode, gscale, d)
    gp_remote().start()

    for s in range(supers):
        for d in others:
            for copy in q_remote(d, s):
                copy.wait_recv()
            column[s] = column[s] - unpacked(qrecv[d, s], mrecv[d, s, :1])

    gp_remote().wait_send()
    span = pl.ds(pl.multiple_of((1 - p) * high, 8), high)
    remote(total.at[span], total.at[span], gp_send.at[0], gp_recv.at[0], {"pole": 1 - p}).wait_recv()
    dp_remote().wait_send()
    for s in range(supers):
        for d in range(n_col):
            p_remote(d, s).wait_send()
    for d in range(1, n):
        for copy in z_remote(d) + g_remote(d):
            copy.wait_send()
    for d in others:
        for copy in x_remote(d):
            copy.wait_send()
        for s in range(supers):
            for copy in q_remote(d, s):
                copy.wait_send()


def close_call(mine, other, diag, row, n, n_col):
    _, part, wide = mine.shape
    tall, width = diag.shape
    supers = wide // width
    high = tall // 2
    slab = high // n
    dma = pltpu.SemaphoreType.DMA
    vmem = pl.BlockSpec(memory_space=pltpu.VMEM)
    hbm = pl.BlockSpec(memory_space=pl.ANY)
    return pl.pallas_call(
        functools.partial(close_kernel, (n, n_col)),
        out_shape=(
            jax.ShapeDtypeStruct((supers, part, width), jnp.float32),
            jax.ShapeDtypeStruct((tall, width), jnp.float32),
            jax.ShapeDtypeStruct((supers, row.shape[1], width), jnp.float32),
        ),
        in_specs=[hbm, hbm, vmem, hbm],
        out_specs=(vmem, vmem, vmem),
        scratch_shapes=[
            pltpu.VMEM(row.shape, jnp.float32),
            pltpu.VMEM((n_col, supers, part, width), jnp.float32),
            pltpu.VMEM((n_col, supers, part, width), jnp.float32),
            pltpu.VMEM((n_col, supers, part, width), jnp.int16),
            pltpu.VMEM((n_col, supers, part, width), jnp.int16),
            pltpu.VMEM((n_col, supers, 8, width), jnp.float32),
            pltpu.VMEM((n_col, supers, 8, width), jnp.float32),
            pltpu.VMEM((high, width), jnp.float32),
            pltpu.VMEM((high, width), jnp.float32),
            pltpu.VMEM((n_col, slab, width), jnp.int16),
            pltpu.VMEM((n_col, 8, width), jnp.float32),
            pltpu.VMEM((n, slab, width), jnp.int16),
            pltpu.VMEM((n, 8, width), jnp.float32),
            pltpu.VMEM((n, slab, width), jnp.int16),
            pltpu.VMEM((n, 8, width), jnp.float32),
            pltpu.VMEM((n, slab, width), jnp.int16),
            pltpu.VMEM((n, 8, width), jnp.float32),
            dma((1,)), *[dma((n_col, supers)) for _ in range(7)],
            dma((1,)), dma((1,)), dma((n_col,)), dma((n_col,)), dma((n_col,)), dma((n_col,)),
            dma((n,)), dma((n,)), dma((n,)), dma((n,)), dma((n,)), dma((n,)), dma((n,)), dma((n,)), dma((1,)), dma((1,)),
        ],
        compiler_params=pltpu.CompilerParams(collective_id=2, has_side_effects=True, vmem_limit_bytes=40 * 2**20),
        name="close",
    )(mine, other, diag, row)


def plan_kernel(cfg, pattern, order, full, keep, count):
    n, n_col, blocks, unit, width = cfg
    supers, entries = pattern.shape
    z = lax.axis_index("row")
    x = lax.axis_index("col")
    p = lax.axis_index("pole")
    per = supers * blocks
    units = n * n_col * blocks
    steps = n * blocks
    split = width // unit

    def clear(i, carry):
        keep[i] = 0
        return carry

    lax.fori_loop(0, supers * units, clear, 0)

    def mark(i, carry):
        s = i // entries
        at = s * units + pattern[s, lax.rem(i, entries)] * split
        for r in range(split):
            keep[at + r] = 1
        return carry

    lax.fori_loop(0, supers * entries, mark, 0)

    def number(i, carry):
        total = jnp.int32(0)
        for s in range(supers):
            for b in range(blocks):
                total = total + keep[s * units + i * blocks + b]
        count[i] = total
        return carry

    lax.fori_loop(0, n * n_col, number, 0)

    def pack(r, rank):
        s = r // blocks
        k = keep[s * units + (x * n + z) * blocks + lax.rem(r, blocks)]
        order[r] = 0

        @pl.when(k > 0)
        def _():
            order[rank] = r

        return rank + k

    lax.fori_loop(0, per, pack, jnp.int32(0))

    def around(i, sums):
        k = count[x * n + i]
        return sums[0] + jnp.where(i > z, k, 0), sums[1] + jnp.where(i < z, k, 0)

    above, below = lax.fori_loop(0, n, around, (jnp.int32(0), jnp.int32(0)))
    order[per] = above
    order[per + 1] = below

    base = 2 * supers * steps
    full[base] = p
    full[base + 1] = jnp.logical_and(z == 0, x == 0).astype(jnp.int32)
    for d in range(n_col):
        full[base + 2 + d] = lax.rem(x - d + n_col, n_col) * blocks * unit

    def rows(i, carry):
        kb = i // supers
        origin = lax.rem(x - kb // blocks + n_col, n_col)
        k = keep[lax.rem(i, supers) * units + (z * n_col + origin) * blocks + lax.rem(kb, blocks)]
        order[per + 2 + i] = k
        full[base + 2 + n_col + i] = k
        return carry

    lax.fori_loop(0, n_col * blocks * supers, rows, 0)

    def device(at, before):
        here = count[x * n + at]
        after = jnp.int32(0)
        for i in range(n):
            after = after + jnp.where(i > at, count[x * n + i], 0)

        def pair(r, rank):
            s = r // blocks
            b = lax.rem(r, blocks)
            k = keep[s * units + (x * n + at) * blocks + b]
            down = blocks * (at - z - 1) + rank + jnp.where(rank < blocks, 0, after)
            up = blocks * (z - 1 - at) + rank + jnp.where(rank < blocks, 0, before)
            to = (at * blocks + b) * supers + s
            place = jnp.where(at == z, r, jnp.where(at > z, per + down, per + room(full_caps(n, per)) - 1 - up))
            full[to] = k
            full[supers * steps + to] = jnp.where(k > 0, place, 0)
            return rank + k

        lax.fori_loop(0, per, pair, jnp.int32(0))
        return before + here

    lax.fori_loop(0, n, device, jnp.int32(0))


def plan_call(pattern, sizes, unit, width, blocks):
    n, n_col = sizes
    supers, _ = pattern.shape
    per = supers * blocks
    table = 2 * supers * n * blocks + 2 + n_col + n_col * blocks * supers
    smem = pl.BlockSpec(memory_space=pltpu.SMEM)
    return pl.pallas_call(
        functools.partial(plan_kernel, (n, n_col, blocks, unit, width)),
        out_shape=(
            jax.ShapeDtypeStruct((per + 2 + n_col * blocks * supers,), jnp.int32),
            jax.ShapeDtypeStruct((table,), jnp.int32),
        ),
        in_specs=[smem],
        out_specs=(smem, smem),
        scratch_shapes=[pltpu.SMEM((supers * n * n_col * blocks,), jnp.int32), pltpu.SMEM((n * n_col,), jnp.int32)],
        name="plan",
    )(pattern)


def scan_kernel(cfg, pattern, order, over, flags, send, recv):
    n_groups, = cfg
    supers, entries = pattern.shape
    g = lax.axis_index("groups")
    lane = lax.broadcasted_iota(jnp.int32, order.shape, 1)
    row = lax.broadcasted_iota(jnp.int32, order.shape, 0)
    rank = jnp.zeros(order.shape, jnp.int32)
    table = jnp.full(order.shape, -1, jnp.int32)
    for s in range(supers):
        hit = jnp.zeros(order.shape, jnp.int32)
        for j in range(entries):
            hit = jnp.where(lane == pattern[s, j], 1, hit)
        table = jnp.where(jnp.where(row == rank, hit, 0) > 0, s, table)
        rank = rank + hit
    order[...] = table
    bad = jnp.max(jnp.where(rank > SLOTS, 1.0, 0.0))
    flags[0] = jnp.full(flags.shape[1:], bad, jnp.float32)

    def copy(d):
        return pltpu.make_async_remote_copy(
            src_ref=flags.at[0], dst_ref=flags.at[d], send_sem=send.at[d], recv_sem=recv.at[d],
            device_id={"groups": lax.rem(g + d, n_groups)}, device_id_type=MESH,
        )

    greet((("groups", n_groups, False),))
    for d in range(1, n_groups):
        copy(d).start()
    for d in range(1, n_groups):
        copy(d).wait_send()
        copy(d).wait_recv()
    over[0] = jnp.max(flags[...])


def scan_call(pattern, owners, n_groups):
    smem = pl.BlockSpec(memory_space=pltpu.SMEM)
    dma = pltpu.SemaphoreType.DMA
    return pl.pallas_call(
        functools.partial(scan_kernel, (n_groups,)),
        out_shape=(
            jax.ShapeDtypeStruct((8, -(-owners // 128) * 128), jnp.int32),
            jax.ShapeDtypeStruct((1,), jnp.float32),
        ),
        in_specs=[smem],
        out_specs=(pl.BlockSpec(memory_space=pltpu.VMEM), smem),
        scratch_shapes=[pltpu.VMEM((n_groups, 8, 128), jnp.float32), dma((n_groups,)), dma((n_groups,))],
        compiler_params=pltpu.CompilerParams(collective_id=1, has_side_effects=True),
        name="scan",
    )(pattern)


def fused_kernel(cfg, order, weights, inverse, own_l, own_u, given, row_out, mine, other, diag, *scratch):
    (acc, cacc, lhs, rhs, abuf, cbuf, uslots, lin, qstage, qrecv, mstage, mrecv,
     a_sem, c_sem, u_send, u_recv, o_sem, l_send, l_recv, p_send, p_recv, q_send, q_recv, m_send, m_recv, w_sem) = scratch[:26]
    n, n_col, supers = cfg
    z = lax.axis_index("row")
    x = lax.axis_index("col")
    p = lax.axis_index("pole")
    kbs, _, _, unit, width = uslots.shape
    blocks = kbs // n_col
    remote_blocks = (n - 1) * blocks
    half = acc.shape[2]
    tile = 2 * half
    rows = cacc.shape[1]
    apart = len(scratch) > 26
    prec = scratch[26] if apart else cacc

    def given_at(s, c):
        return scratch[27].at[s, c] if apart else cbuf.at[0, c, pl.ds(s * width, width)]

    wide = supers * width

    def lower_owner(k, j):
        return order[j, (x * n * blocks + k) * unit // width]

    def upper_owner(kb, j):
        origin = lax.rem(x - kb // blocks + n_col, n_col)
        return order[j, ((z * n_col + origin) * blocks + lax.rem(kb, blocks)) * unit // width]

    def place_of(ch):
        if not apart:
            fit = rows // wide
            return cacc.at[ch // fit, pl.ds(pl.multiple_of(lax.rem(ch, fit) * wide, wide), wide)]
        return prec.at[ch]

    def a_copy(t):
        kb = t // n
        origin = lax.rem(x - kb // blocks + n_col, n_col)
        row = (origin * blocks + lax.rem(kb, blocks)) * unit
        return pltpu.make_async_copy(
            inverse.at[:, pl.ds(pl.multiple_of(row, unit), unit), pl.ds(pl.multiple_of(lax.rem(t, n) * tile, tile), tile)],
            abuf.at[lax.rem(t, 2)],
            a_sem.at[lax.rem(t, 2)],
        )

    per = supers * blocks
    own = [
        pltpu.make_async_copy(source.at[c], lin.at[pl.ds(i * per, per), c], o_sem.at[2 * i + c])
        for i, source in enumerate((own_l, own_u))
        for c in range(2)
    ]
    for copy in own:
        copy.start()
    a_copy(0).start()
    for copy in own:
        copy.wait()
    for b in range(blocks):
        for j in range(SLOTS):
            chosen = jnp.maximum(lower_owner(z * blocks + b, j), 0)
            lin[(remote_blocks + b) * SLOTS + j] = lin[chosen * blocks + b]
            chosen = jnp.maximum(upper_owner(b, j), 0)
            uslots[b, j] = lin[per + chosen * blocks + b]
    greet((("row", n, True), ("col", n_col, False), ("pole", 2, False)))

    def u_remote(d, b):
        return pltpu.make_async_remote_copy(
            src_ref=uslots.at[b], dst_ref=uslots.at[d * blocks + b],
            send_sem=u_send.at[d * blocks + b], recv_sem=u_recv.at[d * blocks + b],
            device_id={"col": lax.rem(x + d, n_col)}, device_id_type=MESH,
        )

    sent = (jnp.where(z > 0, (n - z) * blocks, 0), jnp.where(z < n - 1, (z + 1) * blocks, 0))
    taken = ((n - 1 - z) * blocks, z * blocks)

    def l_place(way, c):
        return c if way == 0 else remote_blocks - 1 - c

    def l_remote(way, c, source):
        return pltpu.make_async_remote_copy(
            src_ref=lin.at[pl.ds(source * SLOTS, SLOTS)], dst_ref=lin.at[pl.ds(l_place(way, c) * SLOTS, SLOTS)],
            send_sem=l_send.at[way, c], recv_sem=l_recv.at[l_place(way, c)],
            device_id={"row": z - 1 if way == 0 else z + 1}, device_id_type=MESH,
        )

    for b in range(blocks):
        for d in range(1, n_col):
            u_remote(d, b).start()
        for way in range(2):
            @pl.when(sent[way] > 0)
            def _():
                l_remote(way, b, remote_blocks + b).start()

    def forward(c):
        for way in range(2):
            @pl.when(c + blocks < sent[way])
            def _():
                l_remote(way, c, l_place(way, c)).wait_recv()
                l_remote(way, c + blocks, l_place(way, c)).start()

    tiles = kbs * n
    events = (n - 2) * blocks
    events_early = events * 5 // 8

    def row_tile(t, carry):
        kb = t // n
        j = lax.rem(t, n)

        @pl.when(t + 1 < tiles)
        def _():
            a_copy(t + 1).start()

        @pl.when(j == 0)
        def _():
            @pl.when(kb >= blocks)
            def _():
                u_remote(kb // blocks, lax.rem(kb, blocks)).wait_recv()

            owner = [upper_owner(kb, j) for j in range(SLOTS)]
            for j in range(SLOTS):
                real = uslots[kb, j, 0].astype(jnp.float32)
                imag = uslots[kb, j, 1].astype(jnp.float32)
                for i, value in enumerate((weights[1] * real + weights[0] * imag, weights[0] * real - weights[1] * imag)):
                    turned = jnp.transpose(value)
                    for s in range(supers):
                        span = slice(s * width, (s + 1) * width)
                        lanes = slice(i * unit, (i + 1) * unit)
                        kept = jnp.where(owner[j] == s, turned, 0.0)
                        high = kept.astype(jnp.bfloat16)
                        low = (kept - high.astype(jnp.float32)).astype(jnp.bfloat16)
                        down = slice(wide + s * width, wide + (s + 1) * width)
                        if j == 0:
                            lhs[span, lanes] = high
                            lhs[down, lanes] = low
                        else:
                            lhs[span, lanes] = jnp.where(owner[j] == s, high, lhs[span, lanes])
                            lhs[down, lanes] = jnp.where(owner[j] == s, low, lhs[down, lanes])

        a_copy(t).wait()
        slot = lax.rem(t, 2)
        total = jnp.dot(lhs[...], abuf[slot].reshape(2 * unit, tile), preferred_element_type=jnp.float32)
        for q in range(2):
            lanes = slice(q * half, (q + 1) * half)
            before = acc[2 * j + q]
            acc[2 * j + q] = total[:wide, lanes] + total[wide:, lanes] + jnp.where(kb == 0, jnp.zeros_like(before), before)

        def some(c, carry):
            forward(c)
            return carry

        lax.fori_loop(t * events_early // tiles, (t + 1) * events_early // tiles, some, 0)
        return carry

    lax.fori_loop(0, tiles, row_tile, 0)

    def p_remote(ch):
        return pltpu.make_async_remote_copy(
            src_ref=acc.at[2 * ch + 1 - p], dst_ref=place_of(ch), send_sem=p_send.at[ch], recv_sem=p_recv.at[ch],
            device_id={"pole": 1 - p}, device_id_type=MESH,
        )

    def p_start(i, carry):
        p_remote(i).start()
        return carry

    lax.fori_loop(0, n, p_start, 0)

    for d in range(1, n_col):
        for b in range(blocks):
            u_remote(d, b).wait_send()
    steps = n * blocks
    turning = unit == width and kbs <= steps

    def block_of(q):
        r = q - blocks
        few = jnp.minimum(taken[0], taken[1])
        up = jnp.where(r < 2 * few, lax.rem(r, 2), jnp.where(taken[0] > taken[1], 0, 1))
        c = jnp.where(r < 2 * few, r // 2, r - few)
        c = jnp.maximum(c, 0)
        place = jnp.where(q < blocks, remote_blocks + q, jnp.where(up == 0, c, remote_blocks - 1 - c))
        device = jnp.where(up == 0, z + 1 + c // blocks, z - 1 - c // blocks)
        column = jnp.where(q < blocks, z * blocks + q, device * blocks + lax.rem(c, blocks))
        return place, column, up, c

    def c_copy(v):
        q = v // 2
        _, column, _, _ = block_of(q)
        return pltpu.make_async_copy(
            inverse.at[:, pl.ds(pl.multiple_of(lax.rem(v, 2) * (rows // 2), rows // 2), rows // 2), pl.ds(pl.multiple_of(column * unit, unit), unit)],
            cbuf.at[lax.rem(v, 2)],
            c_sem.at[lax.rem(v, 2)],
        )

    c_copy(0).start()

    def p_add(ch, carry):
        p_remote(ch).wait_recv()
        acc[2 * ch + p] = acc[2 * ch + p] + place_of(ch)[...]
        return carry

    lax.fori_loop(0, n, p_add, 0)

    def q_remote(way, i):
        to = {"row": z + 1 if way == 0 else z - 1}
        return (
            pltpu.make_async_remote_copy(
                src_ref=qstage.at[way, i], dst_ref=qrecv.at[way, i], send_sem=q_send.at[way, i], recv_sem=q_recv.at[way, i],
                device_id=to, device_id_type=MESH,
            ),
            pltpu.make_async_remote_copy(
                src_ref=mstage.at[way, i], dst_ref=mrecv.at[way, i], send_sem=m_send.at[way, i], recv_sem=m_recv.at[way, i],
                device_id=to, device_id_type=MESH,
            ),
        )

    def arrived(way, i):
        for copy in q_remote(way, i):
            copy.wait_recv()
        return unpacked(qrecv[way, i], mrecv[way, i, :1])

    def wave(w):
        for way in range(2):
            i = w - z if way == 0 else w - (n - 1 - z)
            ch = n - 1 - i if way == 0 else i

            @pl.when(jnp.logical_and(i >= 0, z < ch if way == 0 else z > ch))
            def _():
                @pl.when(z > 0 if way == 0 else z < n - 1)
                def _():
                    acc[2 * ch + p] = acc[2 * ch + p] + arrived(way, i)

                code, scale = packed(acc[2 * ch + p])
                qstage[way, i] = code
                mstage[way, i] = jnp.broadcast_to(scale, mstage.shape[2:])
                for copy in q_remote(way, i):
                    copy.start()

    def row_end():
        row_out[...] = -acc[2 * z + p]

        @pl.when(z > 0)
        def _():
            row_out[...] = row_out[...] - arrived(0, n - 1 - z)

        @pl.when(z < n - 1)
        def _():
            row_out[...] = row_out[...] - arrived(1, z)

    gap = max(1, steps // (n - 1))

    def column_step(q, carry):
        w = q // gap

        @pl.when(jnp.logical_and(lax.rem(q, gap) == 0, w < n - 1))
        def _():
            wave(w)

        e = events_early + q // 2

        @pl.when(jnp.logical_and(lax.rem(q, 2) == 0, e < events))
        def _():
            forward(e)

        place, column, up, c = block_of(q)
        for way in range(2):
            @pl.when(jnp.logical_and(jnp.logical_and(q >= blocks, up == way), c + blocks >= sent[way]))
            def _():
                l_remote(way, c, remote_blocks).wait_recv()

        if turning:
            @pl.when(q < kbs)
            def _():
                for j in range(SLOTS):
                    for c in range(2):
                        uslots[q, j, c] = jnp.transpose(uslots[q, j, c])

        owner = [lower_owner(column, j) for j in range(SLOTS)]
        for s in range(supers):
            real = jnp.zeros((unit, width), jnp.bfloat16)
            imag = jnp.zeros((unit, width), jnp.bfloat16)
            for j in range(SLOTS):
                real = jnp.where(owner[j] == s, lin[place * SLOTS + j, 0], real)
                imag = jnp.where(owner[j] == s, lin[place * SLOTS + j, 1], imag)
            for i, value in enumerate((real, imag, -imag, real)):
                rhs[i // 2 * unit:(i // 2 + 1) * unit, (2 * s + i % 2) * width:(2 * s + i % 2 + 1) * width] = value

        for h in range(2):
            v = 2 * q + h

            @pl.when(v + 1 < 2 * steps)
            def _():
                c_copy(v + 1).start()

            c_copy(v).wait()
            left = jnp.concatenate([cbuf[h, 0], cbuf[h, 1]], axis=1)
            span = slice(h * (rows // 2), (h + 1) * (rows // 2))
            total = jnp.dot(left, rhs[...], preferred_element_type=jnp.float32)
            for s in range(supers):
                before = cacc[s, span]
                cacc[s, span] = total[:, 2 * s * width:2 * (s + 1) * width] + jnp.where(q == 0, jnp.zeros_like(before), before)
        return carry

    lax.fori_loop(0, steps, column_step, 0)


    gcopies = [
        pltpu.make_async_copy(given.at[s, c], given_at(s, c), o_sem.at[2 * s + c]) for s in range(supers) for c in range(2)
    ]
    for copy in gcopies:
        copy.start()
    part = mine.shape[1]

    def writes(s, c):
        lanes = pl.ds(s * width, width)
        return (
            pltpu.make_async_copy(cacc.at[s, pl.ds(pl.multiple_of((2 * c + p) * part, part), part), pl.ds(0, width)], mine.at[c, :, lanes], w_sem.at[0, s, c]),
            pltpu.make_async_copy(cacc.at[s, pl.ds(pl.multiple_of((2 * c + 1 - p) * part, part), part), pl.ds(0, width)], other.at[c, :, lanes], w_sem.at[1, s, c]),
        )

    for copy in gcopies:
        copy.wait()
    origin_flag = jnp.where(jnp.logical_and(z == 0, x == 0), 1.0, 0.0)
    for s in range(supers):
        def mix(i, carry):
            span = pl.ds(pl.multiple_of(i * 2 * part, 2 * part), 2 * part)
            real = cacc[s, span, :width]
            imag = cacc[s, span, width:]
            cacc[s, span, :width] = weights[0] * imag + weights[1] * real
            cacc[s, span, width:] = weights[0] * real - weights[1] * imag
            return carry

        lax.fori_loop(0, n_col, mix, 0)
        for c in range(n_col):
            for copy in writes(s, c):
                copy.start()
        diag[s * width:(s + 1) * width, :] = origin_flag * (
            weights[0] * given_at(s, 1)[...].astype(jnp.float32) + weights[1] * given_at(s, 0)[...].astype(jnp.float32)
        )

    def one(kb, carry):
        start = pl.multiple_of((lax.rem(x - kb // blocks + n_col, n_col) * blocks + lax.rem(kb, blocks)) * unit, unit)
        owner = [upper_owner(kb, j) for j in range(SLOTS)]
        for s in range(supers):
            rights = []
            lefts = []
            for c in range(2):
                value = cacc[s, pl.ds(start, unit), c * width:(c + 1) * width]
                high = value.astype(jnp.bfloat16)
                low = (value - high.astype(jnp.float32)).astype(jnp.bfloat16)
                rights.append(jnp.concatenate([high, low], axis=1))
                chosen = jnp.zeros((unit, width), jnp.bfloat16)
                for j in range(SLOTS):
                    chosen = jnp.where(owner[j] == s, uslots[kb, j, c], chosen)
                lefts.append(chosen if turning else jnp.transpose(chosen))
            total = jnp.dot(
                jnp.concatenate(lefts, axis=1), jnp.concatenate(rights, axis=0), preferred_element_type=jnp.float32
            )
            diag[s * width:(s + 1) * width, :] += total[:, :width] + total[:, width:]
        return carry

    lax.fori_loop(0, kbs, one, 0)
    row_end()

    for s in range(supers):
        for c in range(n_col):
            for copy in writes(s, c):
                copy.wait()

    def finish(i, carry):
        for way in range(2):
            ch = n - 1 - i if way == 0 else i

            @pl.when(z < ch if way == 0 else z > ch)
            def _():
                for copy in q_remote(way, i):
                    copy.wait_send()
        return carry

    lax.fori_loop(0, n - 1, finish, 0)

    def l_finish(c, carry):
        for way in range(2):
            @pl.when(c < sent[way])
            def _():
                l_remote(way, c, remote_blocks).wait_send()
        return carry

    lax.fori_loop(0, remote_blocks, l_finish, 0)

    def p_finish(ch, carry):
        p_remote(ch).wait_send()
        return carry

    lax.fori_loop(0, n, p_finish, 0)


def fused_call(order, weights, inverse, own_l, own_u, given, sizes):
    n, n_col, blocks = sizes
    _, rows, cols = inverse.shape
    _, per, unit, width = own_l.shape
    supers = per // blocks
    wide = supers * width
    kbs = blocks * n_col
    half = cols // n // 2
    part = rows // (2 * n_col)
    dma = pltpu.SemaphoreType.DMA
    shared = unit == width and rows // 2 >= wide and half == 2 * width and n <= supers * (rows // wide)
    scratch = [
        pltpu.VMEM((2 * n, wide, half), jnp.float32),
        pltpu.VMEM((supers, rows, 2 * width), jnp.float32),
        pltpu.VMEM((2 * wide, 2 * unit), jnp.bfloat16),
        pltpu.VMEM((2 * unit, 2 * wide), jnp.bfloat16),
        pltpu.VMEM((2, 2, unit, 2 * half), jnp.bfloat16),
        pltpu.VMEM((2, 2, rows // 2, unit), jnp.bfloat16),
        pltpu.VMEM((kbs, SLOTS, 2, unit, width), jnp.bfloat16),
        pltpu.VMEM((n * blocks * SLOTS, 2, unit, width), jnp.bfloat16),
        pltpu.VMEM((2, n - 1, wide, half), jnp.int16),
        pltpu.VMEM((2, n - 1, wide, half), jnp.int16),
        pltpu.VMEM((2, n - 1, 8, half), jnp.float32),
        pltpu.VMEM((2, n - 1, 8, half), jnp.float32),
        dma((2,)), dma((2,)), dma((kbs,)), dma((kbs,)), dma((max(4, 2 * supers),)),
        dma((2, n * blocks)), dma((n * blocks,)),
        dma((n,)), dma((n,)),
        dma((2, n - 1)), dma((2, n - 1)), dma((2, n - 1)), dma((2, n - 1)),
        dma((2, supers, n_col)),
    ]
    if not shared:
        scratch.append(pltpu.VMEM((n, wide, half), jnp.float32))
        scratch.append(pltpu.VMEM(given.shape, jnp.bfloat16))
    smem = pl.BlockSpec(memory_space=pltpu.SMEM)
    vmem = pl.BlockSpec(memory_space=pltpu.VMEM)
    hbm = pl.BlockSpec(memory_space=pl.ANY)
    return pl.pallas_call(
        functools.partial(fused_kernel, (n, n_col, supers)),
        out_shape=(
            jax.ShapeDtypeStruct((wide, half), jnp.float32),
            jax.ShapeDtypeStruct((n_col, part, wide), jnp.float32),
            jax.ShapeDtypeStruct((n_col, part, wide), jnp.float32),
            jax.ShapeDtypeStruct((wide, width), jnp.float32),
        ),
        in_specs=[smem, smem, hbm, hbm, hbm, hbm],
        out_specs=(vmem, hbm, hbm, vmem),
        scratch_shapes=scratch,
        compiler_params=pltpu.CompilerParams(collective_id=3, has_side_effects=True, vmem_limit_bytes=63 * 2**20),
        name="fused",
    )(order, weights, inverse, own_l, own_u, given)


def body(inverse, lower, upper, diag_inverse, weights, pattern):
    n = lax.axis_size("row")
    n_col = lax.axis_size("col")
    n_groups = lax.axis_size("groups")
    _, local, _, supers, width = lower.shape
    inverse = inverse[0]
    unit = min(width, local)
    blocks = local // unit
    weights = weights[0]
    given = diag_inverse[0]
    order, over = scan_call(pattern, n * n_col * local // width, n_groups)

    def flat(factor):
        return jnp.transpose(factor[0], (1, 2, 0, 3)).reshape(2, supers * blocks, unit, width)

    def usual():
        return fused_call(order, weights, inverse, flat(lower), flat(upper), given, (n, n_col, blocks))

    def rare():
        order, full = plan_call(pattern, (n, n_col), unit, width, blocks)
        own_l = jnp.transpose(flat(lower), (1, 0, 2, 3))
        own_u = jnp.transpose(flat(upper), (1, 0, 2, 3)).reshape(supers, blocks, 2, unit, width)
        lall, uall, row = stream_call(order, weights, inverse, own_l, own_u, (n, n_col))
        return (row,) + tuple(column_call(full, weights, inverse, lall, uall, given, (n_col, supers, blocks)))

    row, mine, other, diag = lax.cond(over[0] <= 0, usual, rare)
    column, diagonal, row = close_call(mine, other, diag, row, n, n_col)
    return (jnp.transpose(column, (1, 0, 2)), jnp.transpose(row, (1, 0, 2)), diagonal.reshape(supers, width, width))


def solution(mesh):
    return jax.shard_map(
        body,
        mesh=mesh,
        in_specs=(
            P(("groups", "pole"), None, "row", "col"),
            P(("groups", "pole"), ("col", "row"), None, None, None),
            P(("groups", "pole"), ("row", "col"), None, None, None),
            P(("groups", "pole"), None, None, None, None),
            P(("groups", "pole"), None),
            P("groups", None),
        ),
        out_specs=(
            P(("groups", "row", "col", "pole"), None, None),
            P(("groups", "col", "row", "pole"), None, None),
            P("groups", None, None),
        ),
        check_vma=False,
    )
```
